32 devices in a mesh: groups: 2 (over x), blk: 16 (over z, y, core).
Axes of the slice: x: 2, y: 2, z: 4, core: 2. Of those that a mesh axis runs over, the one named last changes fastest.
Arguments:
- rows: bfloat16 [131072, 768], P(('groups', 'blk')), parts along dimension 0, may hold values from -8 to 8, as said below
- centroids: bfloat16 [8192, 768], P(('groups', 'blk')), parts along dimension 0, may hold values from -4 to 4, as said below
- lists: int32 [512, 6], P(('groups', 'blk')), parts along dimension 0, may hold values from 0 to 15, as said below
Outputs:
- new_centroids: float32 [8192, 768], P(('groups', 'blk')), parts along dimension 0
- log_totals: float32 [131072], P(('groups', 'blk')), parts along dimension 0
The draws below stay inside these ranges and needn't reach their ends.
There are 2 independent parts, one for each index of `groups`. The reference program is written for one: setup_inputs(seed, part) draws one part's arguments, and reference() takes and returns one part's arrays. A program takes and returns all parts, laid end to end along the dimension named above; each array names one. Nothing has to cross between parts.
Inputs may be any that keep to these rules, and one draw needn't show every extreme that they name: `rows`: embeddings of order one. `centroids`: centroids of order one half. `lists`: the 6 entries of a block are distinct panel numbers. Block b is held by device q = b // 16 along blk; every listed panel lies within cycle distance 6 of panel q (indices taken modulo 16), panel q itself is always listed, and distance 6 is reached. Panels are listed unevenly.
All inputs are finite; a program needn't handle non-finite values.
Results may differ from the reference program's by a relative error of at most 0.00056.
Values may be sent and summed in bfloat16 or wider, within the bound.
No kernel may reach another device: no remote copies, remote signals or barrier semaphores. Data moves between devices by JAX's collectives and lax.ppermute only.
A program may use at most 128 MiB of HBM per device.

```python
import jax
import jax.numpy as jnp
from jax import lax

D = 768
CENT_DEV = 256
ROW_DEV = 4096
BLOCK = 256
LISTED = 6
SPAN = 6
PANELS = 16
K = 4096
ROWS = 65536


def centroid_field(key):
    random_seed_key = jax.random.fold_in(key, 11)
    first_key = jax.random.fold_in(random_seed_key, 0)
    field = 0.5 * jax.random.normal(first_key, (K, D), jnp.float32)
    return jnp.clip(field, -4.0, 4.0)


def draw_centroids(key, part):
    return centroid_field(key).astype(jnp.bfloat16)


def draw_rows(key, part):
    random_seed_key = jax.random.fold_in(key, 23)
    first_key = jax.random.fold_in(random_seed_key, 0)
    field = jax.random.normal(first_key, (ROWS, D), jnp.float32)
    return jnp.clip(field, -8.0, 8.0).astype(jnp.bfloat16)


def draw_lists(key, part):
    random_seed_key = jax.random.fold_in(key, 37)
    first_key, second_key = jax.random.split(random_seed_key)
    blocks = ROWS // BLOCK
    per_device = ROW_DEV // BLOCK
    width = 2 * SPAN + 1
    heat = jax.random.randint(first_key, (PANELS,), 0, 4)
    noise = jax.random.randint(second_key, (blocks, width), 0, 64)
    device = jnp.arange(blocks, dtype=jnp.int32) // per_device
    offsets = jnp.arange(width, dtype=jnp.int32) - SPAN
    panel_ids = (device[:, None] + offsets[None, :]) % PANELS
    scores = heat[panel_ids] * 64 + noise
    first_block = (jnp.arange(blocks, dtype=jnp.int32) % per_device == 0)[:, None]
    scores = scores + jnp.where(offsets[None, :] == 0, 1000, 0)
    edges = jnp.abs(offsets)[None, :] == SPAN
    scores = scores + jnp.where(jnp.logical_and(first_block, edges), 500, 0)
    scores = scores * 16 + jnp.arange(width, dtype=jnp.int32)[None, :]
    selected_values, picked = lax.top_k(scores, LISTED)
    return jnp.take_along_axis(panel_ids, picked, axis=1).astype(jnp.int32)


def setup_inputs(seed: int = 0, part: int = 0) -> dict:
    key_of = jax.random.split(jax.random.key(seed), 4)
    part_keys = jax.random.split(jax.random.fold_in(key_of[3], part), 4)
    rows = draw_rows(jax.random.fold_in(jax.random.fold_in(key_of[3], part), 71), part)
    centroids = draw_centroids(jax.random.fold_in(jax.random.fold_in(key_of[3], part), 71), part)
    lists = draw_lists(jax.random.fold_in(jax.random.fold_in(key_of[3], part), 71), part)
    return dict(rows=rows, centroids=centroids, lists=lists)


logit_scale = 0.25
prior_mass = 8.0


def reference(rows, centroids, lists):
    panel_stack = centroids.reshape(PANELS, CENT_DEV, D)
    norms = jnp.sum(jnp.square(panel_stack.astype(jnp.float32)), axis=-1)
    row_blocks = rows.reshape(ROWS // BLOCK, BLOCK, D)

    def one_block(running_counts, inputs):
        weighted_sums, weight_totals = running_counts
        block_rows, panel_ids = inputs
        panels = panel_stack[panel_ids]
        scores = jnp.einsum('bd,lcd->blc', block_rows.astype(jnp.float32), panels.astype(jnp.float32))
        logits = (scores - 0.5 * norms[panel_ids][None]) * logit_scale
        flat_rows_view = logits.reshape(BLOCK, LISTED * CENT_DEV)
        highest = jnp.max(flat_rows_view, axis=1, keepdims=True)
        log_total = highest[:, 0] + jnp.log(jnp.sum(jnp.exp(flat_rows_view - highest), axis=1))
        weights = jnp.exp(flat_rows_view - log_total[:, None]).astype(jnp.bfloat16)
        partial_value = jnp.dot(weights.T, block_rows, preferred_element_type=jnp.float32).reshape(LISTED, CENT_DEV, D)
        summed_weights = jnp.sum(weights.astype(jnp.float32), axis=0).reshape(LISTED, CENT_DEV)
        weighted_sums = weighted_sums.at[panel_ids].add(partial_value)
        weight_totals = weight_totals.at[panel_ids].add(summed_weights)
        return (weighted_sums, weight_totals), log_total

    start = (jnp.zeros((PANELS, CENT_DEV, D), jnp.float32), jnp.zeros((PANELS, CENT_DEV), jnp.float32))
    (weighted_sums, weight_totals), log_totals = lax.scan(one_block, start, (row_blocks, lists.astype(jnp.int32)))
    updated = (weighted_sums + prior_mass * panel_stack.astype(jnp.float32)) / (weight_totals[..., None] + prior_mass)
    return updated.reshape(K, D), log_totals.reshape(ROWS)
```

```python
import math

import jax
import jax.numpy as jnp
from jax import lax
from jax.experimental import pallas as pl
from jax.experimental.pallas import tpu as pltpu
from jax.sharding import PartitionSpec as P

BLOCK = 256
SPAN = 6
LOGIT_SCALE = 0.25
PRIOR_MASS = 8.0
LOG2E = math.log2(math.e)
LINK_SCALE = 1.0 / 16.0
CHUNKS = 2


def permuted(value, target):
    count = lax.axis_size("blk")
    return lax.ppermute(value, "blk", [(i, target(i, count)) for i in range(count)])


def other_core(value):
    return permuted(value, lambda i, n: i ^ 1)


def other_column(value):
    return permuted(value, lambda i, n: i ^ 2)


def chip_up(value):
    return permuted(value, lambda i, n: (i + 4) % n)


def chip_down(value):
    return permuted(value, lambda i, n: (i - 4) % n)


def grid_gather(centroids):
    rows = centroids.shape[0] // CHUNKS
    levels = lax.axis_size("blk") // 4
    moving = [centroids[h * rows : (h + 1) * rows] for h in range(CHUNKS)]
    places = []
    for shift in range(levels):
        if shift:
            moving = [chip_up(v) for v in moving]
        across = [other_column(v) for v in moving]
        places += [moving, [other_core(v) for v in moving]]
        places += [across, [other_core(v) for v in across]]
    return places


def grid_place(panel, device):
    levels = lax.axis_size("blk") // 4
    shift = (device // 4 - panel // 4) % levels
    return shift * 4 + ((panel ^ device) & 3)


def packed(value):
    return (value * LINK_SCALE).astype(jnp.float16)


def grid_reduce(sums):
    levels = lax.axis_size("blk") // 4
    rows = sums.shape[1] // CHUNKS
    whole = []
    for h in range(CHUNKS):
        part = sums[:, h * rows : (h + 1) * rows] * LINK_SCALE

        def paired(place):
            return part[place] + other_core(part[place + 1].astype(jnp.float16)).astype(jnp.float32)

        total = None
        for shift in reversed(range(levels)):
            away = other_column(paired(shift * 4 + 2).astype(jnp.float16))
            here = paired(shift * 4) + away.astype(jnp.float32)
            if total is not None:
                here = here + chip_down(total.astype(jnp.float16)).astype(jnp.float32)
            total = here
        whole.append(total)
    return jnp.concatenate(whole) * (1.0 / LINK_SCALE)


def ring_gather(centroids):
    places = []
    for offset in range(-SPAN, SPAN + 1):
        piece = permuted(centroids, lambda i, n: (i - offset) % n) if offset else centroids
        rows = piece.shape[0] // CHUNKS
        places.append([piece[h * rows : (h + 1) * rows] for h in range(CHUNKS)])
    return places


def ring_place(panel, device):
    return (panel - device + SPAN) % lax.axis_size("blk")


def ring_reduce(sums):
    total = sums[SPAN]
    for offset in range(-SPAN, SPAN + 1):
        if offset:
            arrived = permuted(packed(sums[offset + SPAN]), lambda i, n: (i + offset) % n)
            total = total + arrived.astype(jnp.float32) * (1.0 / LINK_SCALE)
    return total


def kernel(places, pieces, slots_ref, rows_ref, *refs):
    piece_refs = refs[: places * pieces]
    logs_ref, sums_ref, totals_ref, panels, norms, logits, sem = refs[places * pieces :]
    step = pl.program_id(0)
    listed = logits.shape[0]
    piece_rows = panels.shape[1] // pieces

    @pl.when(step == 0)
    def _():
        copies = [
            pltpu.make_async_copy(
                piece_refs[p * pieces + h],
                panels.at[p, pl.ds(h * piece_rows, piece_rows)],
                sem.at[p * pieces + h],
            )
            for p in range(places)
            for h in range(pieces)
        ]
        for copy in copies:
            copy.start()
        sums_ref[...] = jnp.zeros_like(sums_ref)
        totals_ref[...] = jnp.zeros_like(totals_ref)
        for copy in copies:
            copy.wait()

        @pl.loop(0, places)
        def _(p):
            wide = panels[p].astype(jnp.float32)
            norm = jnp.sum(wide * wide, axis=1, keepdims=True)
            norms[p] = jnp.broadcast_to(norm * (0.5 * LOGIT_SCALE * LOG2E), norms.shape[1:])

    block = rows_ref[...]
    highest = None
    for l in range(listed):
        place = slots_ref[step * listed + l]
        scores = lax.dot_general(
            panels[place], block, (((1,), (1,)), ((), ())), preferred_element_type=jnp.float32
        )
        norm = norms[place]
        scores = scores * (LOGIT_SCALE * LOG2E) - jnp.concatenate([norm, norm], axis=1)
        logits[l] = scores
        top = jnp.max(scores, axis=0, keepdims=True)
        highest = top if highest is None else jnp.maximum(highest, top)
    mass = jnp.zeros_like(highest)
    for l in range(listed):
        powers = jnp.exp2(logits[l] - highest)
        logits[l] = powers
        mass = mass + jnp.sum(powers, axis=0, keepdims=True)
    logs_ref[0] = (highest + jnp.log2(mass)) * (1.0 / LOG2E)
    share = 1.0 / mass
    for l in range(listed):
        place = slots_ref[step * listed + l]
        weights = (logits[l] * share).astype(jnp.bfloat16)
        sums_ref[place] += jnp.dot(weights, block, preferred_element_type=jnp.float32)
        wide = weights.astype(jnp.float32)
        totals_ref[place] += wide[:, :128] + wide[:, 128:]


def scored_sums(pieces_of, rows, slots):
    places, pieces = len(pieces_of), len(pieces_of[0])
    width = rows.shape[1]
    blocks, listed = slots.shape
    cent = pieces_of[0][0].shape[0] * pieces
    flat = [piece for place in pieces_of for piece in place]
    flops = 4 * rows.shape[0] * listed * cent * width

    def body(*refs):
        kernel(places, pieces, *refs)

    logs, sums, totals = pl.pallas_call(
        body,
        out_shape=(
            jax.ShapeDtypeStruct((blocks, 1, BLOCK), jnp.float32),
            jax.ShapeDtypeStruct((places, cent, width), jnp.float32),
            jax.ShapeDtypeStruct((places, cent, 128), jnp.float32),
        ),
        grid_spec=pltpu.PrefetchScalarGridSpec(
            num_scalar_prefetch=1,
            grid=(blocks,),
            in_specs=[pl.BlockSpec((BLOCK, width), lambda b, s: (b, 0))]
            + [pl.BlockSpec(memory_space=pl.ANY)] * len(flat),
            out_specs=(
                pl.BlockSpec((1, 1, BLOCK), lambda b, s: (b, 0, 0)),
                pl.BlockSpec((places, cent, width), lambda b, s: (0, 0, 0), pipeline_mode=pl.Buffered(1)),
                pl.BlockSpec((places, cent, 128), lambda b, s: (0, 0, 0), pipeline_mode=pl.Buffered(1)),
            ),
            scratch_shapes=[
                pltpu.VMEM((places, cent, width), jnp.bfloat16),
                pltpu.VMEM((places, cent, 128), jnp.float32),
                pltpu.VMEM((listed, cent, BLOCK), jnp.float32),
                pltpu.SemaphoreType.DMA((places * pieces,)),
            ],
        ),
        compiler_params=pltpu.CompilerParams(
            dimension_semantics=("arbitrary",), vmem_limit_bytes=48 << 20
        ),
        cost_estimate=pl.CostEstimate(
            flops=flops,
            bytes_accessed=rows.size * 2 + places * cent * width * 6,
            transcendentals=rows.shape[0] * listed * cent,
        ),
        name="scored_sums",
    )(slots.reshape(-1), rows, *flat)
    return logs.reshape(-1), sums, jnp.sum(totals, axis=-1)


def on_device(rows, centroids, lists):
    count = lax.axis_size("blk")
    device = lax.axis_index("blk")
    on_grid = count == 16
    place_of = grid_place if on_grid else ring_place
    pieces_of = grid_gather(centroids) if on_grid else ring_gather(centroids)
    slots = place_of(lists, device).astype(jnp.int32)
    log_totals, sums, totals = scored_sums(pieces_of, rows, slots)
    everyone = jnp.arange(count, dtype=jnp.int32)
    places = place_of(everyone, device)
    used = places < len(pieces_of)
    by_panel = jnp.where(used[:, None], totals[jnp.where(used, places, 0)], 0.0)
    own_totals = lax.psum_scatter(by_panel.reshape(-1), "blk", tiled=True)
    own_sums = grid_reduce(sums) if on_grid else ring_reduce(sums)
    updated = (own_sums + PRIOR_MASS * centroids.astype(jnp.float32)) / (
        own_totals[:, None] + PRIOR_MASS
    )
    return updated, log_totals


def solution(mesh):
    placed = P(("groups", "blk"), None)
    return jax.shard_map(
        on_device,
        mesh=mesh,
        in_specs=(placed, placed, placed),
        out_specs=(placed, P(("groups", "blk"))),
        check_vma=False,
    )
```

```python
import math

import jax
import jax.numpy as jnp
from jax import lax
from jax.experimental import pallas as pl
from jax.experimental.pallas import tpu as pltpu
from jax.sharding import PartitionSpec as P

BLOCK = 256
SPAN = 6
LOGIT_SCALE = 0.25
PRIOR_MASS = 8.0
LOG2E = math.log2(math.e)
LINK_SCALE = 1.0 / 16.0
EXTRA = 8


def grid_plan(count):
    up = 4
    return 0, ((2, 0, up), (1, 0, None), (6, 0, -up), (3, 2, None), (7, 6, None), (5, 3, up))


def ring_plan(count):
    reach = (SPAN + 1) // 2
    steps = []
    for hop in range(reach):
        steps.append((reach + hop + 1, reach + hop, 2))
        steps.append((reach - hop - 1, reach - hop, -2))
    return reach, tuple(steps)


def plan_of(count):
    return grid_plan(count) if count == 16 else ring_plan(count)


def chip_place(panel, device, count):
    if count == 16:
        return (device // 4 - panel // 4) % 4 * 2 + ((panel ^ device) >> 1 & 1)
    chips = count // 2
    return (device // 2 - panel // 2 + (SPAN + 1) // 2) % chips


def moved(value, shift):
    count = lax.axis_size("blk")
    if shift is None:
        return lax.ppermute(value, "blk", [(i, i ^ 2) for i in range(count)])
    return lax.ppermute(value, "blk", [(i, (i + shift) % count) for i in range(count)])


def other_core(value):
    count = lax.axis_size("blk")
    return lax.ppermute(value, "blk", [(i, i ^ 1) for i in range(count)])


def gathered(centroids):
    own, steps = plan_of(lax.axis_size("blk"))
    here = {own: centroids}
    for place, source, shift in steps:
        here[place] = moved(here[source], shift)
    return here, {place: other_core(value) for place, value in here.items()}


def reduced(near, far):
    own, steps = plan_of(lax.axis_size("blk"))
    order = [place for place, _, _ in reversed(steps)] + [own]
    total = {place: (near[place] + other_core(far[place])) * LINK_SCALE for place in order}
    for place, source, shift in reversed(steps):
        back = moved(total[place].astype(jnp.float16), shift if shift is None else -shift)
        total[source] = total[source] + back.astype(jnp.float32)
    return total[own] * (1.0 / LINK_SCALE)


def kernel(places, slots_ref, rows_ref, *refs):
    count = len(places)
    near_refs, far_refs = refs[:count], refs[count : 2 * count]
    logs_ref, near_ref, far_ref, panels, norms, logits, totals, sem = refs[2 * count :]
    step = pl.program_id(0)
    listed = logits.shape[0]
    cent = panels.shape[1]

    @pl.when(step == 0)
    def _():
        copies = []
        for core, piece_refs in enumerate((near_refs, far_refs)):
            for at, ref in zip(places, piece_refs):
                copies.append(pltpu.make_async_copy(ref, panels.at[2 * at + core], sem.at[2 * at + core]))
        for copy in copies:
            copy.start()
        near_ref[...] = jnp.zeros_like(near_ref)
        far_ref[...] = jnp.zeros_like(far_ref)
        totals[...] = jnp.zeros_like(totals)
        for copy in copies:
            copy.wait()

        for at in places:

            @pl.loop(2 * at, 2 * at + 2)
            def _(p):
                wide = panels[p].astype(jnp.float32)
                norm = jnp.sum(wide * wide, axis=1, keepdims=True)
                norms[p] = jnp.broadcast_to(norm * (0.5 * LOGIT_SCALE * LOG2E), norms.shape[1:])

    block = rows_ref[...]
    highest = None
    for l in range(listed):
        place = slots_ref[step * listed + l]
        scores = lax.dot_general(
            panels[place], block, (((1,), (1,)), ((), ())), preferred_element_type=jnp.float32
        )
        norm = norms[place]
        scores = scores * (LOGIT_SCALE * LOG2E) - jnp.concatenate([norm, norm], axis=1)
        logits[l] = scores
        top = jnp.max(scores, axis=0, keepdims=True)
        highest = top if highest is None else jnp.maximum(highest, top)
    mass = jnp.zeros_like(highest)
    for l in range(listed):
        powers = jnp.exp2(logits[l] - highest)
        logits[l] = powers
        mass = mass + jnp.sum(powers, axis=0, keepdims=True)
    logs_ref[0] = (highest + jnp.log2(mass)) * (1.0 / LOG2E)
    share = 1.0 / mass
    for l in range(listed):
        place = slots_ref[step * listed + l]
        weights = (logits[l] * share).astype(jnp.bfloat16)
        partial = jnp.dot(weights, block, preferred_element_type=jnp.float32)
        wide = weights.astype(jnp.float32)
        totals[place] += wide[:, :128] + wide[:, 128:]

        @pl.when(place & 1 == 0)
        def _():
            near_ref[place >> 1, pl.ds(0, cent)] += partial

        @pl.when(place & 1 == 1)
        def _():
            far_ref[place >> 1, pl.ds(0, cent)] += partial

    @pl.when(step == pl.num_programs(0) - 1)
    def _():
        for at in places:
            for core, ref in enumerate((near_ref, far_ref)):
                row = jnp.sum(totals[2 * at + core].T, axis=0, keepdims=True)
                ref[at, pl.ds(cent, EXTRA), pl.ds(0, cent)] = jnp.broadcast_to(row, (EXTRA, cent))


def scored_sums(near, far, rows, slots):
    places = tuple(near)
    room = max(places) + 1
    width = rows.shape[1]
    blocks, listed = slots.shape
    cent = near[places[0]].shape[0]
    pieces = [near[p] for p in places] + [far[p] for p in places]
    whole = pl.BlockSpec((room, cent + EXTRA, width), lambda b, s: (0, 0, 0), pipeline_mode=pl.Buffered(1))

    def body(*refs):
        kernel(places, *refs)

    logs, near_sums, far_sums = pl.pallas_call(
        body,
        out_shape=(
            jax.ShapeDtypeStruct((blocks, 1, BLOCK), jnp.float32),
            jax.ShapeDtypeStruct((room, cent + EXTRA, width), jnp.float32),
            jax.ShapeDtypeStruct((room, cent + EXTRA, width), jnp.float32),
        ),
        grid_spec=pltpu.PrefetchScalarGridSpec(
            num_scalar_prefetch=1,
            grid=(blocks,),
            in_specs=[pl.BlockSpec((BLOCK, width), lambda b, s: (b, 0))]
            + [pl.BlockSpec(memory_space=pl.ANY)] * len(pieces),
            out_specs=(pl.BlockSpec((1, 1, BLOCK), lambda b, s: (b, 0, 0)), whole, whole),
            scratch_shapes=[
                pltpu.VMEM((2 * room, cent, width), jnp.bfloat16),
                pltpu.VMEM((2 * room, cent, 128), jnp.float32),
                pltpu.VMEM((listed, cent, BLOCK), jnp.float32),
                pltpu.VMEM((2 * room, cent, 128), jnp.float32),
                pltpu.SemaphoreType.DMA((2 * room,)),
            ],
        ),
        compiler_params=pltpu.CompilerParams(
            dimension_semantics=("arbitrary",), vmem_limit_bytes=48 << 20
        ),
        cost_estimate=pl.CostEstimate(
            flops=4 * rows.shape[0] * listed * cent * width,
            bytes_accessed=rows.size * 2 + len(pieces) * cent * width * 6,
            transcendentals=rows.shape[0] * listed * cent,
        ),
        name="scored_sums",
    )(slots.reshape(-1), rows, *pieces)
    return (
        logs.reshape(-1),
        {p: near_sums[p] for p in places},
        {p: far_sums[p] for p in places},
    )


def on_device(rows, centroids, lists):
    count = lax.axis_size("blk")
    device = lax.axis_index("blk")
    cent = centroids.shape[0]
    slots = 2 * chip_place(lists, device, count) + ((lists ^ device) & 1)
    near, far = gathered(centroids)
    log_totals, near_sums, far_sums = scored_sums(near, far, rows, slots.astype(jnp.int32))
    own = reduced(near_sums, far_sums)
    updated = (own[:cent] + PRIOR_MASS * centroids.astype(jnp.float32)) / (
        own[cent, :cent][:, None] + PRIOR_MASS
    )
    return updated, log_totals


def solution(mesh):
    placed = P(("groups", "blk"), None)
    return jax.shard_map(
        on_device,
        mesh=mesh,
        in_specs=(placed, placed, placed),
        out_specs=(placed, P(("groups", "blk"))),
        check_vma=False,
    )
```

```python
import functools
import math

import jax
import jax.numpy as jnp
from jax import lax
from jax.experimental import pallas as pl
from jax.experimental.pallas import tpu as pltpu
from jax.sharding import PartitionSpec as P

BLOCK = 256
SPAN = 6
LOGIT_SCALE = 0.25
PRIOR_MASS = 8.0
LOG2E = math.log2(math.e)
LINK_SCALE = 1.0 / 16.0
EXTRA = 8
DEPTH = 4


def grid_plan():
    return 0, (
        ((2, 0, 4), (1, 0, None)),
        ((6, 0, -4), (3, 2, None)),
        ((5, 3, 4), (7, 6, None)),
    )


def ring_plan():
    reach = (SPAN + 1) // 2
    return reach, tuple(
        ((reach + hop + 1, reach + hop, 2), (reach - hop - 1, reach - hop, -2)) for hop in range(reach)
    )


def plan_of(count):
    return grid_plan() if count == 16 else ring_plan()


def chip_place(panel, device, count):
    if count == 16:
        return (device // 4 - panel // 4) % 4 * 2 + ((panel ^ device) >> 1 & 1)
    return (device // 2 - panel // 2 + (SPAN + 1) // 2) % (count // 2)


def moved(value, shift):
    count = lax.axis_size("blk")
    if shift is None:
        return lax.ppermute(value, "blk", [(i, i ^ 2) for i in range(count)])
    return lax.ppermute(value, "blk", [(i, (i + shift) % count) for i in range(count)])


def other_core(value):
    count = lax.axis_size("blk")
    return lax.ppermute(value, "blk", [(i, i ^ 1) for i in range(count)])


def collect(slots_ref, members, ids_ref, blocks, listed):
    def one_block(b, found):
        for l in range(listed):
            chip = slots_ref[b * listed + l] >> 1
            hit = functools.reduce(jnp.logical_or, [chip == m for m in members])
            ids_ref[found] = 8 * b + l
            found = found + hit.astype(jnp.int32)
        return found

    return lax.fori_loop(0, blocks, one_block, jnp.int32(0))


def local_place(slot, members):
    if len(members) == 1:
        return slot & 1
    return (slot & 1) + 2 * ((slot >> 1) == members[1]).astype(jnp.int32)


def start_rows(rows_ref, x, sem):
    for b in range(x.shape[0]):
        pltpu.make_async_copy(rows_ref.at[pl.ds(b * BLOCK, BLOCK)], x.at[b], sem.at[b]).start()


def await_rows(rows_ref, x, sem, ready, upto):
    def one(b, _):
        pltpu.make_async_copy(rows_ref.at[pl.ds(0, BLOCK)], x.at[b], sem.at[b]).wait()
        return 0

    lax.fori_loop(ready, upto, one, 0)
    return jnp.maximum(ready, upto)


def load_panels(piece_refs, panels, norms, sem):
    copies = [
        pltpu.make_async_copy(ref, panels.at[p], sem.at[p]) for p, ref in enumerate(piece_refs)
    ]
    for copy in copies:
        copy.start()

    def finish():
        for copy in copies:
            copy.wait()
        for p in range(len(copies)):
            wide = panels[p].astype(jnp.float32)
            norm = jnp.sum(wide * wide, axis=1, keepdims=True)
            norms[p] = jnp.broadcast_to(norm * (0.5 * LOGIT_SCALE * LOG2E), norms.shape[1:])

    return finish


def tile_of(panel, norm, block):
    scores = lax.dot_general(
        panel, block, (((1,), (1,)), ((), ())), preferred_element_type=jnp.float32
    )
    scores = scores * (LOGIT_SCALE * LOG2E) - jnp.concatenate([norm, norm], axis=1)
    top = jnp.max(scores, axis=0, keepdims=True)
    powers = jnp.exp2(scores - top)
    return powers, top, jnp.sum(powers, axis=0, keepdims=True)


def score_loop(members, slots_ref, ids, found, listed, x, panels, norms, tops, masses, wait_rows, put):
    blocks = x.shape[0]
    tops[...] = jnp.full_like(tops, -jnp.inf)
    masses[...] = jnp.zeros_like(masses)

    def two(half, ready):
        work = []
        for side in range(2):
            j = 2 * half + side
            code = ids[jnp.minimum(j, found - 1)]
            b, l = code >> 3, code & 7
            work.append((j, b, l, local_place(slots_ref[b * listed + l], members)))
        ready = wait_rows(ready, work[1][1] + 1)
        tiles = [tile_of(panels[p], norms[p], x[b]) for _, b, _, p in work]
        for (j, b, l, _), (powers, top, mass) in zip(work, tiles):
            put(j, powers)
            tops[pl.ds(l * blocks + b, 1)] = top
            masses[pl.ds(l * blocks + b, 1)] = mass
        return ready

    return lax.fori_loop(0, (found + 1) // 2, two, jnp.int32(0))


def sum_loop(members, slots_ref, ids, found, listed, x, shares, acc, totals, wait_rows, ready, get):
    blocks = x.shape[0]
    cent = totals.shape[1]

    def two(half, ready):
        work = []
        for side in range(2):
            j = 2 * half + side
            code = ids[jnp.minimum(j, found - 1)]
            b, l = code >> 3, code & 7
            work.append((j, b, l, local_place(slots_ref[b * listed + l], members)))
        ready = wait_rows(ready, work[1][1] + 1)
        live = (work[1][0] < found).astype(jnp.float32)
        for side, (j, b, l, p) in enumerate(work):
            share = shares[pl.ds(l * blocks + b, 1)]
            if side:
                share = share * live
            weights = (get(j) * share).astype(jnp.bfloat16)
            wide = weights.astype(jnp.float32)
            totals[p] += wide[:, :128] + wide[:, 128:]
            acc[p, pl.ds(0, cent)] += jnp.dot(weights, x[b], preferred_element_type=jnp.float32)
        return ready

    return lax.fori_loop(0, (found + 1) // 2, two, ready)


def clear_sums(acc, totals):
    acc[...] = jnp.zeros_like(acc)
    totals[...] = jnp.zeros_like(totals)


def store_sums(acc, totals, out_refs, sem):
    cent = totals.shape[1]
    copies = []
    for p, ref in enumerate(out_refs):
        row = jnp.sum(totals[p].T, axis=0, keepdims=True)
        acc[p, pl.ds(cent, EXTRA), pl.ds(0, cent)] = jnp.broadcast_to(row, (EXTRA, cent))
        copies.append(pltpu.make_async_copy(acc.at[p], ref, sem.at[p]))
        copies[-1].start()
    for copy in copies:
        copy.wait()


def score_kernel(members, listed, slots_ref, rows_ref, *refs):
    pieces = 2 * len(members)
    piece_refs = refs[:pieces]
    tiles_ref, tops, masses, x, panels, norms, ring, ids, row_sem, panel_sem, ring_sem = refs[pieces:]
    blocks = x.shape[0]
    finish_panels = load_panels(piece_refs, panels, norms, panel_sem)
    start_rows(rows_ref, x, row_sem)
    found = collect(slots_ref, members, ids, blocks, listed)
    finish_panels()

    def outgoing(j):
        slot = j % DEPTH
        return pltpu.make_async_copy(ring.at[slot], tiles_ref.at[j], ring_sem.at[slot])

    def put(j, powers):
        @pl.when(j >= DEPTH)
        def _():
            outgoing(j - DEPTH).wait()

        ring[j % DEPTH] = powers
        outgoing(j).start()

    wait_rows = functools.partial(await_rows, rows_ref, x, row_sem)
    ready = score_loop(
        members, slots_ref, ids, found, listed, x, panels, norms, tops, masses, wait_rows, put
    )
    written = (found + 1) // 2 * 2
    lax.fori_loop(jnp.maximum(written - DEPTH, 0), written, lambda j, _: (outgoing(j).wait(), 0)[1], 0)
    wait_rows(ready, blocks)


def sum_kernel(members, listed, slots_ref, rows_ref, tiles_ref, shares, *refs):
    pieces = 2 * len(members)
    out_refs = refs[:pieces]
    x, acc, totals, ring, ids, row_sem, ring_sem, out_sem = refs[pieces:]
    blocks = x.shape[0]
    start_rows(rows_ref, x, row_sem)
    found = collect(slots_ref, members, ids, blocks, listed)
    held = (found + 1) // 2 * 2

    def incoming(j):
        slot = j % DEPTH
        return pltpu.make_async_copy(tiles_ref.at[j], ring.at[slot], ring_sem.at[slot])

    lax.fori_loop(0, jnp.minimum(held, DEPTH), lambda j, _: (incoming(j).start(), 0)[1], 0)
    clear_sums(acc, totals)

    def get(j):
        incoming(j).wait()
        return ring[j % DEPTH]

    def wait_rows(ready, upto):
        return await_rows(rows_ref, x, row_sem, ready, upto)

    cent = totals.shape[1]

    def two(half, ready):
        work = []
        for side in range(2):
            j = 2 * half + side
            code = ids[jnp.minimum(j, found - 1)]
            b, l = code >> 3, code & 7
            work.append((j, b, l, local_place(slots_ref[b * listed + l], members)))
        ready = wait_rows(ready, work[1][1] + 1)
        live = (work[1][0] < found).astype(jnp.float32)
        for side, (j, b, l, p) in enumerate(work):
            share = shares[pl.ds(l * blocks + b, 1)]
            if side:
                share = share * live
            weights = (get(j) * share).astype(jnp.bfloat16)
            wide = weights.astype(jnp.float32)
            totals[p] += wide[:, :128] + wide[:, 128:]
            acc[p, pl.ds(0, cent)] += jnp.dot(weights, x[b], preferred_element_type=jnp.float32)
        for j, _, _, _ in work:

            @pl.when(j + DEPTH < held)
            def _(j=j):
                incoming(j + DEPTH).start()

        return ready

    ready = lax.fori_loop(0, held // 2, two, jnp.int32(0))
    store_sums(acc, totals, out_refs, out_sem)
    wait_rows(ready, blocks)


def middle_kernel(members, listed, earlier, slots_ref, rows_ref, *refs):
    pieces = 2 * len(members)
    stat_refs = refs[: 2 * earlier]
    piece_refs = refs[2 * earlier : 2 * earlier + pieces]
    refs = refs[2 * earlier + pieces :]
    logs_ref, shares = refs[:2]
    out_refs = refs[2 : 2 + pieces]
    refs = refs[2 + pieces :]
    x, panels, norms, tiles, tops, masses, acc, totals, ids, row_sem, panel_sem, out_sem = refs
    blocks = x.shape[0]
    finish_panels = load_panels(piece_refs, panels, norms, panel_sem)
    start_rows(rows_ref, x, row_sem)
    found = collect(slots_ref, members, ids, blocks, listed)
    finish_panels()

    def put(j, powers):
        tiles[j] = powers

    def get(j):
        return tiles[j]

    wait_rows = functools.partial(await_rows, rows_ref, x, row_sem)
    ready = score_loop(
        members, slots_ref, ids, found, listed, x, panels, norms, tops, masses, wait_rows, put
    )
    clear_sums(acc, totals)
    width = tops.shape[1]
    top = functools.reduce(jnp.maximum, [ref[...] for ref in stat_refs[:earlier]], tops[...])
    mass = functools.reduce(jnp.add, [ref[...] for ref in stat_refs[earlier:]], masses[...])
    top = top.reshape(listed, blocks, width)
    mass = mass.reshape(listed, blocks, width)
    highest = jnp.max(top, axis=0)
    factor = jnp.exp2(top - highest[None])
    whole = jnp.sum(factor * mass, axis=0)
    logs_ref[...] = (highest + jnp.log2(whole)) * (1.0 / LOG2E)
    shares[...] = (factor / whole[None]).reshape(listed * blocks, width)
    ready = sum_loop(
        members, slots_ref, ids, found, listed, x, shares, acc, totals, wait_rows, ready, get
    )
    store_sums(acc, totals, out_refs, out_sem)
    wait_rows(ready, blocks)


SMEM = pl.BlockSpec(memory_space=pltpu.SMEM)
ANY = pl.BlockSpec(memory_space=pl.ANY)
VMEM = pl.BlockSpec(memory_space=pltpu.VMEM)


class Sizes:
    def __init__(self, rows, slots, cent):
        self.blocks, self.listed = slots.shape
        self.width = rows.shape[1]
        self.cent = cent
        self.stats = jax.ShapeDtypeStruct((self.listed * self.blocks, BLOCK), jnp.float32)
        self.sums = jax.ShapeDtypeStruct((cent + EXTRA, self.width), jnp.float32)

    def tiles(self, members):
        return self.blocks * min(2 * len(members), self.listed) + 2

    def cost(self, members, products):
        share = 2 * len(members) / 14
        pairs = self.blocks * self.listed * share
        return pl.CostEstimate(
            flops=int(2 * products * pairs * self.cent * BLOCK * self.width),
            bytes_accessed=int(2 * self.blocks * BLOCK * self.width + 4 * pairs * self.cent * BLOCK),
            transcendentals=int(pairs * self.cent * BLOCK),
        )

    def rows_scratch(self):
        return pltpu.VMEM((self.blocks, BLOCK, self.width), jnp.bfloat16)

    def panel_scratch(self, pieces):
        return [
            pltpu.VMEM((pieces, self.cent, self.width), jnp.bfloat16),
            pltpu.VMEM((pieces, self.cent, 128), jnp.float32),
        ]

    def sum_scratch(self, pieces):
        return [
            pltpu.VMEM((pieces, self.cent + EXTRA, self.width), jnp.float32),
            pltpu.VMEM((pieces, self.cent, 128), jnp.float32),
        ]

    def ids_scratch(self):
        return pltpu.SMEM((self.blocks * self.listed + 8,), jnp.int32)


def score_group(sizes, members, slots, rows, pieces):
    count = len(pieces)
    return pl.pallas_call(
        functools.partial(score_kernel, members, sizes.listed),
        out_shape=(
            jax.ShapeDtypeStruct((sizes.tiles(members), sizes.cent, BLOCK), jnp.float32),
            sizes.stats,
            sizes.stats,
        ),
        in_specs=[SMEM, ANY] + [ANY] * count,
        out_specs=(ANY, VMEM, VMEM),
        scratch_shapes=[sizes.rows_scratch()]
        + sizes.panel_scratch(count)
        + [
            pltpu.VMEM((DEPTH, sizes.cent, BLOCK), jnp.float32),
            sizes.ids_scratch(),
            pltpu.SemaphoreType.DMA((sizes.blocks,)),
            pltpu.SemaphoreType.DMA((count,)),
            pltpu.SemaphoreType.DMA((DEPTH,)),
        ],
        compiler_params=pltpu.CompilerParams(vmem_limit_bytes=24 << 20),
        cost_estimate=sizes.cost(members, 1),
        name="score_group",
    )(slots, rows, *pieces)


def sum_group(sizes, members, slots, rows, tiles, shares):
    count = 2 * len(members)
    return pl.pallas_call(
        functools.partial(sum_kernel, members, sizes.listed),
        out_shape=(sizes.sums,) * count,
        in_specs=[SMEM, ANY, ANY, VMEM],
        out_specs=(ANY,) * count,
        scratch_shapes=[sizes.rows_scratch()]
        + sizes.sum_scratch(count)
        + [
            pltpu.VMEM((DEPTH, sizes.cent, BLOCK), jnp.float32),
            sizes.ids_scratch(),
            pltpu.SemaphoreType.DMA((sizes.blocks,)),
            pltpu.SemaphoreType.DMA((DEPTH,)),
            pltpu.SemaphoreType.DMA((count,)),
        ],
        compiler_params=pltpu.CompilerParams(vmem_limit_bytes=24 << 20),
        cost_estimate=sizes.cost(members, 1),
        name="sum_group",
    )(slots, rows, tiles, shares)


def middle_group(sizes, members, slots, rows, tops, masses, pieces):
    count = len(pieces)
    earlier = len(tops)
    return pl.pallas_call(
        functools.partial(middle_kernel, members, sizes.listed, earlier),
        out_shape=(jax.ShapeDtypeStruct((sizes.blocks, BLOCK), jnp.float32), sizes.stats)
        + (sizes.sums,) * count,
        in_specs=[SMEM, ANY] + [VMEM] * (2 * earlier) + [ANY] * count,
        out_specs=(VMEM, VMEM) + (ANY,) * count,
        scratch_shapes=[sizes.rows_scratch()]
        + sizes.panel_scratch(count)
        + [
            pltpu.VMEM((sizes.tiles(members), sizes.cent, BLOCK), jnp.float32),
            pltpu.VMEM(sizes.stats.shape, jnp.float32),
            pltpu.VMEM(sizes.stats.shape, jnp.float32),
        ]
        + sizes.sum_scratch(count)
        + [
            sizes.ids_scratch(),
            pltpu.SemaphoreType.DMA((sizes.blocks,)),
            pltpu.SemaphoreType.DMA((count,)),
            pltpu.SemaphoreType.DMA((count,)),
        ],
        compiler_params=pltpu.CompilerParams(vmem_limit_bytes=44 << 20),
        cost_estimate=sizes.cost(members, 2),
        name="middle_group",
    )(slots, rows, *tops, *masses, *pieces)


def on_device(rows, centroids, lists):
    count = lax.axis_size("blk")
    device = lax.axis_index("blk")
    cent = centroids.shape[0]
    own, stages = plan_of(count)
    groups = [(own,)] + [tuple(q for q, _, _ in stage) for stage in stages]
    slots = (2 * chip_place(lists, device, count) + ((lists ^ device) & 1)).astype(jnp.int32)
    sizes = Sizes(rows, slots, cent)
    slots = slots.reshape(-1)

    near = {own: centroids}
    tiles, tops, masses = [], [], []
    for members, stage in zip(groups, stages):
        arriving = [moved(near[source], shift) for _, source, shift in stage]
        pieces = [v for q in members for v in (near[q], other_core(near[q]))]
        scored = score_group(sizes, members, slots, rows, pieces)
        arriving, scored, near = lax.optimization_barrier((arriving, scored, near))
        tiles.append(scored[0])
        tops.append(scored[1])
        masses.append(scored[2])
        for (q, _, _), value in zip(stage, arriving):
            near[q] = value
    members = groups[-1]
    pieces = [v for q in members for v in (near[q], other_core(near[q]))]
    log_totals, shares, *sums = middle_group(sizes, members, slots, rows, tops, masses, pieces)

    total = {}
    back = {}
    for at in reversed(range(len(groups))):
        for q, (mine, theirs) in zip(groups[at], zip(sums[::2], sums[1::2])):
            total[q] = (mine + other_core(theirs)) * LINK_SCALE
            for value in back.pop(q, ()):
                total[q] = total[q] + value.astype(jnp.float32)
        if at:
            leaving = [total[q].astype(jnp.float16) for q, _, _ in stages[at - 1]]
            leaving, shares = lax.optimization_barrier((leaving, shares))
            for value, (q, source, shift) in zip(leaving, stages[at - 1]):
                arrived = moved(value, shift if shift is None else -shift)
                back.setdefault(source, []).append(arrived)
            sums = sum_group(sizes, groups[at - 1], slots, rows, tiles[at - 1], shares)
    own_sums = total[own] * (1.0 / LINK_SCALE)
    updated = (own_sums[:cent] + PRIOR_MASS * centroids.astype(jnp.float32)) / (
        own_sums[cent, :cent][:, None] + PRIOR_MASS
    )
    return updated, log_totals.reshape(-1)


def solution(mesh):
    placed = P(("groups", "blk"), None)
    return jax.shard_map(
        on_device,
        mesh=mesh,
        in_specs=(placed, placed, placed),
        out_specs=(placed, P(("groups", "blk"))),
        check_vma=False,
    )
```

```python
import functools
import math

import jax
import jax.numpy as jnp
from jax import lax
from jax.experimental import pallas as pl
from jax.experimental.pallas import tpu as pltpu
from jax.sharding import PartitionSpec as P

BLOCK = 256
SPAN = 6
LOGIT_SCALE = 0.25
PRIOR_MASS = 8.0
LOG2E = math.log2(math.e)
LINK_SCALE = 1.0 / 16.0
EXTRA = 8
DEPTH = 4


def grid_plan():
    return 0, (
        ((2, 0, 4), (1, 0, None)),
        ((6, 0, -4), (3, 2, None)),
        ((5, 3, 4), (7, 6, None)),
    )


def ring_plan():
    reach = (SPAN + 1) // 2
    return reach, tuple(
        ((reach + hop + 1, reach + hop, 2), (reach - hop - 1, reach - hop, -2)) for hop in range(reach)
    )


def plan_of(count):
    return grid_plan() if count == 16 else ring_plan()


def chip_place(panel, device, count):
    if count == 16:
        return (device // 4 - panel // 4) % 4 * 2 + ((panel ^ device) >> 1 & 1)
    return (device // 2 - panel // 2 + (SPAN + 1) // 2) % (count // 2)


def moved(value, shift):
    count = lax.axis_size("blk")
    if shift is None:
        return lax.ppermute(value, "blk", [(i, i ^ 2) for i in range(count)])
    return lax.ppermute(value, "blk", [(i, (i + shift) % count) for i in range(count)])


def other_core(value):
    count = lax.axis_size("blk")
    return lax.ppermute(value, "blk", [(i, i ^ 1) for i in range(count)])


def collect(slots_ref, members, ids_ref, blocks, listed):
    def one_block(b, found):
        for l in range(listed):
            chip = slots_ref[b * listed + l] >> 1
            hit = functools.reduce(jnp.logical_or, [chip == m for m in members])
            ids_ref[found] = 8 * b + l
            found = found + hit.astype(jnp.int32)
        return found

    return lax.fori_loop(0, blocks, one_block, jnp.int32(0))


def local_place(slot, members):
    if len(members) == 1:
        return slot & 1
    return (slot & 1) + 2 * ((slot >> 1) == members[1]).astype(jnp.int32)


def start_rows(rows_ref, x, sem):
    for b in range(x.shape[0]):
        pltpu.make_async_copy(rows_ref.at[pl.ds(b * BLOCK, BLOCK)], x.at[b], sem.at[b]).start()


def await_rows(rows_ref, x, sem, ready, upto):
    def one(b, _):
        pltpu.make_async_copy(rows_ref.at[pl.ds(0, BLOCK)], x.at[b], sem.at[b]).wait()
        return 0

    lax.fori_loop(ready, upto, one, 0)
    return jnp.maximum(ready, upto)


def load_panels(piece_refs, panels, norms, sem):
    copies = [
        pltpu.make_async_copy(ref, panels.at[p], sem.at[p]) for p, ref in enumerate(piece_refs)
    ]
    for copy in copies:
        copy.start()

    def finish():
        for copy in copies:
            copy.wait()
        for p in range(len(copies)):
            wide = panels[p].astype(jnp.float32)
            norm = jnp.sum(wide * wide, axis=1, keepdims=True)
            norms[p] = jnp.broadcast_to(norm * (0.5 * LOGIT_SCALE * LOG2E), norms.shape[1:])

    return finish


def tile_of(panel, norm, block):
    scores = lax.dot_general(
        panel, block, (((1,), (1,)), ((), ())), preferred_element_type=jnp.float32
    )
    scores = scores * (LOGIT_SCALE * LOG2E) - jnp.concatenate([norm, norm], axis=1)
    top = jnp.max(scores, axis=0, keepdims=True)
    powers = jnp.exp2(scores - top)
    return powers, top, jnp.sum(powers, axis=0, keepdims=True)


def score_loop(members, slots_ref, ids, found, listed, x, panels, norms, tops, masses, wait_rows, put):
    blocks = x.shape[0]
    tops[...] = jnp.full_like(tops, -jnp.inf)
    masses[...] = jnp.zeros_like(masses)

    def two(half, ready):
        work = []
        for side in range(2):
            j = 2 * half + side
            code = ids[jnp.minimum(j, found - 1)]
            b, l = code >> 3, code & 7
            work.append((j, b, l, local_place(slots_ref[b * listed + l], members)))
        ready = wait_rows(ready, work[1][1] + 1)
        tiles = [tile_of(panels[p], norms[p], x[b]) for _, b, _, p in work]
        for (j, b, l, _), (powers, top, mass) in zip(work, tiles):
            put(j, powers)
            tops[pl.ds(l * blocks + b, 1)] = top
            masses[pl.ds(l * blocks + b, 1)] = mass
        return ready

    return lax.fori_loop(0, (found + 1) // 2, two, jnp.int32(0))


def sum_loop(members, slots_ref, ids, found, listed, x, shares, acc, totals, wait_rows, ready, get):
    blocks = x.shape[0]
    cent = totals.shape[1]

    def two(half, ready):
        work = []
        for side in range(2):
            j = 2 * half + side
            code = ids[jnp.minimum(j, found - 1)]
            b, l = code >> 3, code & 7
            work.append((j, b, l, local_place(slots_ref[b * listed + l], members)))
        ready = wait_rows(ready, work[1][1] + 1)
        live = (work[1][0] < found).astype(jnp.float32)
        for side, (j, b, l, p) in enumerate(work):
            share = shares[pl.ds(l * blocks + b, 1)]
            if side:
                share = share * live
            weights = (get(j) * share).astype(jnp.bfloat16)
            wide = weights.astype(jnp.float32)
            totals[p] += wide[:, :128] + wide[:, 128:]
            acc[p, pl.ds(0, cent)] += jnp.dot(weights, x[b], preferred_element_type=jnp.float32)
        return ready

    return lax.fori_loop(0, (found + 1) // 2, two, ready)


def clear_sums(acc, totals):
    acc[...] = jnp.zeros_like(acc)
    totals[...] = jnp.zeros_like(totals)


def store_sums(acc, totals, out_refs, sem):
    cent = totals.shape[1]
    copies = []
    for p, ref in enumerate(out_refs):
        row = jnp.sum(totals[p].T, axis=0, keepdims=True)
        acc[p, pl.ds(cent, EXTRA), pl.ds(0, cent)] = jnp.broadcast_to(row, (EXTRA, cent))
        copies.append(pltpu.make_async_copy(acc.at[p], ref, sem.at[p]))
        copies[-1].start()
    for copy in copies:
        copy.wait()


def score_kernel(members, listed, slots_ref, rows_ref, *refs):
    pieces = 2 * len(members)
    piece_refs = refs[:pieces]
    tiles_ref, tops, masses, x, panels, norms, ring, ids, row_sem, panel_sem, ring_sem = refs[pieces:]
    blocks = x.shape[0]
    finish_panels = load_panels(piece_refs, panels, norms, panel_sem)
    start_rows(rows_ref, x, row_sem)
    found = collect(slots_ref, members, ids, blocks, listed)
    finish_panels()

    def outgoing(j):
        slot = j % DEPTH
        return pltpu.make_async_copy(ring.at[slot], tiles_ref.at[j], ring_sem.at[slot])

    def put(j, powers):
        @pl.when(j >= DEPTH)
        def _():
            outgoing(j - DEPTH).wait()

        ring[j % DEPTH] = powers
        outgoing(j).start()

    wait_rows = functools.partial(await_rows, rows_ref, x, row_sem)
    ready = score_loop(
        members, slots_ref, ids, found, listed, x, panels, norms, tops, masses, wait_rows, put
    )
    written = (found + 1) // 2 * 2
    lax.fori_loop(jnp.maximum(written - DEPTH, 0), written, lambda j, _: (outgoing(j).wait(), 0)[1], 0)
    wait_rows(ready, blocks)


def sum_kernel(members, listed, slots_ref, rows_ref, tiles_ref, shares, *refs):
    pieces = 2 * len(members)
    out_refs = refs[:pieces]
    x, acc, totals, ring, ids, row_sem, ring_sem, out_sem = refs[pieces:]
    blocks = x.shape[0]
    start_rows(rows_ref, x, row_sem)
    found = collect(slots_ref, members, ids, blocks, listed)
    held = (found + 1) // 2 * 2

    def incoming(j):
        slot = j % DEPTH
        return pltpu.make_async_copy(tiles_ref.at[j], ring.at[slot], ring_sem.at[slot])

    lax.fori_loop(0, jnp.minimum(held, DEPTH), lambda j, _: (incoming(j).start(), 0)[1], 0)
    clear_sums(acc, totals)

    def get(j):
        incoming(j).wait()
        return ring[j % DEPTH]

    def wait_rows(ready, upto):
        return await_rows(rows_ref, x, row_sem, ready, upto)

    cent = totals.shape[1]

    def two(half, ready):
        work = []
        for side in range(2):
            j = 2 * half + side
            code = ids[jnp.minimum(j, found - 1)]
            b, l = code >> 3, code & 7
            work.append((j, b, l, local_place(slots_ref[b * listed + l], members)))
        ready = wait_rows(ready, work[1][1] + 1)
        live = (work[1][0] < found).astype(jnp.float32)
        for side, (j, b, l, p) in enumerate(work):
            share = shares[pl.ds(l * blocks + b, 1)]
            if side:
                share = share * live
            weights = (get(j) * share).astype(jnp.bfloat16)
            wide = weights.astype(jnp.float32)
            totals[p] += wide[:, :128] + wide[:, 128:]
            acc[p, pl.ds(0, cent)] += jnp.dot(weights, x[b], preferred_element_type=jnp.float32)
        for j, _, _, _ in work:

            @pl.when(j + DEPTH < held)
            def _(j=j):
                incoming(j + DEPTH).start()

        return ready

    ready = lax.fori_loop(0, held // 2, two, jnp.int32(0))
    store_sums(acc, totals, out_refs, out_sem)
    wait_rows(ready, blocks)


def middle_kernel(members, listed, earlier, slots_ref, rows_ref, *refs):
    pieces = 2 * len(members)
    stat_refs = refs[: 2 * earlier]
    piece_refs = refs[2 * earlier : 2 * earlier + pieces]
    refs = refs[2 * earlier + pieces :]
    logs_ref, shares = refs[:2]
    out_refs = refs[2 : 2 + pieces]
    refs = refs[2 + pieces :]
    x, panels, norms, tiles, tops, masses, acc, totals, ids, row_sem, panel_sem, out_sem = refs
    blocks = x.shape[0]
    finish_panels = load_panels(piece_refs, panels, norms, panel_sem)
    start_rows(rows_ref, x, row_sem)
    found = collect(slots_ref, members, ids, blocks, listed)
    finish_panels()

    def put(j, powers):
        tiles[j] = powers

    def get(j):
        return tiles[j]

    wait_rows = functools.partial(await_rows, rows_ref, x, row_sem)
    ready = score_loop(
        members, slots_ref, ids, found, listed, x, panels, norms, tops, masses, wait_rows, put
    )
    clear_sums(acc, totals)
    width = tops.shape[1]
    top = functools.reduce(jnp.maximum, [ref[...] for ref in stat_refs[:earlier]], tops[...])
    mass = functools.reduce(jnp.add, [ref[...] for ref in stat_refs[earlier:]], masses[...])
    top = top.reshape(listed, blocks, width)
    mass = mass.reshape(listed, blocks, width)
    highest = jnp.max(top, axis=0)
    factor = jnp.exp2(top - highest[None])
    whole = jnp.sum(factor * mass, axis=0)
    logs_ref[...] = (highest + jnp.log2(whole)) * (1.0 / LOG2E)
    shares[...] = (factor / whole[None]).reshape(listed * blocks, width)
    ready = sum_loop(
        members, slots_ref, ids, found, listed, x, shares, acc, totals, wait_rows, ready, get
    )
    store_sums(acc, totals, out_refs, out_sem)
    wait_rows(ready, blocks)


SMEM = pl.BlockSpec(memory_space=pltpu.SMEM)
ANY = pl.BlockSpec(memory_space=pl.ANY)
HBM = pl.BlockSpec(memory_space=pltpu.HBM)
VMEM = pl.BlockSpec(memory_space=pltpu.VMEM)


class Sizes:
    def __init__(self, rows, slots, cent):
        self.blocks, self.listed = slots.shape
        self.width = rows.shape[1]
        self.cent = cent
        self.stats = jax.ShapeDtypeStruct((self.listed * self.blocks, BLOCK), jnp.float32)
        self.sums = jax.ShapeDtypeStruct((cent + EXTRA, self.width), jnp.float32)

    def tiles(self, members):
        return self.blocks * 4 + 2

    def cost(self, members, products):
        share = 2 * len(members) / 14
        pairs = self.blocks * self.listed * share
        return pl.CostEstimate(
            flops=int(2 * products * pairs * self.cent * BLOCK * self.width),
            bytes_accessed=int(2 * self.blocks * BLOCK * self.width + 4 * pairs * self.cent * BLOCK),
            transcendentals=int(pairs * self.cent * BLOCK),
        )

    def rows_scratch(self):
        return pltpu.VMEM((self.blocks, BLOCK, self.width), jnp.bfloat16)

    def panel_scratch(self, pieces):
        return [
            pltpu.VMEM((pieces, self.cent, self.width), jnp.bfloat16),
            pltpu.VMEM((pieces, self.cent, 128), jnp.float32),
        ]

    def sum_scratch(self, pieces):
        return [
            pltpu.VMEM((pieces, self.cent + EXTRA, self.width), jnp.float32),
            pltpu.VMEM((pieces, self.cent, 128), jnp.float32),
        ]

    def ids_scratch(self):
        return pltpu.SMEM((self.blocks * self.listed + 8,), jnp.int32)


def score_group(sizes, members, slots, rows, pieces):
    count = len(pieces)
    return pl.pallas_call(
        functools.partial(score_kernel, members, sizes.listed),
        out_shape=(
            jax.ShapeDtypeStruct((sizes.tiles(members), sizes.cent, BLOCK), jnp.float32),
            sizes.stats,
            sizes.stats,
        ),
        in_specs=[SMEM, HBM] + [ANY] * count,
        out_specs=(HBM, VMEM, VMEM),
        scratch_shapes=[sizes.rows_scratch()]
        + sizes.panel_scratch(count)
        + [
            pltpu.VMEM((DEPTH, sizes.cent, BLOCK), jnp.float32),
            sizes.ids_scratch(),
            pltpu.SemaphoreType.DMA((sizes.blocks,)),
            pltpu.SemaphoreType.DMA((count,)),
            pltpu.SemaphoreType.DMA((DEPTH,)),
        ],
        compiler_params=pltpu.CompilerParams(vmem_limit_bytes=48 << 20),
        cost_estimate=sizes.cost(members, 1),
        name="score_group",
    )(slots, rows, *pieces)


def sum_group(sizes, members, slots, rows, tiles, shares):
    count = 2 * len(members)
    return pl.pallas_call(
        functools.partial(sum_kernel, members, sizes.listed),
        out_shape=(sizes.sums,) * count,
        in_specs=[SMEM, HBM, HBM, VMEM],
        out_specs=(ANY,) * count,
        scratch_shapes=[sizes.rows_scratch()]
        + sizes.sum_scratch(count)
        + [
            pltpu.VMEM((DEPTH, sizes.cent, BLOCK), jnp.float32),
            sizes.ids_scratch(),
            pltpu.SemaphoreType.DMA((sizes.blocks,)),
            pltpu.SemaphoreType.DMA((DEPTH,)),
            pltpu.SemaphoreType.DMA((count,)),
        ],
        compiler_params=pltpu.CompilerParams(vmem_limit_bytes=48 << 20),
        cost_estimate=sizes.cost(members, 1),
        name="sum_group",
    )(slots, rows, tiles, shares)


def middle_group(sizes, members, slots, rows, tops, masses, pieces):
    count = len(pieces)
    earlier = len(tops)
    return pl.pallas_call(
        functools.partial(middle_kernel, members, sizes.listed, earlier),
        out_shape=(jax.ShapeDtypeStruct((sizes.blocks, BLOCK), jnp.float32), sizes.stats)
        + (sizes.sums,) * count,
        in_specs=[SMEM, HBM] + [VMEM] * (2 * earlier) + [ANY] * count,
        out_specs=(VMEM, VMEM) + (ANY,) * count,
        scratch_shapes=[sizes.rows_scratch()]
        + sizes.panel_scratch(count)
        + [
            pltpu.VMEM((sizes.tiles(members), sizes.cent, BLOCK), jnp.float32),
            pltpu.VMEM(sizes.stats.shape, jnp.float32),
            pltpu.VMEM(sizes.stats.shape, jnp.float32),
        ]
        + sizes.sum_scratch(count)
        + [
            sizes.ids_scratch(),
            pltpu.SemaphoreType.DMA((sizes.blocks,)),
            pltpu.SemaphoreType.DMA((count,)),
            pltpu.SemaphoreType.DMA((count,)),
        ],
        compiler_params=pltpu.CompilerParams(vmem_limit_bytes=48 << 20),
        cost_estimate=sizes.cost(members, 2),
        name="middle_group",
    )(slots, rows, *tops, *masses, *pieces)


def on_device(rows, centroids, lists):
    count = lax.axis_size("blk")
    device = lax.axis_index("blk")
    cent = centroids.shape[0]
    own, stages = plan_of(count)
    groups = [(own,)] + [tuple(q for q, _, _ in stage) for stage in stages]
    slots = (2 * chip_place(lists, device, count) + ((lists ^ device) & 1)).astype(jnp.int32)
    sizes = Sizes(rows, slots, cent)
    slots = slots.reshape(-1)

    near = {own: centroids}
    tiles, tops, masses = [], [], []
    for members, stage in zip(groups, stages):
        arriving = [moved(near[source], shift) for _, source, shift in stage]
        pieces = [v for q in members for v in (near[q], other_core(near[q]))]
        scored = score_group(sizes, members, slots, rows, pieces)
        arriving, scored, near = lax.optimization_barrier((arriving, scored, near))
        tiles.append(scored[0])
        tops.append(scored[1])
        masses.append(scored[2])
        for (q, _, _), value in zip(stage, arriving):
            near[q] = value
    members = groups[-1]
    pieces = [v for q in members for v in (near[q], other_core(near[q]))]
    log_totals, shares, *sums = middle_group(sizes, members, slots, rows, tops, masses, pieces)

    back = {q: [] for members in groups for q in members}
    sums = {q: pair for q, pair in zip(groups[-1], zip(sums[::2], sums[1::2]))}
    arriving = []
    for at in reversed(range(len(groups))):
        crossed = {q: other_core(theirs) for q, (_, theirs) in sums.items()}
        ahead = []
        if at:
            ahead = sum_group(sizes, groups[at - 1], slots, rows, tiles[at - 1], shares)
        crossed, ahead, arriving, shares = lax.optimization_barrier((crossed, ahead, arriving, shares))
        if arriving:
            for value, (_, source, _) in zip(arriving, stages[at]):
                back[source].append(value)
        total = {}
        for q, (mine, _) in sums.items():
            total[q] = (mine + crossed[q]) * LINK_SCALE
            for value in back[q]:
                total[q] = total[q] + value.astype(jnp.float32)
        if at:
            arriving = [
                moved(total[q].astype(jnp.float16), shift if shift is None else -shift)
                for q, _, shift in stages[at - 1]
            ]
            sums = {q: pair for q, pair in zip(groups[at - 1], zip(ahead[::2], ahead[1::2]))}
    own_sums = total[own] * (1.0 / LINK_SCALE)
    updated = (own_sums[:cent] + PRIOR_MASS * centroids.astype(jnp.float32)) / (
        own_sums[cent, :cent][:, None] + PRIOR_MASS
    )
    return updated, log_totals.reshape(-1)


def solution(mesh):
    placed = P(("groups", "blk"), None)
    return jax.shard_map(
        on_device,
        mesh=mesh,
        in_specs=(placed, placed, placed),
        out_specs=(placed, P(("groups", "blk"))),
        check_vma=False,
    )
```

```python
import functools
import math

import jax
import jax.numpy as jnp
from jax import lax
from jax.experimental import pallas as pl
from jax.experimental.pallas import tpu as pltpu
from jax.sharding import PartitionSpec as P

BLOCK = 256
SPAN = 6
LOGIT_SCALE = 0.25
PRIOR_MASS = 8.0
LOG2E = math.log2(math.e)
LINK_SCALE = 1.0 / 16.0
EXTRA = 8
VMEM_GRANT = 42 << 20


def grid_plan():
    return 0, (
        ((2, 0, 4), (1, 0, None)),
        ((6, 0, -4), (3, 2, None)),
        ((5, 3, 4), (7, 6, None)),
    )


def ring_plan():
    reach = (SPAN + 1) // 2
    return reach, tuple(
        ((reach + hop + 1, reach + hop, 2), (reach - hop - 1, reach - hop, -2)) for hop in range(reach)
    )


def plan_of(count):
    return grid_plan() if count == 16 else ring_plan()


def chip_place(panel, device, count):
    if count == 16:
        return (device // 4 - panel // 4) % 4 * 2 + ((panel ^ device) >> 1 & 1)
    return (device // 2 - panel // 2 + (SPAN + 1) // 2) % (count // 2)


def moved(value, shift):
    count = lax.axis_size("blk")
    if shift is None:
        return lax.ppermute(value, "blk", [(i, i ^ 2) for i in range(count)])
    return lax.ppermute(value, "blk", [(i, (i + shift) % count) for i in range(count)])


def other_core(value):
    count = lax.axis_size("blk")
    return lax.ppermute(value, "blk", [(i, i ^ 1) for i in range(count)])


def pairs_of(slots, room):
    blocks, listed = slots.shape
    hit = slots[:, :, None] == jnp.arange(room, dtype=jnp.int32)
    listing = jnp.any(hit, axis=1)
    code = 8 * jnp.arange(blocks, dtype=jnp.int32)[:, None] + jnp.sum(
        jnp.where(hit, jnp.arange(listed, dtype=jnp.int32)[None, :, None], 0), axis=1
    )
    before = jnp.arange(blocks)[:, None] > jnp.arange(blocks)[None, :]
    rank = jnp.sum(jnp.where(before[:, :, None] & listing[None], 1, 0), axis=1)
    chosen = listing[:, :, None] & (rank[:, :, None] == jnp.arange(blocks))
    order = jnp.sum(jnp.where(chosen, code[:, :, None], 0), axis=0)
    return order.reshape(-1).astype(jnp.int32), jnp.sum(listing, axis=0).astype(jnp.int32)


def local_slots(members):
    return [2 * q + core for q in members for core in (0, 1)]


def some_pairs(order_ref, counts_ref, slot, blocks, first, number):
    work = []
    for i in range(number):
        code = order_ref[slot * blocks + jnp.minimum(first + i, counts_ref[slot] - 1)]
        work.append((first + i, code >> 3, (code & 7) * blocks + (code >> 3)))
    return work


def by_fours(count, act):
    fours = count // 4
    lax.fori_loop(0, fours, lambda k, _: (act(4 * k, 4), 0)[1], 0)
    lax.fori_loop(2 * fours, (count + 1) // 2, lambda k, _: (act(2 * k, 2), 0)[1], 0)


def rows_of(x, block):
    return x[pl.ds(pl.multiple_of(block * BLOCK, BLOCK), BLOCK)]


def load_panels(piece_refs, panels, norms, sem):
    copies = [
        pltpu.make_async_copy(ref, panels.at[p], sem.at[p]) for p, ref in enumerate(piece_refs)
    ]
    for copy in copies:
        copy.start()

    def finish():
        for copy in copies:
            copy.wait()
        for p in range(len(copies)):
            wide = panels[p].astype(jnp.float32)
            norm = jnp.sum(wide * wide, axis=1, keepdims=True)
            norms[p] = jnp.broadcast_to(norm * (0.5 * LOGIT_SCALE * LOG2E), norms.shape[1:])

    return finish


def tile_of(panel, norm, block):
    scores = lax.dot_general(
        panel, block, (((1,), (1,)), ((), ())), preferred_element_type=jnp.float32
    )
    scores = scores * (LOGIT_SCALE * LOG2E) - jnp.concatenate([norm, norm], axis=1)
    top = jnp.max(scores, axis=0, keepdims=True)
    powers = jnp.exp2(scores - top)
    return powers, top, jnp.sum(powers, axis=0, keepdims=True)


def score_loop(slots, order_ref, counts_ref, x, panels, norms, tops, masses, tiles, done):
    blocks = x.shape[0] // BLOCK
    tops[...] = jnp.full_like(tops, -jnp.inf)
    masses[...] = jnp.zeros_like(masses)
    for p, slot in enumerate(slots):

        def some(first, number):
            work = some_pairs(order_ref, counts_ref, slot, blocks, first, number)
            found = [tile_of(panels[p], norms[p], rows_of(x, b)) for _, b, _ in work]
            for (i, _, at), (powers, top, mass) in zip(work, found):
                tiles[p * blocks + i] = powers
                tops[pl.ds(at, 1)] = top
                masses[pl.ds(at, 1)] = mass
            for i, _, _ in work:
                done(p * blocks + i)

        by_fours(counts_ref[slot], some)


def sum_loop(slots, order_ref, counts_ref, x, shares, acc, totals, tiles, ready):
    blocks = x.shape[0] // BLOCK
    cent = totals.shape[1]
    for p, slot in enumerate(slots):

        def some(first, number):
            work = some_pairs(order_ref, counts_ref, slot, blocks, first, number)
            for i, _, _ in work:
                ready(p * blocks + i)
            partial, count = None, None
            for i, b, at in work:
                share = shares[pl.ds(at, 1)]
                if number == 2:
                    share = share * (i < counts_ref[slot]).astype(jnp.float32)
                weights = (tiles[p * blocks + i] * share).astype(jnp.bfloat16)
                wide = weights.astype(jnp.float32)
                wide = wide[:, :128] + wide[:, 128:]
                product = jnp.dot(weights, rows_of(x, b), preferred_element_type=jnp.float32)
                partial = product if partial is None else partial + product
                count = wide if count is None else count + wide
            totals[p] += count
            acc[p, pl.ds(0, cent)] += partial

        by_fours(counts_ref[slot], some)


def clear_sums(acc, totals):
    acc[...] = jnp.zeros_like(acc)
    totals[...] = jnp.zeros_like(totals)


def store_sums(acc, totals, out_refs, sem):
    cent = totals.shape[1]
    copies = []
    for p, ref in enumerate(out_refs):
        row = jnp.sum(totals[p].T, axis=0, keepdims=True)
        acc[p, pl.ds(cent, EXTRA), pl.ds(0, cent)] = jnp.broadcast_to(row, (EXTRA, cent))
        copies.append(pltpu.make_async_copy(acc.at[p], ref, sem.at[p]))
        copies[-1].start()
    for copy in copies:
        copy.wait()


def over_tiles(slots, counts_ref, blocks, act):
    for p, slot in enumerate(slots):
        held = (counts_ref[slot] + 1) // 2 * 2
        lax.fori_loop(0, held, lambda i, _: (act(p * blocks + i), 0)[1], 0)


def score_kernel(slots, order_ref, counts_ref, x, *refs):
    pieces = len(slots)
    piece_refs = refs[:pieces]
    tiles_ref, tops, masses, panels, norms, tiles, panel_sem, tile_sem = refs[pieces:]
    load_panels(piece_refs, panels, norms, panel_sem)()

    def outgoing(j):
        return pltpu.make_async_copy(tiles.at[j], tiles_ref.at[j], tile_sem.at[j])

    score_loop(
        slots, order_ref, counts_ref, x, panels, norms, tops, masses, tiles,
        lambda j: outgoing(j).start(),
    )
    over_tiles(slots, counts_ref, x.shape[0] // BLOCK, lambda j: outgoing(j).wait())


def sum_kernel(slots, order_ref, counts_ref, x, tiles_ref, shares, *refs):
    pieces = len(slots)
    out_refs = refs[:pieces]
    acc, totals, tiles, tile_sem, out_sem = refs[pieces:]

    def incoming(j):
        return pltpu.make_async_copy(tiles_ref.at[j], tiles.at[j], tile_sem.at[j])

    over_tiles(slots, counts_ref, x.shape[0] // BLOCK, lambda j: incoming(j).start())
    clear_sums(acc, totals)
    sum_loop(
        slots, order_ref, counts_ref, x, shares, acc, totals, tiles, lambda j: incoming(j).wait()
    )
    store_sums(acc, totals, out_refs, out_sem)


def middle_kernel(slots, listed, earlier, order_ref, counts_ref, x, *refs):
    pieces = len(slots)
    stat_refs = refs[: 2 * earlier]
    piece_refs = refs[2 * earlier : 2 * earlier + pieces]
    refs = refs[2 * earlier + pieces :]
    logs_ref, shares = refs[:2]
    out_refs = refs[2 : 2 + pieces]
    panels, norms, tiles, tops, masses, acc, totals, panel_sem, out_sem = refs[2 + pieces :]
    blocks = x.shape[0] // BLOCK
    finish_panels = load_panels(piece_refs, panels, norms, panel_sem)
    clear_sums(acc, totals)
    finish_panels()
    score_loop(
        slots, order_ref, counts_ref, x, panels, norms, tops, masses, tiles, lambda j: None
    )
    width = tops.shape[1]
    top = functools.reduce(jnp.maximum, [ref[...] for ref in stat_refs[:earlier]], tops[...])
    mass = functools.reduce(jnp.add, [ref[...] for ref in stat_refs[earlier:]], masses[...])
    top = top.reshape(listed, blocks, width)
    mass = mass.reshape(listed, blocks, width)
    highest = jnp.max(top, axis=0)
    factor = jnp.exp2(top - highest[None])
    whole = jnp.sum(factor * mass, axis=0)
    logs_ref[...] = (highest + jnp.log2(whole)) * (1.0 / LOG2E)
    shares[...] = (factor / whole[None]).reshape(listed * blocks, width)
    sum_loop(slots, order_ref, counts_ref, x, shares, acc, totals, tiles, lambda j: None)
    store_sums(acc, totals, out_refs, out_sem)


SMEM = pl.BlockSpec(memory_space=pltpu.SMEM)
ANY = pl.BlockSpec(memory_space=pl.ANY)
HBM = pl.BlockSpec(memory_space=pltpu.HBM)
VMEM = pl.BlockSpec(memory_space=pltpu.VMEM)


class Sizes:
    def __init__(self, rows, blocks, listed, cent):
        self.blocks, self.listed, self.cent = blocks, listed, cent
        self.width = rows.shape[1]
        self.stats = jax.ShapeDtypeStruct((listed * blocks, BLOCK), jnp.float32)
        self.sums = jax.ShapeDtypeStruct((cent + EXTRA, self.width), jnp.float32)
        self.tiles = jax.ShapeDtypeStruct((4 * blocks, cent, BLOCK), jnp.float32)

    def cost(self, members, products):
        pairs = self.blocks * self.listed * 2 * len(members) / 14
        return pl.CostEstimate(
            flops=int(2 * products * pairs * self.cent * BLOCK * self.width),
            bytes_accessed=int(2 * self.blocks * BLOCK * self.width + 4 * pairs * self.cent * BLOCK),
            transcendentals=int(pairs * self.cent * BLOCK),
        )

    def panel_scratch(self, pieces):
        return [
            pltpu.VMEM((pieces, self.cent, self.width), jnp.bfloat16),
            pltpu.VMEM((pieces, self.cent, 128), jnp.float32),
        ]

    def sum_scratch(self, pieces):
        return [
            pltpu.VMEM((pieces, self.cent + EXTRA, self.width), jnp.float32),
            pltpu.VMEM((pieces, self.cent, 128), jnp.float32),
        ]

    def tile_scratch(self, pieces):
        return pltpu.VMEM((pieces * self.blocks, self.cent, BLOCK), jnp.float32)


def score_group(sizes, members, order, counts, rows, pieces):
    count = len(pieces)
    return pl.pallas_call(
        functools.partial(score_kernel, local_slots(members)),
        out_shape=(sizes.tiles, sizes.stats, sizes.stats),
        in_specs=[SMEM, SMEM, VMEM] + [ANY] * count,
        out_specs=(HBM, VMEM, VMEM),
        scratch_shapes=sizes.panel_scratch(count)
        + [
            sizes.tile_scratch(count),
            pltpu.SemaphoreType.DMA((count,)),
            pltpu.SemaphoreType.DMA((count * sizes.blocks,)),
        ],
        compiler_params=pltpu.CompilerParams(vmem_limit_bytes=VMEM_GRANT),
        cost_estimate=sizes.cost(members, 1),
        name="score_group",
    )(order, counts, rows, *pieces)


def sum_group(sizes, members, order, counts, rows, tiles, shares):
    count = 2 * len(members)
    return pl.pallas_call(
        functools.partial(sum_kernel, local_slots(members)),
        out_shape=(sizes.sums,) * count,
        in_specs=[SMEM, SMEM, VMEM, HBM, VMEM],
        out_specs=(ANY,) * count,
        scratch_shapes=sizes.sum_scratch(count)
        + [
            sizes.tile_scratch(count),
            pltpu.SemaphoreType.DMA((count * sizes.blocks,)),
            pltpu.SemaphoreType.DMA((count,)),
        ],
        compiler_params=pltpu.CompilerParams(vmem_limit_bytes=VMEM_GRANT),
        cost_estimate=sizes.cost(members, 1),
        name="sum_group",
    )(order, counts, rows, tiles, shares)


def middle_group(sizes, members, order, counts, rows, tops, masses, pieces):
    count = len(pieces)
    earlier = len(tops)
    return pl.pallas_call(
        functools.partial(middle_kernel, local_slots(members), sizes.listed, earlier),
        out_shape=(jax.ShapeDtypeStruct((sizes.blocks, BLOCK), jnp.float32), sizes.stats)
        + (sizes.sums,) * count,
        in_specs=[SMEM, SMEM, VMEM] + [VMEM] * (2 * earlier) + [ANY] * count,
        out_specs=(VMEM, VMEM) + (ANY,) * count,
        scratch_shapes=sizes.panel_scratch(count)
        + [
            sizes.tile_scratch(count),
            pltpu.VMEM(sizes.stats.shape, jnp.float32),
            pltpu.VMEM(sizes.stats.shape, jnp.float32),
        ]
        + sizes.sum_scratch(count)
        + [pltpu.SemaphoreType.DMA((count,)), pltpu.SemaphoreType.DMA((count,))],
        compiler_params=pltpu.CompilerParams(vmem_limit_bytes=VMEM_GRANT),
        cost_estimate=sizes.cost(members, 2),
        name="middle_group",
    )(order, counts, rows, *tops, *masses, *pieces)


def on_device(rows, centroids, lists):
    count = lax.axis_size("blk")
    device = lax.axis_index("blk")
    cent = centroids.shape[0]
    own, stages = plan_of(count)
    groups = [(own,)] + [tuple(q for q, _, _ in stage) for stage in stages]
    slots = (2 * chip_place(lists, device, count) + ((lists ^ device) & 1)).astype(jnp.int32)
    sizes = Sizes(rows, *slots.shape, cent)
    order, counts = pairs_of(slots, 2 * max(q for members in groups for q in members) + 2)

    near = {own: centroids}
    tiles, tops, masses = [], [], []
    for members, stage in zip(groups, stages):
        arriving = [moved(near[source], shift) for _, source, shift in stage]
        pieces = [v for q in members for v in (near[q], other_core(near[q]))]
        scored = score_group(sizes, members, order, counts, rows, pieces)
        arriving, scored, near = lax.optimization_barrier((arriving, scored, near))
        tiles.append(scored[0])
        tops.append(scored[1])
        masses.append(scored[2])
        for (q, _, _), value in zip(stage, arriving):
            near[q] = value
    members = groups[-1]
    pieces = [v for q in members for v in (near[q], other_core(near[q]))]
    log_totals, shares, *sums = middle_group(sizes, members, order, counts, rows, tops, masses, pieces)

    back = {q: [] for members in groups for q in members}
    sums = {q: pair for q, pair in zip(groups[-1], zip(sums[::2], sums[1::2]))}
    arriving = []
    for at in reversed(range(len(groups))):
        crossed = {q: other_core(theirs) for q, (_, theirs) in sums.items()}
        ahead = []
        if at:
            ahead = sum_group(sizes, groups[at - 1], order, counts, rows, tiles[at - 1], shares)
        crossed, ahead, arriving, shares = lax.optimization_barrier((crossed, ahead, arriving, shares))
        if arriving:
            for value, (_, source, _) in zip(arriving, stages[at]):
                back[source].append(value)
        total = {}
        for q, (mine, _) in sums.items():
            total[q] = (mine + crossed[q]) * LINK_SCALE
            for value in back[q]:
                total[q] = total[q] + value.astype(jnp.float32)
        if at:
            arriving = [
                moved(total[q].astype(jnp.float16), shift if shift is None else -shift)
                for q, _, shift in stages[at - 1]
            ]
            sums = {q: pair for q, pair in zip(groups[at - 1], zip(ahead[::2], ahead[1::2]))}
    own_sums = total[own] * (1.0 / LINK_SCALE)
    updated = (own_sums[:cent] + PRIOR_MASS * centroids.astype(jnp.float32)) / (
        own_sums[cent, :cent][:, None] + PRIOR_MASS
    )
    return updated, log_totals.reshape(-1)


def solution(mesh):
    placed = P(("groups", "blk"), None)
    return jax.shard_map(
        on_device,
        mesh=mesh,
        in_specs=(placed, placed, placed),
        out_specs=(placed, P(("groups", "blk"))),
        check_vma=False,
    )
```

```python
import functools
import math

import jax
import jax.numpy as jnp
from jax import lax
from jax.experimental import pallas as pl
from jax.experimental.pallas import tpu as pltpu
from jax.sharding import PartitionSpec as P

BLOCK = 256
SPAN = 6
LOGIT_SCALE = 0.25
PRIOR_MASS = 8.0
LOG2E = math.log2(math.e)
LINK_SCALE = 1.0 / 16.0
EXTRA = 8
VMEM_GRANT = 42 << 20


def grid_plan():
    return 0, (
        ((2, 0, 4), (1, 0, None)),
        ((6, 0, -4), (3, 2, None)),
        ((5, 3, 4), (7, 6, None)),
    )


def ring_plan():
    reach = (SPAN + 1) // 2
    return reach, tuple(
        ((reach + hop + 1, reach + hop, 2), (reach - hop - 1, reach - hop, -2)) for hop in range(reach)
    )


def plan_of(count):
    return grid_plan() if count == 16 else ring_plan()


def chip_place(panel, device, count):
    if count == 16:
        return (device // 4 - panel // 4) % 4 * 2 + ((panel ^ device) >> 1 & 1)
    return (device // 2 - panel // 2 + (SPAN + 1) // 2) % (count // 2)


def moved(value, shift):
    count = lax.axis_size("blk")
    if shift is None:
        return lax.ppermute(value, "blk", [(i, i ^ 2) for i in range(count)])
    return lax.ppermute(value, "blk", [(i, (i + shift) % count) for i in range(count)])


def other_core(value):
    count = lax.axis_size("blk")
    return lax.ppermute(value, "blk", [(i, i ^ 1) for i in range(count)])


def pairs_of(slots, room):
    blocks, listed = slots.shape
    hit = slots[:, :, None] == jnp.arange(room, dtype=jnp.int32)
    listing = jnp.any(hit, axis=1)
    code = 8 * jnp.arange(blocks, dtype=jnp.int32)[:, None] + jnp.sum(
        jnp.where(hit, jnp.arange(listed, dtype=jnp.int32)[None, :, None], 0), axis=1
    )
    before = jnp.arange(blocks)[:, None] > jnp.arange(blocks)[None, :]
    rank = jnp.sum(jnp.where(before[:, :, None] & listing[None], 1, 0), axis=1)
    chosen = listing[:, :, None] & (rank[:, :, None] == jnp.arange(blocks))
    order = jnp.sum(jnp.where(chosen, code[:, :, None], 0), axis=0)
    return order.reshape(-1).astype(jnp.int32), jnp.sum(listing, axis=0).astype(jnp.int32)


def local_slots(members):
    return [2 * q + core for q in members for core in (0, 1)]


def some_pairs(order_ref, counts_ref, slot, blocks, first, number):
    work = []
    for i in range(number):
        code = order_ref[slot * blocks + jnp.minimum(first + i, counts_ref[slot] - 1)]
        work.append((first + i, code >> 3, (code & 7) * blocks + (code >> 3)))
    return work


def by_fours(count, act):
    fours = count // 4
    lax.fori_loop(0, fours, lambda k, _: (act(4 * k, 4), 0)[1], 0)
    lax.fori_loop(2 * fours, (count + 1) // 2, lambda k, _: (act(2 * k, 2), 0)[1], 0)


def rows_of(x, block):
    return x[pl.ds(pl.multiple_of(block * BLOCK, BLOCK), BLOCK)]


def load_panels(piece_refs, panels, norms, sem):
    copies = [
        pltpu.make_async_copy(ref, panels.at[p], sem.at[p]) for p, ref in enumerate(piece_refs)
    ]
    for copy in copies:
        copy.start()

    def finish():
        for copy in copies:
            copy.wait()
        for p in range(len(copies)):
            wide = panels[p].astype(jnp.float32)
            norm = jnp.sum(wide * wide, axis=1, keepdims=True)
            norms[p] = jnp.broadcast_to(norm * (0.5 * LOGIT_SCALE * LOG2E), norms.shape[1:])

    return finish


def tile_of(panel, norm, block):
    scores = lax.dot_general(
        panel, block, (((1,), (1,)), ((), ())), preferred_element_type=jnp.float32
    )
    scores = scores * (LOGIT_SCALE * LOG2E) - jnp.concatenate([norm, norm], axis=1)
    top = jnp.max(scores, axis=0, keepdims=True)
    powers = jnp.exp2(scores - top)
    return powers, top, jnp.sum(powers, axis=0, keepdims=True)


def score_loop(
    slots, order_ref, counts_ref, x, panels, norms, tops, masses, tiles, here, done
):
    blocks = x.shape[0] // BLOCK
    tops[...] = jnp.full_like(tops, -jnp.inf)
    masses[...] = jnp.zeros_like(masses)
    for p, slot in enumerate(slots):

        def some(first, number):
            work = some_pairs(order_ref, counts_ref, slot, blocks, first, number)
            here(work[-1][1])
            found = [tile_of(panels[p], norms[p], rows_of(x, b)) for _, b, _ in work]
            for (i, _, at), (powers, top, mass) in zip(work, found):
                tiles[p * blocks + i] = powers
                tops[pl.ds(at, 1)] = top
                masses[pl.ds(at, 1)] = mass
            for i, _, _ in work:
                done(p * blocks + i)

        by_fours(counts_ref[slot], some)


def sum_loop(slots, order_ref, counts_ref, x, shares, acc, totals, tiles, ready):
    blocks = x.shape[0] // BLOCK
    cent = totals.shape[1]
    for p, slot in enumerate(slots):

        def some(first, number):
            work = some_pairs(order_ref, counts_ref, slot, blocks, first, number)
            for i, _, _ in work:
                ready(p * blocks + i)
            partial, count = None, None
            for i, b, at in work:
                share = shares[pl.ds(at, 1)]
                if number == 2:
                    share = share * (i < counts_ref[slot]).astype(jnp.float32)
                weights = (tiles[p * blocks + i] * share).astype(jnp.bfloat16)
                wide = weights.astype(jnp.float32)
                wide = wide[:, :128] + wide[:, 128:]
                product = jnp.dot(weights, rows_of(x, b), preferred_element_type=jnp.float32)
                partial = product if partial is None else partial + product
                count = wide if count is None else count + wide
            totals[p] += count
            acc[p, pl.ds(0, cent)] += partial

        by_fours(counts_ref[slot], some)


def clear_sums(acc, totals):
    acc[...] = jnp.zeros_like(acc)
    totals[...] = jnp.zeros_like(totals)


def store_sums(acc, totals, out_refs, sem):
    cent = totals.shape[1]
    copies = []
    for p, ref in enumerate(out_refs):
        row = jnp.sum(totals[p].T, axis=0, keepdims=True)
        acc[p, pl.ds(cent, EXTRA), pl.ds(0, cent)] = jnp.broadcast_to(row, (EXTRA, cent))
        copies.append(pltpu.make_async_copy(acc.at[p], ref, sem.at[p]))
        copies[-1].start()
    for copy in copies:
        copy.wait()


def over_tiles(slots, counts_ref, blocks, act):
    for p, slot in enumerate(slots):
        held = (counts_ref[slot] + 1) // 2 * 2
        lax.fori_loop(0, held, lambda i, _: (act(p * blocks + i), 0)[1], 0)


def score_kernel(slots, fetch, order_ref, counts_ref, rows_ref, *refs):
    pieces = len(slots)
    piece_refs = refs[:pieces]
    tiles_ref, tops, masses = refs[pieces : pieces + 3]
    refs = refs[pieces + 3 :]
    x = refs[0] if fetch else rows_ref
    panels, norms, tiles, panel_sem, tile_sem = refs[1:6] if fetch else refs[:5]
    blocks = x.shape[0] // BLOCK
    finish_panels = load_panels(piece_refs, panels, norms, panel_sem)
    here = lambda b: None
    if fetch:
        row_sem, fetched = refs[6:]

        def bring(b):
            span = pl.ds(pl.multiple_of(b * BLOCK, BLOCK), BLOCK)
            return pltpu.make_async_copy(rows_ref.at[span], x.at[span], row_sem.at[b])

        for b in range(blocks):
            bring(b).start()
        fetched[0] = 0

        def here(b):
            first = fetched[0]
            lax.fori_loop(first, b + 1, lambda k, _: (bring(k).wait(), 0)[1], 0)
            fetched[0] = jnp.maximum(first, b + 1)

    finish_panels()

    def outgoing(j):
        return pltpu.make_async_copy(tiles.at[j], tiles_ref.at[j], tile_sem.at[j])

    score_loop(
        slots, order_ref, counts_ref, x, panels, norms, tops, masses, tiles, here,
        lambda j: outgoing(j).start(),
    )
    here(blocks - 1)
    over_tiles(slots, counts_ref, blocks, lambda j: outgoing(j).wait())


def sum_kernel(slots, order_ref, counts_ref, x, tiles_ref, shares, *refs):
    pieces = len(slots)
    out_refs = refs[:pieces]
    acc, totals, tiles, tile_sem, out_sem = refs[pieces:]

    def incoming(j):
        return pltpu.make_async_copy(tiles_ref.at[j], tiles.at[j], tile_sem.at[j])

    over_tiles(slots, counts_ref, x.shape[0] // BLOCK, lambda j: incoming(j).start())
    clear_sums(acc, totals)
    sum_loop(
        slots, order_ref, counts_ref, x, shares, acc, totals, tiles, lambda j: incoming(j).wait()
    )
    store_sums(acc, totals, out_refs, out_sem)


def middle_kernel(slots, listed, earlier, order_ref, counts_ref, x, *refs):
    pieces = len(slots)
    stat_refs = refs[: 2 * earlier]
    piece_refs = refs[2 * earlier : 2 * earlier + pieces]
    refs = refs[2 * earlier + pieces :]
    logs_ref, shares = refs[:2]
    out_refs = refs[2 : 2 + pieces]
    panels, norms, tiles, tops, masses, acc, totals, panel_sem, out_sem = refs[2 + pieces :]
    blocks = x.shape[0] // BLOCK
    finish_panels = load_panels(piece_refs, panels, norms, panel_sem)
    clear_sums(acc, totals)
    finish_panels()
    score_loop(
        slots, order_ref, counts_ref, x, panels, norms, tops, masses, tiles,
        lambda b: None, lambda j: None,
    )
    width = tops.shape[1]
    top = functools.reduce(jnp.maximum, [ref[...] for ref in stat_refs[:earlier]], tops[...])
    mass = functools.reduce(jnp.add, [ref[...] for ref in stat_refs[earlier:]], masses[...])
    top = top.reshape(listed, blocks, width)
    mass = mass.reshape(listed, blocks, width)
    highest = jnp.max(top, axis=0)
    factor = jnp.exp2(top - highest[None])
    whole = jnp.sum(factor * mass, axis=0)
    logs_ref[...] = (highest + jnp.log2(whole)) * (1.0 / LOG2E)
    shares[...] = (factor / whole[None]).reshape(listed * blocks, width)
    sum_loop(slots, order_ref, counts_ref, x, shares, acc, totals, tiles, lambda j: None)
    store_sums(acc, totals, out_refs, out_sem)


SMEM = pl.BlockSpec(memory_space=pltpu.SMEM)
ANY = pl.BlockSpec(memory_space=pl.ANY)
HBM = pl.BlockSpec(memory_space=pltpu.HBM)
VMEM = pl.BlockSpec(memory_space=pltpu.VMEM)


class Sizes:
    def __init__(self, rows, blocks, listed, cent):
        self.blocks, self.listed, self.cent = blocks, listed, cent
        self.width = rows.shape[1]
        self.stats = jax.ShapeDtypeStruct((listed * blocks, BLOCK), jnp.float32)
        self.sums = jax.ShapeDtypeStruct((cent + EXTRA, self.width), jnp.float32)
        self.tiles = jax.ShapeDtypeStruct((4 * blocks, cent, BLOCK), jnp.float32)

    def cost(self, slots, products):
        pairs = self.blocks * self.listed * len(slots) / 14
        return pl.CostEstimate(
            flops=int(2 * products * pairs * self.cent * BLOCK * self.width),
            bytes_accessed=int(2 * self.blocks * BLOCK * self.width + 4 * pairs * self.cent * BLOCK),
            transcendentals=int(pairs * self.cent * BLOCK),
        )

    def panel_scratch(self, pieces):
        return [
            pltpu.VMEM((pieces, self.cent, self.width), jnp.bfloat16),
            pltpu.VMEM((pieces, self.cent, 128), jnp.float32),
        ]

    def sum_scratch(self, pieces):
        return [
            pltpu.VMEM((pieces, self.cent + EXTRA, self.width), jnp.float32),
            pltpu.VMEM((pieces, self.cent, 128), jnp.float32),
        ]

    def tile_scratch(self, pieces):
        return pltpu.VMEM((pieces * self.blocks, self.cent, BLOCK), jnp.float32)


def score_group(sizes, slots, order, counts, rows, pieces, fetch):
    count = len(pieces)
    outs = (sizes.tiles, sizes.stats, sizes.stats)
    rows_outs, rows_scratch = (), []
    if fetch:
        rows_outs = (jax.ShapeDtypeStruct(rows.shape, rows.dtype),)
        rows_scratch = [pltpu.SemaphoreType.DMA((sizes.blocks,)), pltpu.SMEM((1,), jnp.int32)]
    return pl.pallas_call(
        functools.partial(score_kernel, slots, fetch),
        out_shape=outs + rows_outs,
        in_specs=[SMEM, SMEM, HBM if fetch else VMEM] + [ANY] * count,
        out_specs=(HBM, VMEM, VMEM) + (VMEM,) * len(rows_outs),
        scratch_shapes=sizes.panel_scratch(count)
        + [
            sizes.tile_scratch(count),
            pltpu.SemaphoreType.DMA((count,)),
            pltpu.SemaphoreType.DMA((count * sizes.blocks,)),
        ]
        + rows_scratch,
        compiler_params=pltpu.CompilerParams(vmem_limit_bytes=VMEM_GRANT),
        cost_estimate=sizes.cost(slots, 1),
        name="score_group",
    )(order, counts, rows, *pieces)


def sum_group(sizes, slots, order, counts, rows, tiles, shares):
    count = len(slots)
    return pl.pallas_call(
        functools.partial(sum_kernel, slots),
        out_shape=(sizes.sums,) * count,
        in_specs=[SMEM, SMEM, VMEM, HBM, VMEM],
        out_specs=(ANY,) * count,
        scratch_shapes=sizes.sum_scratch(count)
        + [
            sizes.tile_scratch(count),
            pltpu.SemaphoreType.DMA((count * sizes.blocks,)),
            pltpu.SemaphoreType.DMA((count,)),
        ],
        compiler_params=pltpu.CompilerParams(vmem_limit_bytes=VMEM_GRANT),
        cost_estimate=sizes.cost(slots, 1),
        name="sum_group",
    )(order, counts, rows, tiles, shares)


def middle_group(sizes, slots, order, counts, rows, tops, masses, pieces):
    count = len(pieces)
    earlier = len(tops)
    return pl.pallas_call(
        functools.partial(middle_kernel, slots, sizes.listed, earlier),
        out_shape=(jax.ShapeDtypeStruct((sizes.blocks, BLOCK), jnp.float32), sizes.stats)
        + (sizes.sums,) * count,
        in_specs=[SMEM, SMEM, VMEM] + [VMEM] * (2 * earlier) + [ANY] * count,
        out_specs=(VMEM, VMEM) + (ANY,) * count,
        scratch_shapes=sizes.panel_scratch(count)
        + [
            sizes.tile_scratch(count),
            pltpu.VMEM(sizes.stats.shape, jnp.float32),
            pltpu.VMEM(sizes.stats.shape, jnp.float32),
        ]
        + sizes.sum_scratch(count)
        + [pltpu.SemaphoreType.DMA((count,)), pltpu.SemaphoreType.DMA((count,))],
        compiler_params=pltpu.CompilerParams(vmem_limit_bytes=VMEM_GRANT),
        cost_estimate=sizes.cost(slots, 2),
        name="middle_group",
    )(order, counts, rows, *tops, *masses, *pieces)


def add_kernel(mine_ref, back_ref, out_ref):
    out_ref[...] = mine_ref[...] * LINK_SCALE + back_ref[...]


def scaled_sum(mine, back):
    return pl.pallas_call(
        add_kernel,
        out_shape=jax.ShapeDtypeStruct(mine.shape, mine.dtype),
        in_specs=[VMEM, VMEM],
        out_specs=VMEM,
        compiler_params=pltpu.CompilerParams(vmem_limit_bytes=VMEM_GRANT),
        cost_estimate=pl.CostEstimate(flops=30 * 10**9, bytes_accessed=12 * mine.size, transcendentals=0),
        name="scaled_sum",
    )(mine, back)


def on_device(rows, centroids, lists):
    count = lax.axis_size("blk")
    device = lax.axis_index("blk")
    cent = centroids.shape[0]
    own, stages = plan_of(count)
    groups = [(own,)] + [tuple(q for q, _, _ in stage) for stage in stages]
    slots = (2 * chip_place(lists, device, count) + ((lists ^ device) & 1)).astype(jnp.int32)
    sizes = Sizes(rows, *slots.shape, cent)
    order, counts = pairs_of(slots, 2 * max(q for members in groups for q in members) + 2)

    near = {own: centroids}
    tiles, tops, masses = [], [], []
    for members, stage in zip(groups, stages):
        arriving = [moved(near[source], shift) for _, source, shift in stage]
        pieces = [v for q in members for v in (near[q], other_core(near[q]))]
        scored = score_group(
            sizes, local_slots(members), order, counts, rows, pieces, fetch=not tiles
        )
        arriving, scored, near = lax.optimization_barrier((arriving, scored, near))
        if not tiles:
            rows = scored[3]
        tiles.append(scored[0])
        tops.append(scored[1])
        masses.append(scored[2])
        for (q, _, _), value in zip(stage, arriving):
            near[q] = value
    last = groups[-1]
    near_slots, far_slots = [2 * q for q in last], [2 * q + 1 for q in last]
    far = [other_core(near[q]) for q in last]
    near_tiles, top, mass = score_group(
        sizes, near_slots, order, counts, rows, [near[q] for q in last], fetch=False
    )
    tops.append(top)
    masses.append(mass)
    log_totals, shares, *far_sums = middle_group(
        sizes, far_slots, order, counts, rows, tops, masses, far
    )
    near_sums = sum_group(sizes, near_slots, order, counts, rows, near_tiles, shares)
    mine = dict(zip(last, near_sums))
    crossed = {q: other_core(v) for q, v in zip(last, far_sums)}
    total = {q: (mine[q] + crossed[q]) * LINK_SCALE for q in last}

    back = {q: [] for members in groups for q in members}
    for members, stage in zip(reversed(groups[:-1]), reversed(stages)):
        leaving = [total[q].astype(jnp.float16) for q, _, _ in stage]
        leaving, shares = lax.optimization_barrier((leaving, shares))
        arriving = [
            moved(value, shift if shift is None else -shift)
            for value, (_, _, shift) in zip(leaving, stage)
        ]
        at = groups.index(members)
        sums = sum_group(sizes, local_slots(members), order, counts, rows, tiles[at], shares)
        crossed = {q: other_core(v) for q, v in zip(members, sums[1::2])}
        arriving = lax.optimization_barrier(arriving)
        for value, (_, source, _) in zip(arriving, stage):
            back[source].append(value.astype(jnp.float32))
        for q, near_sum in zip(members, sums[::2]):
            if back[q]:
                part = scaled_sum(near_sum, functools.reduce(jnp.add, back[q]))
            else:
                part = near_sum * LINK_SCALE
            total[q] = part + crossed[q] * LINK_SCALE
    own_sums = total[own] * (1.0 / LINK_SCALE)
    updated = (own_sums[:cent] + PRIOR_MASS * centroids.astype(jnp.float32)) / (
        own_sums[cent, :cent][:, None] + PRIOR_MASS
    )
    return updated, log_totals.reshape(-1)


def solution(mesh):
    placed = P(("groups", "blk"), None)
    return jax.shard_map(
        on_device,
        mesh=mesh,
        in_specs=(placed, placed, placed),
        out_specs=(placed, P(("groups", "blk"))),
        check_vma=False,
    )
```

```python
import functools
import math

import jax
import jax.numpy as jnp
from jax import lax
from jax.experimental import pallas as pl
from jax.experimental.pallas import tpu as pltpu
from jax.sharding import PartitionSpec as P

BLOCK = 256
SPAN = 6
LOGIT_SCALE = 0.25
PRIOR_MASS = 8.0
LOG2E = math.log2(math.e)
LINK_SCALE = 1.0 / 16.0
EXTRA = 8
VMEM_GRANT = 42 << 20


def grid_plan():
    return 0, (
        ((2, 0, 4), (1, 0, None)),
        ((6, 0, -4), (3, 2, None)),
        ((5, 3, 4), (7, 6, None)),
    )


def ring_plan():
    reach = (SPAN + 1) // 2
    return reach, tuple(
        ((reach + hop + 1, reach + hop, 2), (reach - hop - 1, reach - hop, -2)) for hop in range(reach)
    )


def plan_of(count):
    return grid_plan() if count == 16 else ring_plan()


def chip_place(panel, device, count):
    if count == 16:
        return (device // 4 - panel // 4) % 4 * 2 + ((panel ^ device) >> 1 & 1)
    return (device // 2 - panel // 2 + (SPAN + 1) // 2) % (count // 2)


def moved(value, shift):
    count = lax.axis_size("blk")
    if shift is None:
        return lax.ppermute(value, "blk", [(i, i ^ 2) for i in range(count)])
    return lax.ppermute(value, "blk", [(i, (i + shift) % count) for i in range(count)])


def other_core(value):
    count = lax.axis_size("blk")
    return lax.ppermute(value, "blk", [(i, i ^ 1) for i in range(count)])


def pairs_of(slots, room):
    blocks, listed = slots.shape
    hit = slots[:, :, None] == jnp.arange(room, dtype=jnp.int32)
    listing = jnp.any(hit, axis=1)
    code = 8 * jnp.arange(blocks, dtype=jnp.int32)[:, None] + jnp.sum(
        jnp.where(hit, jnp.arange(listed, dtype=jnp.int32)[None, :, None], 0), axis=1
    )
    before = jnp.arange(blocks)[:, None] > jnp.arange(blocks)[None, :]
    rank = jnp.sum(jnp.where(before[:, :, None] & listing[None], 1, 0), axis=1)
    chosen = listing[:, :, None] & (rank[:, :, None] == jnp.arange(blocks))
    order = jnp.sum(jnp.where(chosen, code[:, :, None], 0), axis=0)
    return order.reshape(-1).astype(jnp.int32), jnp.sum(listing, axis=0).astype(jnp.int32)


def local_slots(members):
    return [2 * q + core for q in members for core in (0, 1)]


def some_pairs(order_ref, counts_ref, slot, blocks, first, number):
    work = []
    for i in range(number):
        code = order_ref[slot * blocks + jnp.minimum(first + i, counts_ref[slot] - 1)]
        work.append((first + i, code >> 3, (code & 7) * blocks + (code >> 3)))
    return work


def by_fours(count, act):
    fours = count // 4
    lax.fori_loop(0, fours, lambda k, _: (act(4 * k, 4), 0)[1], 0)
    lax.fori_loop(2 * fours, (count + 1) // 2, lambda k, _: (act(2 * k, 2), 0)[1], 0)


def rows_of(x, block):
    return x[pl.ds(pl.multiple_of(block * BLOCK, BLOCK), BLOCK)]


def find_norms(panels, norms):
    for p, panel in enumerate(panels):
        wide = panel[...].astype(jnp.float32)
        norm = jnp.sum(wide * wide, axis=1, keepdims=True)
        norms[p] = jnp.broadcast_to(norm * (0.5 * LOGIT_SCALE * LOG2E), norms.shape[1:])


def tile_of(panel, norm, block):
    scores = lax.dot_general(
        panel, block, (((1,), (1,)), ((), ())), preferred_element_type=jnp.float32
    )
    scores = scores * (LOGIT_SCALE * LOG2E) - jnp.concatenate([norm, norm], axis=1)
    top = jnp.max(scores, axis=0, keepdims=True)
    powers = jnp.exp2(scores - top)
    return powers, top, jnp.sum(powers, axis=0, keepdims=True)


def score_loop(
    slots, order_ref, counts_ref, x, panels, norms, tops, masses, tiles, here, done
):
    blocks = x.shape[0] // BLOCK
    tops[...] = jnp.full_like(tops, -jnp.inf)
    masses[...] = jnp.zeros_like(masses)
    for p, slot in enumerate(slots):

        def some(first, number):
            work = some_pairs(order_ref, counts_ref, slot, blocks, first, number)
            here(work[-1][1])
            found = [tile_of(panels[p][...], norms[p], rows_of(x, b)) for _, b, _ in work]
            for (i, _, at), (powers, top, mass) in zip(work, found):
                tiles[p * blocks + i] = powers
                tops[pl.ds(at, 1)] = top
                masses[pl.ds(at, 1)] = mass
            for i, _, _ in work:
                done(p * blocks + i)

        by_fours(counts_ref[slot], some)


def sum_loop(slots, order_ref, counts_ref, x, shares, acc, totals, tiles, ready):
    blocks = x.shape[0] // BLOCK
    cent = totals.shape[1]
    for p, slot in enumerate(slots):

        def some(first, number):
            work = some_pairs(order_ref, counts_ref, slot, blocks, first, number)
            for i, _, _ in work:
                ready(p * blocks + i)
            partial, count = None, None
            for i, b, at in work:
                share = shares[pl.ds(at, 1)]
                if number == 2:
                    share = share * (i < counts_ref[slot]).astype(jnp.float32)
                weights = (tiles[p * blocks + i] * share).astype(jnp.bfloat16)
                wide = weights.astype(jnp.float32)
                wide = wide[:, :128] + wide[:, 128:]
                product = jnp.dot(weights, rows_of(x, b), preferred_element_type=jnp.float32)
                partial = product if partial is None else partial + product
                count = wide if count is None else count + wide
            totals[p] += count
            acc[p][pl.ds(0, cent)] += partial

        by_fours(counts_ref[slot], some)


def clear_sums(acc, totals):
    for ref in acc:
        ref[...] = jnp.zeros_like(ref)
    totals[...] = jnp.zeros_like(totals)


def store_totals(acc, totals):
    cent = totals.shape[1]
    for p, ref in enumerate(acc):
        row = jnp.sum(totals[p].T, axis=0, keepdims=True)
        ref[pl.ds(cent, EXTRA), pl.ds(0, cent)] = jnp.broadcast_to(row, (EXTRA, cent))


def over_tiles(slots, counts_ref, blocks, act):
    for p, slot in enumerate(slots):
        held = (counts_ref[slot] + 1) // 2 * 2
        lax.fori_loop(0, held, lambda i, _: (act(p * blocks + i), 0)[1], 0)


def score_kernel(slots, fetch, order_ref, counts_ref, rows_ref, *refs):
    pieces = len(slots)
    piece_refs = refs[:pieces]
    tiles_ref, tops, masses = refs[pieces : pieces + 3]
    refs = refs[pieces + 3 :]
    x = refs[0] if fetch else rows_ref
    norms, tiles, tile_sem = refs[1:4] if fetch else refs[:3]
    blocks = x.shape[0] // BLOCK
    here = lambda b: None
    if fetch:
        row_sem, fetched = refs[4:]

        def bring(b):
            span = pl.ds(pl.multiple_of(b * BLOCK, BLOCK), BLOCK)
            return pltpu.make_async_copy(rows_ref.at[span], x.at[span], row_sem.at[b])

        for b in range(blocks):
            bring(b).start()
        fetched[0] = 0

        def here(b):
            first = fetched[0]
            lax.fori_loop(first, b + 1, lambda k, _: (bring(k).wait(), 0)[1], 0)
            fetched[0] = jnp.maximum(first, b + 1)

    find_norms(piece_refs, norms)

    def outgoing(j):
        return pltpu.make_async_copy(tiles.at[j], tiles_ref.at[j], tile_sem.at[j])

    score_loop(
        slots, order_ref, counts_ref, x, piece_refs, norms, tops, masses, tiles, here,
        lambda j: outgoing(j).start(),
    )
    here(blocks - 1)
    over_tiles(slots, counts_ref, blocks, lambda j: outgoing(j).wait())


def sum_kernel(slots, order_ref, counts_ref, x, tiles_ref, shares, *refs):
    pieces = len(slots)
    out_refs = refs[:pieces]
    totals, tiles, tile_sem = refs[pieces:]

    def incoming(j):
        return pltpu.make_async_copy(tiles_ref.at[j], tiles.at[j], tile_sem.at[j])

    over_tiles(slots, counts_ref, x.shape[0] // BLOCK, lambda j: incoming(j).start())
    clear_sums(out_refs, totals)
    sum_loop(
        slots, order_ref, counts_ref, x, shares, out_refs, totals, tiles,
        lambda j: incoming(j).wait(),
    )
    store_totals(out_refs, totals)


def middle_kernel(slots, listed, earlier, order_ref, counts_ref, x, *refs):
    pieces = len(slots)
    stat_refs = refs[: 2 * earlier]
    piece_refs = refs[2 * earlier : 2 * earlier + pieces]
    refs = refs[2 * earlier + pieces :]
    logs_ref, shares = refs[:2]
    out_refs = refs[2 : 2 + pieces]
    norms, tiles, tops, masses, totals = refs[2 + pieces :]
    blocks = x.shape[0] // BLOCK
    clear_sums(out_refs, totals)
    find_norms(piece_refs, norms)
    score_loop(
        slots, order_ref, counts_ref, x, piece_refs, norms, tops, masses, tiles,
        lambda b: None, lambda j: None,
    )
    width = tops.shape[1]
    top = functools.reduce(jnp.maximum, [ref[...] for ref in stat_refs[:earlier]], tops[...])
    mass = functools.reduce(jnp.add, [ref[...] for ref in stat_refs[earlier:]], masses[...])
    top = top.reshape(listed, blocks, width)
    mass = mass.reshape(listed, blocks, width)
    highest = jnp.max(top, axis=0)
    factor = jnp.exp2(top - highest[None])
    whole = jnp.sum(factor * mass, axis=0)
    logs_ref[...] = (highest + jnp.log2(whole)) * (1.0 / LOG2E)
    shares[...] = (factor / whole[None]).reshape(listed * blocks, width)
    sum_loop(slots, order_ref, counts_ref, x, shares, out_refs, totals, tiles, lambda j: None)
    store_totals(out_refs, totals)


SMEM = pl.BlockSpec(memory_space=pltpu.SMEM)
HBM = pl.BlockSpec(memory_space=pltpu.HBM)
VMEM = pl.BlockSpec(memory_space=pltpu.VMEM)


class Sizes:
    def __init__(self, rows, blocks, listed, cent):
        self.blocks, self.listed, self.cent = blocks, listed, cent
        self.width = rows.shape[1]
        self.stats = jax.ShapeDtypeStruct((listed * blocks, BLOCK), jnp.float32)
        self.sums = jax.ShapeDtypeStruct((cent + EXTRA, self.width), jnp.float32)
        self.tiles = jax.ShapeDtypeStruct((4 * blocks, cent, BLOCK), jnp.float32)

    def cost(self, slots, products):
        pairs = self.blocks * self.listed * len(slots) / 14
        return pl.CostEstimate(
            flops=int(2 * products * pairs * self.cent * BLOCK * self.width),
            bytes_accessed=int(2 * self.blocks * BLOCK * self.width + 4 * pairs * self.cent * BLOCK),
            transcendentals=int(pairs * self.cent * BLOCK),
        )

    def columns(self, pieces):
        return pltpu.VMEM((pieces, self.cent, 128), jnp.float32)

    def tile_scratch(self, pieces):
        return pltpu.VMEM((pieces * self.blocks, self.cent, BLOCK), jnp.float32)


def score_group(sizes, slots, order, counts, rows, pieces, fetch):
    count = len(pieces)
    outs = (sizes.tiles, sizes.stats, sizes.stats)
    rows_outs, rows_scratch = (), []
    if fetch:
        rows_outs = (jax.ShapeDtypeStruct(rows.shape, rows.dtype),)
        rows_scratch = [pltpu.SemaphoreType.DMA((sizes.blocks,)), pltpu.SMEM((1,), jnp.int32)]
    return pl.pallas_call(
        functools.partial(score_kernel, slots, fetch),
        out_shape=outs + rows_outs,
        in_specs=[SMEM, SMEM, HBM if fetch else VMEM] + [VMEM] * count,
        out_specs=(HBM, VMEM, VMEM) + (VMEM,) * len(rows_outs),
        scratch_shapes=[
            sizes.columns(count),
            sizes.tile_scratch(count),
            pltpu.SemaphoreType.DMA((count * sizes.blocks,)),
        ]
        + rows_scratch,
        compiler_params=pltpu.CompilerParams(vmem_limit_bytes=VMEM_GRANT),
        cost_estimate=sizes.cost(slots, 1),
        name="score_group",
    )(order, counts, rows, *pieces)


def sum_group(sizes, slots, order, counts, rows, tiles, shares):
    count = len(slots)
    return pl.pallas_call(
        functools.partial(sum_kernel, slots),
        out_shape=(sizes.sums,) * count,
        in_specs=[SMEM, SMEM, VMEM, HBM, VMEM],
        out_specs=(VMEM,) * count,
        scratch_shapes=[
            sizes.columns(count),
            sizes.tile_scratch(count),
            pltpu.SemaphoreType.DMA((count * sizes.blocks,)),
        ],
        compiler_params=pltpu.CompilerParams(vmem_limit_bytes=VMEM_GRANT),
        cost_estimate=sizes.cost(slots, 1),
        name="sum_group",
    )(order, counts, rows, tiles, shares)


def middle_group(sizes, slots, order, counts, rows, tops, masses, pieces):
    count = len(pieces)
    earlier = len(tops)
    return pl.pallas_call(
        functools.partial(middle_kernel, slots, sizes.listed, earlier),
        out_shape=(jax.ShapeDtypeStruct((sizes.blocks, BLOCK), jnp.float32), sizes.stats)
        + (sizes.sums,) * count,
        in_specs=[SMEM, SMEM, VMEM] + [VMEM] * (2 * earlier + count),
        out_specs=(VMEM, VMEM) + (VMEM,) * count,
        scratch_shapes=[
            sizes.columns(count),
            sizes.tile_scratch(count),
            pltpu.VMEM(sizes.stats.shape, jnp.float32),
            pltpu.VMEM(sizes.stats.shape, jnp.float32),
            sizes.columns(count),
        ],
        compiler_params=pltpu.CompilerParams(vmem_limit_bytes=VMEM_GRANT),
        cost_estimate=sizes.cost(slots, 2),
        name="middle_group",
    )(order, counts, rows, *tops, *masses, *pieces)


def add_kernel(mine_ref, back_ref, out_ref):
    out_ref[...] = mine_ref[...] * LINK_SCALE + back_ref[...]


def scaled_sum(mine, back):
    return pl.pallas_call(
        add_kernel,
        out_shape=jax.ShapeDtypeStruct(mine.shape, mine.dtype),
        in_specs=[VMEM, VMEM],
        out_specs=VMEM,
        compiler_params=pltpu.CompilerParams(vmem_limit_bytes=VMEM_GRANT),
        cost_estimate=pl.CostEstimate(flops=30 * 10**9, bytes_accessed=12 * mine.size, transcendentals=0),
        name="scaled_sum",
    )(mine, back)


def on_device(rows, centroids, lists):
    count = lax.axis_size("blk")
    device = lax.axis_index("blk")
    cent = centroids.shape[0]
    own, stages = plan_of(count)
    groups = [(own,)] + [tuple(q for q, _, _ in stage) for stage in stages]
    slots = (2 * chip_place(lists, device, count) + ((lists ^ device) & 1)).astype(jnp.int32)
    sizes = Sizes(rows, *slots.shape, cent)
    order, counts = pairs_of(slots, 2 * max(q for members in groups for q in members) + 2)

    near = {own: centroids}
    tiles, tops, masses = [], [], []
    for members, stage in zip(groups, stages):
        arriving = [moved(near[source], shift) for _, source, shift in stage]
        pieces = [v for q in members for v in (near[q], other_core(near[q]))]
        scored = score_group(
            sizes, local_slots(members), order, counts, rows, pieces, fetch=not tiles
        )
        arriving, scored, near = lax.optimization_barrier((arriving, scored, near))
        if not tiles:
            rows = scored[3]
        tiles.append(scored[0])
        tops.append(scored[1])
        masses.append(scored[2])
        for (q, _, _), value in zip(stage, arriving):
            near[q] = value
    last = groups[-1]
    near_slots, far_slots = [2 * q for q in last], [2 * q + 1 for q in last]
    far = [other_core(near[q]) for q in last]
    near_tiles, top, mass = score_group(
        sizes, near_slots, order, counts, rows, [near[q] for q in last], fetch=False
    )
    tops.append(top)
    masses.append(mass)
    log_totals, shares, *far_sums = middle_group(
        sizes, far_slots, order, counts, rows, tops, masses, far
    )
    near_sums = sum_group(sizes, near_slots, order, counts, rows, near_tiles, shares)
    mine = dict(zip(last, near_sums))
    crossed = {q: other_core(v) for q, v in zip(last, far_sums)}
    total = {q: (mine[q] + crossed[q]) * LINK_SCALE for q in last}

    back = {q: [] for members in groups for q in members}
    for members, stage in zip(reversed(groups[:-1]), reversed(stages)):
        leaving = [total[q].astype(jnp.float16) for q, _, _ in stage]
        leaving, shares = lax.optimization_barrier((leaving, shares))
        arriving = [
            moved(value, shift if shift is None else -shift)
            for value, (_, _, shift) in zip(leaving, stage)
        ]
        at = groups.index(members)
        sums = sum_group(sizes, local_slots(members), order, counts, rows, tiles[at], shares)
        crossed = {q: other_core(v) for q, v in zip(members, sums[1::2])}
        arriving = lax.optimization_barrier(arriving)
        for value, (_, source, _) in zip(arriving, stage):
            back[source].append(value.astype(jnp.float32))
        for q, near_sum in zip(members, sums[::2]):
            if back[q]:
                part = scaled_sum(near_sum, functools.reduce(jnp.add, back[q]))
            else:
                part = near_sum * LINK_SCALE
            total[q] = part + crossed[q] * LINK_SCALE
    own_sums = total[own] * (1.0 / LINK_SCALE)
    updated = (own_sums[:cent] + PRIOR_MASS * centroids.astype(jnp.float32)) / (
        own_sums[cent, :cent][:, None] + PRIOR_MASS
    )
    return updated, log_totals.reshape(-1)


def solution(mesh):
    placed = P(("groups", "blk"), None)
    return jax.shard_map(
        on_device,
        mesh=mesh,
        in_specs=(placed, placed, placed),
        out_specs=(placed, P(("groups", "blk"))),
        check_vma=False,
    )
```

```python
import functools
import math

import jax
import jax.numpy as jnp
from jax import lax
from jax.experimental import pallas as pl
from jax.experimental.pallas import tpu as pltpu
from jax.sharding import PartitionSpec as P

BLOCK = 256
SPAN = 6
LOGIT_SCALE = 0.25
PRIOR_MASS = 8.0
LOG2E = math.log2(math.e)
LINK_SCALE = 1.0 / 16.0
EXTRA = 8
VMEM_GRANT = 42 << 20


def grid_plan():
    return 0, (
        ((2, 0, 4), (1, 0, None)),
        ((6, 0, -4), (3, 2, None)),
        ((5, 3, 4), (7, 6, None)),
    )


def ring_plan():
    reach = (SPAN + 1) // 2
    return reach, tuple(
        ((reach + hop + 1, reach + hop, 2), (reach - hop - 1, reach - hop, -2)) for hop in range(reach)
    )


def plan_of(count):
    return grid_plan() if count == 16 else ring_plan()


def chip_place(panel, device, count):
    if count == 16:
        return (device // 4 - panel // 4) % 4 * 2 + ((panel ^ device) >> 1 & 1)
    return (device // 2 - panel // 2 + (SPAN + 1) // 2) % (count // 2)


def moved(value, shift):
    count = lax.axis_size("blk")
    if shift is None:
        return lax.ppermute(value, "blk", [(i, i ^ 2) for i in range(count)])
    return lax.ppermute(value, "blk", [(i, (i + shift) % count) for i in range(count)])


def other_core(value):
    count = lax.axis_size("blk")
    return lax.ppermute(value, "blk", [(i, i ^ 1) for i in range(count)])


def pairs_of(slots, room):
    blocks, listed = slots.shape
    hit = slots[:, :, None] == jnp.arange(room, dtype=jnp.int32)
    listing = jnp.any(hit, axis=1)
    code = 8 * jnp.arange(blocks, dtype=jnp.int32)[:, None] + jnp.sum(
        jnp.where(hit, jnp.arange(listed, dtype=jnp.int32)[None, :, None], 0), axis=1
    )
    before = jnp.arange(blocks)[:, None] > jnp.arange(blocks)[None, :]
    rank = jnp.sum(jnp.where(before[:, :, None] & listing[None], 1, 0), axis=1)
    chosen = listing[:, :, None] & (rank[:, :, None] == jnp.arange(blocks))
    order = jnp.sum(jnp.where(chosen, code[:, :, None], 0), axis=0)
    return order.reshape(-1).astype(jnp.int32), jnp.sum(listing, axis=0).astype(jnp.int32)


def local_slots(members):
    return [2 * q + core for q in members for core in (0, 1)]


def some_pairs(order_ref, counts_ref, slot, blocks, first, number):
    work = []
    for i in range(number):
        code = order_ref[slot * blocks + jnp.minimum(first + i, counts_ref[slot] - 1)]
        work.append((first + i, code >> 3, (code & 7) * blocks + (code >> 3)))
    return work


def by_fours(count, act):
    fours = count // 4
    lax.fori_loop(0, fours, lambda k, _: (act(4 * k, 4), 0)[1], 0)
    lax.fori_loop(2 * fours, (count + 1) // 2, lambda k, _: (act(2 * k, 2), 0)[1], 0)


def by_eights(count, act):
    eights = count // 8
    lax.fori_loop(0, eights, lambda k, _: (act(8 * k, 8), 0)[1], 0)
    fours = (count - 8 * eights) // 4

    @pl.when(fours == 1)
    def _():
        act(8 * eights, 4)

    lax.fori_loop(
        4 * eights + 2 * fours, (count + 1) // 2, lambda k, _: (act(2 * k, 2), 0)[1], 0
    )


def rows_of(x, block):
    return x[pl.ds(pl.multiple_of(block * BLOCK, BLOCK), BLOCK)]


def find_norms(piece_refs, panels, norms):
    for p, piece in enumerate(piece_refs):
        panels[p] = piece[...]
        wide = piece[...].astype(jnp.float32)
        norm = jnp.sum(wide * wide, axis=1, keepdims=True)
        norms[p] = jnp.broadcast_to(norm * (0.5 * LOGIT_SCALE * LOG2E), norms.shape[1:])


def tile_of(panel, norm, block):
    scores = lax.dot_general(
        panel, block, (((1,), (1,)), ((), ())), preferred_element_type=jnp.float32
    )
    scores = scores * (LOGIT_SCALE * LOG2E) - jnp.concatenate([norm, norm], axis=1)
    top = jnp.max(scores, axis=0, keepdims=True)
    powers = jnp.exp2(scores - top)
    return powers, top, jnp.sum(powers, axis=0, keepdims=True)


def score_loop(
    slots, order_ref, counts_ref, x, panels, norms, tops, masses, tiles, here, done
):
    blocks = x.shape[0] // BLOCK
    tops[...] = jnp.full_like(tops, -jnp.inf)
    masses[...] = jnp.zeros_like(masses)
    starts = [jnp.int32(0)]
    for slot in slots:
        starts.append(starts[-1] + counts_ref[slot])
    count = starts.pop()

    def pair(j):
        p = functools.reduce(jnp.add, [(j >= start).astype(jnp.int32) for start in starts[1:]])
        first, slot = starts[0], jnp.int32(slots[0])
        for later, start in zip(slots[1:], starts[1:]):
            first = jnp.where(j >= start, start, first)
            slot = jnp.where(j >= start, later, slot)
        code = order_ref[slot * blocks + j - first]
        return p, p * blocks + j - first, code >> 3, (code & 7) * blocks + (code >> 3)

    def some(first, number):
        work = [pair(jnp.minimum(first + i, count - 1)) for i in range(number)]
        for _, _, b, _ in work:
            here(b)
        found = [tile_of(panels[p], norms[p], rows_of(x, b)) for p, _, b, _ in work]
        for (_, tile, _, at), (powers, top, mass) in zip(work, found):
            tiles[tile] = powers
            tops[pl.ds(at, 1)] = top
            masses[pl.ds(at, 1)] = mass
        for i, (_, tile, _, _) in enumerate(work):
            if number == 2 and i:
                pl.when(first + i < count)(functools.partial(done, tile))
            else:
                done(tile)

    by_eights(count, some)


def sum_loop(slots, order_ref, counts_ref, x, shares, acc, totals, tiles, ready):
    blocks = x.shape[0] // BLOCK
    cent = totals.shape[1]
    for p, slot in enumerate(slots):

        def some(first, number):
            work = some_pairs(order_ref, counts_ref, slot, blocks, first, number)
            for i, (j, _, _) in enumerate(work):
                if number == 2 and i:
                    pl.when(j < counts_ref[slot])(functools.partial(ready, p * blocks + j))
                else:
                    ready(p * blocks + j)
            partial, count = None, None
            for i, (j, b, at) in enumerate(work):
                share = shares[pl.ds(at, 1)]
                if number == 2 and i:
                    share = share * (j < counts_ref[slot]).astype(jnp.float32)
                    j = jnp.minimum(j, counts_ref[slot] - 1)
                weights = (tiles[p * blocks + j] * share).astype(jnp.bfloat16)
                wide = weights.astype(jnp.float32)
                wide = wide[:, :128] + wide[:, 128:]
                product = jnp.dot(weights, rows_of(x, b), preferred_element_type=jnp.float32)
                partial = product if partial is None else partial + product
                count = wide if count is None else count + wide
            totals[p] += count
            acc[p][pl.ds(0, cent)] += partial

        by_fours(counts_ref[slot], some)


def clear_sums(acc, totals):
    for ref in acc:
        ref[...] = jnp.zeros_like(ref)
    totals[...] = jnp.zeros_like(totals)


def store_totals(acc, totals):
    cent = totals.shape[1]
    for p, ref in enumerate(acc):
        row = jnp.sum(totals[p].T, axis=0, keepdims=True)
        ref[pl.ds(cent, EXTRA), pl.ds(0, cent)] = jnp.broadcast_to(row, (EXTRA, cent))


def over_tiles(slots, counts_ref, blocks, act):
    for p, slot in enumerate(slots):
        lax.fori_loop(0, counts_ref[slot], lambda i, _: (act(p * blocks + i), 0)[1], 0)


def score_kernel(slots, fetch, order_ref, counts_ref, rows_ref, *refs):
    pieces = len(slots)
    piece_refs = refs[:pieces]
    tiles_ref, tops, masses = refs[pieces : pieces + 3]
    refs = refs[pieces + 3 :]
    x = refs[0] if fetch else rows_ref
    panels, norms, tiles, tile_sem = refs[1:5] if fetch else refs[:4]
    blocks = x.shape[0] // BLOCK
    here = lambda b: None
    if fetch:
        row_sem, fetched = refs[5:]

        def bring(b):
            span = pl.ds(pl.multiple_of(b * BLOCK, BLOCK), BLOCK)
            return pltpu.make_async_copy(rows_ref.at[span], x.at[span], row_sem.at[b])

        for b in range(blocks):
            bring(b).start()
        fetched[0] = 0

        def here(b):
            first = fetched[0]
            lax.fori_loop(first, b + 1, lambda k, _: (bring(k).wait(), 0)[1], 0)
            fetched[0] = jnp.maximum(first, b + 1)

    find_norms(piece_refs, panels, norms)

    def outgoing(j):
        return pltpu.make_async_copy(tiles.at[j], tiles_ref.at[j], tile_sem.at[j])

    score_loop(
        slots, order_ref, counts_ref, x, panels, norms, tops, masses, tiles, here,
        lambda j: outgoing(j).start(),
    )
    here(blocks - 1)
    over_tiles(slots, counts_ref, blocks, lambda j: outgoing(j).wait())


def sum_kernel(slots, order_ref, counts_ref, x, tiles_ref, shares, *refs):
    pieces = len(slots)
    out_refs = refs[:pieces]
    totals, tiles, tile_sem = refs[pieces:]

    def incoming(j):
        return pltpu.make_async_copy(tiles_ref.at[j], tiles.at[j], tile_sem.at[j])

    over_tiles(slots, counts_ref, x.shape[0] // BLOCK, lambda j: incoming(j).start())
    clear_sums(out_refs, totals)
    sum_loop(
        slots, order_ref, counts_ref, x, shares, out_refs, totals, tiles,
        lambda j: incoming(j).wait(),
    )
    store_totals(out_refs, totals)


def middle_kernel(slots, listed, earlier, order_ref, counts_ref, x, *refs):
    pieces = len(slots)
    stat_refs = refs[: 2 * earlier]
    piece_refs = refs[2 * earlier : 2 * earlier + pieces]
    refs = refs[2 * earlier + pieces :]
    logs_ref, shares = refs[:2]
    out_refs = refs[2 : 2 + pieces]
    panels, norms, tiles, tops, masses, totals = refs[2 + pieces :]
    blocks = x.shape[0] // BLOCK
    clear_sums(out_refs, totals)
    find_norms(piece_refs, panels, norms)
    score_loop(
        slots, order_ref, counts_ref, x, panels, norms, tops, masses, tiles,
        lambda b: None, lambda j: None,
    )
    width = tops.shape[1]
    top = functools.reduce(jnp.maximum, [ref[...] for ref in stat_refs[:earlier]], tops[...])
    mass = functools.reduce(jnp.add, [ref[...] for ref in stat_refs[earlier:]], masses[...])
    top = top.reshape(listed, blocks, width)
    mass = mass.reshape(listed, blocks, width)
    highest = jnp.max(top, axis=0)
    factor = jnp.exp2(top - highest[None])
    whole = jnp.sum(factor * mass, axis=0)
    logs_ref[...] = (highest + jnp.log2(whole)) * (1.0 / LOG2E)
    shares[...] = (factor / whole[None]).reshape(listed * blocks, width)
    sum_loop(slots, order_ref, counts_ref, x, shares, out_refs, totals, tiles, lambda j: None)
    store_totals(out_refs, totals)


SMEM = pl.BlockSpec(memory_space=pltpu.SMEM)
HBM = pl.BlockSpec(memory_space=pltpu.HBM)
VMEM = pl.BlockSpec(memory_space=pltpu.VMEM)


class Sizes:
    def __init__(self, rows, blocks, listed, cent):
        self.blocks, self.listed, self.cent = blocks, listed, cent
        self.width = rows.shape[1]
        self.stats = jax.ShapeDtypeStruct((listed * blocks, BLOCK), jnp.float32)
        self.sums = jax.ShapeDtypeStruct((cent + EXTRA, self.width), jnp.float32)
        self.tiles = jax.ShapeDtypeStruct((4 * blocks, cent, BLOCK), jnp.float32)

    def cost(self, slots, products):
        pairs = self.blocks * self.listed * len(slots) / 14
        return pl.CostEstimate(
            flops=int(2 * products * pairs * self.cent * BLOCK * self.width),
            bytes_accessed=int(2 * self.blocks * BLOCK * self.width + 4 * pairs * self.cent * BLOCK),
            transcendentals=int(pairs * self.cent * BLOCK),
        )

    def panels(self, pieces):
        return pltpu.VMEM((pieces, self.cent, self.width), jnp.bfloat16)

    def columns(self, pieces):
        return pltpu.VMEM((pieces, self.cent, 128), jnp.float32)

    def tile_scratch(self, pieces):
        return pltpu.VMEM((pieces * self.blocks, self.cent, BLOCK), jnp.float32)


def score_group(sizes, slots, order, counts, rows, pieces, fetch):
    count = len(pieces)
    outs = (sizes.tiles, sizes.stats, sizes.stats)
    rows_outs, rows_scratch = (), []
    if fetch:
        rows_outs = (jax.ShapeDtypeStruct(rows.shape, rows.dtype),)
        rows_scratch = [pltpu.SemaphoreType.DMA((sizes.blocks,)), pltpu.SMEM((1,), jnp.int32)]
    return pl.pallas_call(
        functools.partial(score_kernel, slots, fetch),
        out_shape=outs + rows_outs,
        in_specs=[SMEM, SMEM, HBM if fetch else VMEM] + [VMEM] * count,
        out_specs=(HBM, VMEM, VMEM) + (VMEM,) * len(rows_outs),
        scratch_shapes=[
            sizes.panels(count),
            sizes.columns(count),
            sizes.tile_scratch(count),
            pltpu.SemaphoreType.DMA((count * sizes.blocks,)),
        ]
        + rows_scratch,
        compiler_params=pltpu.CompilerParams(vmem_limit_bytes=VMEM_GRANT),
        cost_estimate=sizes.cost(slots, 1),
        name="score_group",
    )(order, counts, rows, *pieces)


def sum_group(sizes, slots, order, counts, rows, tiles, shares):
    count = len(slots)
    return pl.pallas_call(
        functools.partial(sum_kernel, slots),
        out_shape=(sizes.sums,) * count,
        in_specs=[SMEM, SMEM, VMEM, HBM, VMEM],
        out_specs=(VMEM,) * count,
        scratch_shapes=[
            sizes.columns(count),
            sizes.tile_scratch(count),
            pltpu.SemaphoreType.DMA((count * sizes.blocks,)),
        ],
        compiler_params=pltpu.CompilerParams(vmem_limit_bytes=VMEM_GRANT),
        cost_estimate=sizes.cost(slots, 1),
        name="sum_group",
    )(order, counts, rows, tiles, shares)


def middle_group(sizes, slots, order, counts, rows, tops, masses, pieces):
    count = len(pieces)
    earlier = len(tops)
    return pl.pallas_call(
        functools.partial(middle_kernel, slots, sizes.listed, earlier),
        out_shape=(jax.ShapeDtypeStruct((sizes.blocks, BLOCK), jnp.float32), sizes.stats)
        + (sizes.sums,) * count,
        in_specs=[SMEM, SMEM, VMEM] + [VMEM] * (2 * earlier + count),
        out_specs=(VMEM, VMEM) + (VMEM,) * count,
        scratch_shapes=[
            sizes.panels(count),
            sizes.columns(count),
            sizes.tile_scratch(count),
            pltpu.VMEM(sizes.stats.shape, jnp.float32),
            pltpu.VMEM(sizes.stats.shape, jnp.float32),
            sizes.columns(count),
        ],
        compiler_params=pltpu.CompilerParams(vmem_limit_bytes=VMEM_GRANT),
        cost_estimate=sizes.cost(slots, 2),
        name="middle_group",
    )(order, counts, rows, *tops, *masses, *pieces)


def add_kernel(mine_ref, back_ref, out_ref):
    out_ref[...] = mine_ref[...] * LINK_SCALE + back_ref[...]


def scaled_sum(mine, back):
    return pl.pallas_call(
        add_kernel,
        out_shape=jax.ShapeDtypeStruct(mine.shape, mine.dtype),
        in_specs=[VMEM, VMEM],
        out_specs=VMEM,
        compiler_params=pltpu.CompilerParams(vmem_limit_bytes=VMEM_GRANT),
        cost_estimate=pl.CostEstimate(flops=30 * 10**9, bytes_accessed=12 * mine.size, transcendentals=0),
        name="scaled_sum",
    )(mine, back)


def on_device(rows, centroids, lists):
    count = lax.axis_size("blk")
    device = lax.axis_index("blk")
    cent = centroids.shape[0]
    own, stages = plan_of(count)
    groups = [(own,)] + [tuple(q for q, _, _ in stage) for stage in stages]
    slots = (2 * chip_place(lists, device, count) + ((lists ^ device) & 1)).astype(jnp.int32)
    sizes = Sizes(rows, *slots.shape, cent)
    order, counts = pairs_of(slots, 2 * max(q for members in groups for q in members) + 2)

    near = {own: centroids}
    tiles, tops, masses = [], [], []
    for members, stage in zip(groups, stages):
        arriving = [moved(near[source], shift) for _, source, shift in stage]
        pieces = [v for q in members for v in (near[q], other_core(near[q]))]
        scored = score_group(
            sizes, local_slots(members), order, counts, rows, pieces, fetch=not tiles
        )
        arriving, scored, near = lax.optimization_barrier((arriving, scored, near))
        if not tiles:
            rows = scored[3]
        tiles.append(scored[0])
        tops.append(scored[1])
        masses.append(scored[2])
        for (q, _, _), value in zip(stage, arriving):
            near[q] = value
    last = groups[-1]
    near_slots, far_slots = [2 * q for q in last], [2 * q + 1 for q in last]
    far = [other_core(near[q]) for q in last]
    near_tiles, top, mass = score_group(
        sizes, near_slots, order, counts, rows, [near[q] for q in last], fetch=False
    )
    tops.append(top)
    masses.append(mass)
    log_totals, shares, *far_sums = middle_group(
        sizes, far_slots, order, counts, rows, tops, masses, far
    )
    near_sums = sum_group(sizes, near_slots, order, counts, rows, near_tiles, shares)
    mine = dict(zip(last, near_sums))
    crossed = {q: other_core(v) for q, v in zip(last, far_sums)}
    total = {q: (mine[q] + crossed[q]) * LINK_SCALE for q in last}

    back = {q: [] for members in groups for q in members}
    for members, stage in zip(reversed(groups[:-1]), reversed(stages)):
        leaving = [total[q].astype(jnp.float16) for q, _, _ in stage]
        leaving, shares = lax.optimization_barrier((leaving, shares))
        arriving = [
            moved(value, shift if shift is None else -shift)
            for value, (_, _, shift) in zip(leaving, stage)
        ]
        at = groups.index(members)
        sums = sum_group(sizes, local_slots(members), order, counts, rows, tiles[at], shares)
        crossed = {q: other_core(v) for q, v in zip(members, sums[1::2])}
        arriving = lax.optimization_barrier(arriving)
        for value, (_, source, _) in zip(arriving, stage):
            back[source].append(value.astype(jnp.float32))
        for q, near_sum in zip(members, sums[::2]):
            if back[q]:
                part = scaled_sum(near_sum, functools.reduce(jnp.add, back[q]))
            else:
                part = near_sum * LINK_SCALE
            total[q] = part + crossed[q] * LINK_SCALE
    own_sums = total[own] * (1.0 / LINK_SCALE)
    updated = (own_sums[:cent] + PRIOR_MASS * centroids.astype(jnp.float32)) / (
        own_sums[cent, :cent][:, None] + PRIOR_MASS
    )
    return updated, log_totals.reshape(-1)


def solution(mesh):
    placed = P(("groups", "blk"), None)
    return jax.shard_map(
        on_device,
        mesh=mesh,
        in_specs=(placed, placed, placed),
        out_specs=(placed, P(("groups", "blk"))),
        check_vma=False,
    )
```

```python
import functools
import math

import jax
import jax.numpy as jnp
from jax import lax
from jax.experimental import pallas as pl
from jax.experimental.pallas import tpu as pltpu
from jax.sharding import PartitionSpec as P

BLOCK = 256
SPAN = 6
LOGIT_SCALE = 0.25
PRIOR_MASS = 8.0
LOG2E = math.log2(math.e)
LINK_SCALE = 1.0 / 16.0
EXTRA = 8
VMEM_GRANT = 42 << 20


def grid_plan():
    return 0, (
        ((1, 0, None), (2, 0, 4)),
        ((6, 0, -4), (3, 2, None)),
        ((5, 3, 4), (7, 6, None)),
    )


def ring_plan():
    reach = (SPAN + 1) // 2
    return reach, tuple(
        ((reach + hop + 1, reach + hop, 2), (reach - hop - 1, reach - hop, -2)) for hop in range(reach)
    )


def plan_of(count):
    return grid_plan() if count == 16 else ring_plan()


def chip_place(panel, device, count):
    if count == 16:
        return (device // 4 - panel // 4) % 4 * 2 + ((panel ^ device) >> 1 & 1)
    return (device // 2 - panel // 2 + (SPAN + 1) // 2) % (count // 2)


def moved(value, shift):
    count = lax.axis_size("blk")
    if shift is None:
        return lax.ppermute(value, "blk", [(i, i ^ 2) for i in range(count)])
    return lax.ppermute(value, "blk", [(i, (i + shift) % count) for i in range(count)])


def other_core(value):
    count = lax.axis_size("blk")
    return lax.ppermute(value, "blk", [(i, i ^ 1) for i in range(count)])


def packed(value):
    return (value * LINK_SCALE).astype(jnp.float16)


def pairs_of(slots, room):
    blocks, listed = slots.shape
    hit = slots[:, :, None] == jnp.arange(room, dtype=jnp.int32)
    listing = jnp.any(hit, axis=1)
    code = 8 * jnp.arange(blocks, dtype=jnp.int32)[:, None] + jnp.sum(
        jnp.where(hit, jnp.arange(listed, dtype=jnp.int32)[None, :, None], 0), axis=1
    )
    before = jnp.arange(blocks)[:, None] > jnp.arange(blocks)[None, :]
    rank = jnp.sum(jnp.where(before[:, :, None] & listing[None], 1, 0), axis=1)
    chosen = listing[:, :, None] & (rank[:, :, None] == jnp.arange(blocks))
    order = jnp.sum(jnp.where(chosen, code[:, :, None], 0), axis=0)
    return order.reshape(-1).astype(jnp.int32), jnp.sum(listing, axis=0).astype(jnp.int32)


def local_slots(members):
    return [2 * q + core for q in members for core in (0, 1)]


def some_pairs(order_ref, counts_ref, slot, blocks, first, number):
    work = []
    for i in range(number):
        code = order_ref[slot * blocks + jnp.minimum(first + i, counts_ref[slot] - 1)]
        work.append((first + i, code >> 3, (code & 7) * blocks + (code >> 3)))
    return work


def by_fours(count, act):
    fours = count // 4
    lax.fori_loop(0, fours, lambda k, _: (act(4 * k, 4), 0)[1], 0)
    lax.fori_loop(2 * fours, (count + 1) // 2, lambda k, _: (act(2 * k, 2), 0)[1], 0)


def by_eights(count, act):
    eights = count // 8
    lax.fori_loop(0, eights, lambda k, _: (act(8 * k, 8), 0)[1], 0)
    fours = (count - 8 * eights) // 4

    @pl.when(fours == 1)
    def _():
        act(8 * eights, 4)

    lax.fori_loop(
        4 * eights + 2 * fours, (count + 1) // 2, lambda k, _: (act(2 * k, 2), 0)[1], 0
    )


def rows_of(x, block):
    return x[pl.ds(pl.multiple_of(block * BLOCK, BLOCK), BLOCK)]


def find_norms(piece_refs, panels, norms):
    for p, piece in enumerate(piece_refs):
        panels[p] = piece[...]
        wide = piece[...].astype(jnp.float32)
        norm = jnp.sum(wide * wide, axis=1, keepdims=True)
        norms[p] = jnp.broadcast_to(norm * (0.5 * LOGIT_SCALE * LOG2E), norms.shape[1:])


def tile_of(panel, norm, block):
    scores = lax.dot_general(
        panel, block, (((1,), (1,)), ((), ())), preferred_element_type=jnp.float32
    )
    scores = scores * (LOGIT_SCALE * LOG2E) - jnp.concatenate([norm, norm], axis=1)
    top = jnp.max(scores, axis=0, keepdims=True)
    powers = jnp.exp2(scores - top)
    return powers, top, jnp.sum(powers, axis=0, keepdims=True)


def score_loop(
    slots, order_ref, counts_ref, x, panels, norms, tops, masses, tiles, here, done
):
    blocks = x.shape[0] // BLOCK
    tops[...] = jnp.full_like(tops, -jnp.inf)
    masses[...] = jnp.zeros_like(masses)
    starts = [jnp.int32(0)]
    for slot in slots:
        starts.append(starts[-1] + counts_ref[slot])
    count = starts.pop()

    def pair(j):
        p = functools.reduce(jnp.add, [(j >= start).astype(jnp.int32) for start in starts[1:]])
        first, slot = starts[0], jnp.int32(slots[0])
        for later, start in zip(slots[1:], starts[1:]):
            first = jnp.where(j >= start, start, first)
            slot = jnp.where(j >= start, later, slot)
        code = order_ref[slot * blocks + j - first]
        return p, p * blocks + j - first, code >> 3, (code & 7) * blocks + (code >> 3)

    def some(first, number):
        work = [pair(jnp.minimum(first + i, count - 1)) for i in range(number)]
        for _, _, b, _ in work:
            here(b)
        found = [tile_of(panels[p], norms[p], rows_of(x, b)) for p, _, b, _ in work]
        for (_, tile, _, at), (powers, top, mass) in zip(work, found):
            tiles[tile] = powers
            tops[pl.ds(at, 1)] = top
            masses[pl.ds(at, 1)] = mass
        for i, (_, tile, _, _) in enumerate(work):
            if number == 2 and i:
                pl.when(first + i < count)(functools.partial(done, tile))
            else:
                done(tile)

    by_eights(count, some)


def sum_loop(slots, order_ref, counts_ref, x, shares, acc, totals, tiles, ready):
    blocks = x.shape[0] // BLOCK
    cent = totals.shape[1]
    for p, slot in enumerate(slots):

        def some(first, number):
            work = some_pairs(order_ref, counts_ref, slot, blocks, first, number)
            for i, (j, _, _) in enumerate(work):
                if number == 2 and i:
                    pl.when(j < counts_ref[slot])(functools.partial(ready, p * blocks + j))
                else:
                    ready(p * blocks + j)
            partial, count = None, None
            for i, (j, b, at) in enumerate(work):
                share = shares[pl.ds(at, 1)]
                if number == 2 and i:
                    share = share * (j < counts_ref[slot]).astype(jnp.float32)
                    j = jnp.minimum(j, counts_ref[slot] - 1)
                weights = (tiles[p * blocks + j] * share).astype(jnp.bfloat16)
                wide = weights.astype(jnp.float32)
                wide = wide[:, :128] + wide[:, 128:]
                product = jnp.dot(weights, rows_of(x, b), preferred_element_type=jnp.float32)
                partial = product if partial is None else partial + product
                count = wide if count is None else count + wide
            totals[p] += count
            acc[p][pl.ds(0, cent)] += partial

        by_fours(counts_ref[slot], some)


def clear_sums(acc, totals):
    for ref in acc:
        ref[...] = jnp.zeros_like(ref)
    totals[...] = jnp.zeros_like(totals)


def store_totals(acc, totals):
    cent = totals.shape[1]
    for p, ref in enumerate(acc):
        row = jnp.sum(totals[p].T, axis=0, keepdims=True)
        ref[pl.ds(cent, EXTRA), pl.ds(0, cent)] = jnp.broadcast_to(row, (EXTRA, cent))


def over_tiles(slots, counts_ref, blocks, act):
    for p, slot in enumerate(slots):
        lax.fori_loop(0, counts_ref[slot], lambda i, _: (act(p * blocks + i), 0)[1], 0)


def score_kernel(slots, fetch, order_ref, counts_ref, rows_ref, *refs):
    pieces = len(slots)
    piece_refs = refs[:pieces]
    tiles_ref, tops, masses = refs[pieces : pieces + 3]
    refs = refs[pieces + 3 :]
    x = refs[0] if fetch else rows_ref
    panels, norms, tiles, tile_sem = refs[1:5] if fetch else refs[:4]
    blocks = x.shape[0] // BLOCK
    here = lambda b: None
    if fetch:
        row_sem, fetched = refs[5:]

        def bring(b):
            span = pl.ds(pl.multiple_of(b * BLOCK, BLOCK), BLOCK)
            return pltpu.make_async_copy(rows_ref.at[span], x.at[span], row_sem.at[b])

        for b in range(blocks):
            bring(b).start()
        fetched[0] = 0

        def here(b):
            first = fetched[0]
            lax.fori_loop(first, b + 1, lambda k, _: (bring(k).wait(), 0)[1], 0)
            fetched[0] = jnp.maximum(first, b + 1)

    find_norms(piece_refs, panels, norms)

    def outgoing(j):
        return pltpu.make_async_copy(tiles.at[j], tiles_ref.at[j], tile_sem.at[j])

    score_loop(
        slots, order_ref, counts_ref, x, panels, norms, tops, masses, tiles, here,
        lambda j: outgoing(j).start(),
    )
    here(blocks - 1)
    over_tiles(slots, counts_ref, blocks, lambda j: outgoing(j).wait())


def sum_kernel(slots, order_ref, counts_ref, x, tiles_ref, shares, *refs):
    pieces = len(slots)
    out_refs = refs[:pieces]
    totals, tiles, tile_sem = refs[pieces:]

    def incoming(j):
        return pltpu.make_async_copy(tiles_ref.at[j], tiles.at[j], tile_sem.at[j])

    over_tiles(slots, counts_ref, x.shape[0] // BLOCK, lambda j: incoming(j).start())
    clear_sums(out_refs, totals)
    sum_loop(
        slots, order_ref, counts_ref, x, shares, out_refs, totals, tiles,
        lambda j: incoming(j).wait(),
    )
    store_totals(out_refs, totals)


def middle_kernel(slots, listed, earlier, order_ref, counts_ref, x, *refs):
    pieces = len(slots)
    stat_refs = refs[: 2 * earlier]
    piece_refs = refs[2 * earlier : 2 * earlier + pieces]
    refs = refs[2 * earlier + pieces :]
    logs_ref, shares = refs[:2]
    out_refs = refs[2 : 2 + pieces]
    panels, norms, tiles, tops, masses, totals = refs[2 + pieces :]
    blocks = x.shape[0] // BLOCK
    clear_sums(out_refs, totals)
    find_norms(piece_refs, panels, norms)
    score_loop(
        slots, order_ref, counts_ref, x, panels, norms, tops, masses, tiles,
        lambda b: None, lambda j: None,
    )
    width = tops.shape[1]
    top = functools.reduce(jnp.maximum, [ref[...] for ref in stat_refs[:earlier]], tops[...])
    mass = functools.reduce(jnp.add, [ref[...] for ref in stat_refs[earlier:]], masses[...])
    top = top.reshape(listed, blocks, width)
    mass = mass.reshape(listed, blocks, width)
    highest = jnp.max(top, axis=0)
    factor = jnp.exp2(top - highest[None])
    whole = jnp.sum(factor * mass, axis=0)
    logs_ref[...] = (highest + jnp.log2(whole)) * (1.0 / LOG2E)
    shares[...] = (factor / whole[None]).reshape(listed * blocks, width)
    sum_loop(slots, order_ref, counts_ref, x, shares, out_refs, totals, tiles, lambda j: None)
    store_totals(out_refs, totals)


SMEM = pl.BlockSpec(memory_space=pltpu.SMEM)
HBM = pl.BlockSpec(memory_space=pltpu.HBM)
VMEM = pl.BlockSpec(memory_space=pltpu.VMEM)


class Sizes:
    def __init__(self, rows, blocks, listed, cent):
        self.blocks, self.listed, self.cent = blocks, listed, cent
        self.width = rows.shape[1]
        self.stats = jax.ShapeDtypeStruct((listed * blocks, BLOCK), jnp.float32)
        self.sums = jax.ShapeDtypeStruct((cent + EXTRA, self.width), jnp.float32)
        self.tiles = jax.ShapeDtypeStruct((4 * blocks, cent, BLOCK), jnp.float32)

    def cost(self, slots, products):
        pairs = self.blocks * self.listed * len(slots) / 14
        return pl.CostEstimate(
            flops=int(2 * products * pairs * self.cent * BLOCK * self.width),
            bytes_accessed=int(2 * self.blocks * BLOCK * self.width + 4 * pairs * self.cent * BLOCK),
            transcendentals=int(pairs * self.cent * BLOCK),
        )

    def panels(self, pieces):
        return pltpu.VMEM((pieces, self.cent, self.width), jnp.bfloat16)

    def columns(self, pieces):
        return pltpu.VMEM((pieces, self.cent, 128), jnp.float32)

    def tile_scratch(self, pieces):
        return pltpu.VMEM((pieces * self.blocks, self.cent, BLOCK), jnp.float32)


def score_group(sizes, slots, order, counts, rows, pieces, fetch):
    count = len(pieces)
    outs = (sizes.tiles, sizes.stats, sizes.stats)
    rows_outs, rows_scratch = (), []
    if fetch:
        rows_outs = (jax.ShapeDtypeStruct(rows.shape, rows.dtype),)
        rows_scratch = [pltpu.SemaphoreType.DMA((sizes.blocks,)), pltpu.SMEM((1,), jnp.int32)]
    return pl.pallas_call(
        functools.partial(score_kernel, slots, fetch),
        out_shape=outs + rows_outs,
        in_specs=[SMEM, SMEM, HBM if fetch else VMEM] + [VMEM] * count,
        out_specs=(HBM, VMEM, VMEM) + (VMEM,) * len(rows_outs),
        scratch_shapes=[
            sizes.panels(count),
            sizes.columns(count),
            sizes.tile_scratch(count),
            pltpu.SemaphoreType.DMA((count * sizes.blocks,)),
        ]
        + rows_scratch,
        compiler_params=pltpu.CompilerParams(vmem_limit_bytes=VMEM_GRANT),
        cost_estimate=sizes.cost(slots, 1),
        name="score_group",
    )(order, counts, rows, *pieces)


def sum_group(sizes, slots, order, counts, rows, tiles, shares):
    count = len(slots)
    return pl.pallas_call(
        functools.partial(sum_kernel, slots),
        out_shape=(sizes.sums,) * count,
        in_specs=[SMEM, SMEM, VMEM, HBM, VMEM],
        out_specs=(VMEM,) * count,
        scratch_shapes=[
            sizes.columns(count),
            sizes.tile_scratch(count),
            pltpu.SemaphoreType.DMA((count * sizes.blocks,)),
        ],
        compiler_params=pltpu.CompilerParams(vmem_limit_bytes=VMEM_GRANT),
        cost_estimate=sizes.cost(slots, 1),
        name="sum_group",
    )(order, counts, rows, tiles, shares)


def middle_group(sizes, slots, order, counts, rows, tops, masses, pieces):
    count = len(pieces)
    earlier = len(tops)
    return pl.pallas_call(
        functools.partial(middle_kernel, slots, sizes.listed, earlier),
        out_shape=(jax.ShapeDtypeStruct((sizes.blocks, BLOCK), jnp.float32), sizes.stats)
        + (sizes.sums,) * count,
        in_specs=[SMEM, SMEM, VMEM] + [VMEM] * (2 * earlier + count),
        out_specs=(VMEM, VMEM) + (VMEM,) * count,
        scratch_shapes=[
            sizes.panels(count),
            sizes.columns(count),
            sizes.tile_scratch(count),
            pltpu.VMEM(sizes.stats.shape, jnp.float32),
            pltpu.VMEM(sizes.stats.shape, jnp.float32),
            sizes.columns(count),
        ],
        compiler_params=pltpu.CompilerParams(vmem_limit_bytes=VMEM_GRANT),
        cost_estimate=sizes.cost(slots, 2),
        name="middle_group",
    )(order, counts, rows, *tops, *masses, *pieces)


def add_kernel(mine_ref, back_ref, out_ref):
    out_ref[...] = mine_ref[...] * LINK_SCALE + back_ref[...]


def scaled_sum(mine, back):
    return pl.pallas_call(
        add_kernel,
        out_shape=jax.ShapeDtypeStruct(mine.shape, mine.dtype),
        in_specs=[VMEM, VMEM],
        out_specs=VMEM,
        compiler_params=pltpu.CompilerParams(vmem_limit_bytes=VMEM_GRANT),
        cost_estimate=pl.CostEstimate(flops=30 * 10**9, bytes_accessed=12 * mine.size, transcendentals=0),
        name="scaled_sum",
    )(mine, back)


def on_device(rows, centroids, lists):
    count = lax.axis_size("blk")
    device = lax.axis_index("blk")
    cent = centroids.shape[0]
    own, stages = plan_of(count)
    groups = [(own,)] + [tuple(q for q, _, _ in stage) for stage in stages]
    slots = (2 * chip_place(lists, device, count) + ((lists ^ device) & 1)).astype(jnp.int32)
    sizes = Sizes(rows, *slots.shape, cent)
    order, counts = pairs_of(slots, 2 * max(q for members in groups for q in members) + 2)

    near = {own: centroids}
    tiles, tops, masses = [], [], []
    for members, stage in zip(groups, stages):
        arriving = [moved(near[source], shift) for _, source, shift in stage]
        pieces = [v for q in members for v in (near[q], other_core(near[q]))]
        scored = score_group(
            sizes, local_slots(members), order, counts, rows, pieces, fetch=not tiles
        )
        arriving, scored, near = lax.optimization_barrier((arriving, scored, near))
        if not tiles:
            rows = scored[3]
        tiles.append(scored[0])
        tops.append(scored[1])
        masses.append(scored[2])
        for (q, _, _), value in zip(stage, arriving):
            near[q] = value
    last = groups[-1]
    near_slots, far_slots = [2 * q for q in last], [2 * q + 1 for q in last]
    far = [other_core(near[q]) for q in last]
    near_tiles, top, mass = score_group(
        sizes, near_slots, order, counts, rows, [near[q] for q in last], fetch=False
    )
    tops.append(top)
    masses.append(mass)
    log_totals, shares, *far_sums = middle_group(
        sizes, far_slots, order, counts, rows, tops, masses, far
    )
    near_sums = sum_group(sizes, near_slots, order, counts, rows, near_tiles, shares)
    mine = dict(zip(last, near_sums))
    crossed = {q: other_core(packed(v)) for q, v in zip(last, far_sums)}
    total = {q: mine[q] * LINK_SCALE + crossed[q].astype(jnp.float32) for q in last}

    back = {q: [] for members in groups for q in members}
    for members, stage in zip(reversed(groups[:-1]), reversed(stages)):
        stage = sorted(stage, key=lambda move: move[2] is None)
        leaving = [total[q].astype(jnp.float16) for q, _, _ in stage]
        leaving, shares = lax.optimization_barrier((leaving, shares))
        arriving = [
            moved(value, shift if shift is None else -shift)
            for value, (_, _, shift) in zip(leaving, stage)
        ]
        at = groups.index(members)
        sums = sum_group(sizes, local_slots(members), order, counts, rows, tiles[at], shares)
        crossed = {q: other_core(packed(v)) for q, v in zip(members, sums[1::2])}
        arriving = lax.optimization_barrier(arriving)
        for value, (_, source, _) in zip(arriving, stage):
            back[source].append(value.astype(jnp.float32))
        for q, near_sum in zip(members, sums[::2]):
            if back[q]:
                part = scaled_sum(near_sum, functools.reduce(jnp.add, back[q]))
            else:
                part = near_sum * LINK_SCALE
            total[q] = part + crossed[q].astype(jnp.float32)
    own_sums = total[own] * (1.0 / LINK_SCALE)
    updated = (own_sums[:cent] + PRIOR_MASS * centroids.astype(jnp.float32)) / (
        own_sums[cent, :cent][:, None] + PRIOR_MASS
    )
    return updated, log_totals.reshape(-1)


def solution(mesh):
    placed = P(("groups", "blk"), None)
    return jax.shard_map(
        on_device,
        mesh=mesh,
        in_specs=(placed, placed, placed),
        out_specs=(placed, P(("groups", "blk"))),
        check_vma=False,
    )
```

```python
import functools
import math

import jax
import jax.numpy as jnp
from jax import lax
from jax.experimental import pallas as pl
from jax.experimental.pallas import tpu as pltpu
from jax.sharding import PartitionSpec as P

BLOCK = 256
SPAN = 6
LOGIT_SCALE = 0.25
PRIOR_MASS = 8.0
LOG2E = math.log2(math.e)
LINK_SCALE = 1.0 / 16.0
EXTRA = 8
VMEM_GRANT = 42 << 20


def grid_plan():
    return 0, (
        ((1, 0, None), (2, 0, 4)),
        ((6, 0, -4), (3, 2, None)),
        ((5, 3, 4), (7, 6, None)),
    )


def ring_plan():
    reach = (SPAN + 1) // 2
    return reach, tuple(
        ((reach + hop + 1, reach + hop, 2), (reach - hop - 1, reach - hop, -2)) for hop in range(reach)
    )


def plan_of(count):
    return grid_plan() if count == 16 else ring_plan()


def chip_place(panel, device, count):
    if count == 16:
        return (device // 4 - panel // 4) % 4 * 2 + ((panel ^ device) >> 1 & 1)
    return (device // 2 - panel // 2 + (SPAN + 1) // 2) % (count // 2)


def moved(value, shift):
    count = lax.axis_size("blk")
    if shift is None:
        return lax.ppermute(value, "blk", [(i, i ^ 2) for i in range(count)])
    return lax.ppermute(value, "blk", [(i, (i + shift) % count) for i in range(count)])


def other_core(value):
    count = lax.axis_size("blk")
    return lax.ppermute(value, "blk", [(i, i ^ 1) for i in range(count)])


def packed(value):
    return (value * LINK_SCALE).astype(jnp.float16)


def pairs_of(slots, room):
    blocks, listed = slots.shape
    hit = slots[:, :, None] == jnp.arange(room, dtype=jnp.int32)
    listing = jnp.any(hit, axis=1)
    code = 8 * jnp.arange(blocks, dtype=jnp.int32)[:, None] + jnp.sum(
        jnp.where(hit, jnp.arange(listed, dtype=jnp.int32)[None, :, None], 0), axis=1
    )
    before = jnp.arange(blocks)[:, None] > jnp.arange(blocks)[None, :]
    rank = jnp.sum(jnp.where(before[:, :, None] & listing[None], 1, 0), axis=1)
    chosen = listing[:, :, None] & (rank[:, :, None] == jnp.arange(blocks))
    order = jnp.sum(jnp.where(chosen, code[:, :, None], 0), axis=0)
    return order.reshape(-1).astype(jnp.int32), jnp.sum(listing, axis=0).astype(jnp.int32)


def local_slots(members):
    return [2 * q + core for q in members for core in (0, 1)]


def some_pairs(order_ref, counts_ref, slot, blocks, first, number):
    work = []
    for i in range(number):
        code = order_ref[slot * blocks + jnp.minimum(first + i, counts_ref[slot] - 1)]
        work.append((first + i, code >> 3, (code & 7) * blocks + (code >> 3)))
    return work


def by_fours(count, act):
    fours = count // 4
    lax.fori_loop(0, fours, lambda k, _: (act(4 * k, 4), 0)[1], 0)
    lax.fori_loop(2 * fours, (count + 1) // 2, lambda k, _: (act(2 * k, 2), 0)[1], 0)


def by_eights(count, act):
    eights = count // 8
    lax.fori_loop(0, eights, lambda k, _: (act(8 * k, 8), 0)[1], 0)
    fours = (count - 8 * eights) // 4

    @pl.when(fours == 1)
    def _():
        act(8 * eights, 4)

    lax.fori_loop(
        4 * eights + 2 * fours, (count + 1) // 2, lambda k, _: (act(2 * k, 2), 0)[1], 0
    )


def rows_of(x, block):
    return x[pl.ds(pl.multiple_of(block * BLOCK, BLOCK), BLOCK)]


def find_norms(piece_refs, panels, norms):
    for p, piece in enumerate(piece_refs):
        if piece is not None:
            panels[p] = piece[...]
        wide = panels[p].astype(jnp.float32)
        norm = jnp.sum(wide * wide, axis=1, keepdims=True)
        norms[p] = jnp.broadcast_to(norm * (0.5 * LOGIT_SCALE * LOG2E), norms.shape[1:])


def tile_of(panel, norm, block):
    scores = lax.dot_general(
        panel, block, (((1,), (1,)), ((), ())), preferred_element_type=jnp.float32
    )
    scores = scores * (LOGIT_SCALE * LOG2E) - jnp.concatenate([norm, norm], axis=1)
    top = jnp.max(scores, axis=0, keepdims=True)
    powers = jnp.exp2(scores - top)
    return powers, top, jnp.sum(powers, axis=0, keepdims=True)


def score_loop(
    slots, order_ref, counts_ref, x, panels, norms, tops, masses, tiles, here, done
):
    blocks = x.shape[0] // BLOCK
    tops[...] = jnp.full_like(tops, -jnp.inf)
    masses[...] = jnp.zeros_like(masses)
    starts = [jnp.int32(0)]
    for slot in slots:
        starts.append(starts[-1] + counts_ref[slot])
    count = starts.pop()

    def pair(j):
        p = sum([(j >= start).astype(jnp.int32) for start in starts[1:]], jnp.int32(0))
        first, slot = starts[0], jnp.int32(slots[0])
        for later, start in zip(slots[1:], starts[1:]):
            first = jnp.where(j >= start, start, first)
            slot = jnp.where(j >= start, later, slot)
        code = order_ref[slot * blocks + j - first]
        return p, p * blocks + j - first, code >> 3, (code & 7) * blocks + (code >> 3)

    def some(first, number):
        work = [pair(jnp.minimum(first + i, count - 1)) for i in range(number)]
        for _, _, b, _ in work:
            here(b)
        found = [tile_of(panels[p], norms[p], rows_of(x, b)) for p, _, b, _ in work]
        for (_, tile, _, at), (powers, top, mass) in zip(work, found):
            tiles[tile] = powers
            tops[pl.ds(at, 1)] = top
            masses[pl.ds(at, 1)] = mass
        for i, (_, tile, _, _) in enumerate(work):
            if number == 2 and i:
                pl.when(first + i < count)(functools.partial(done, tile))
            else:
                done(tile)

    by_eights(count, some)


def sum_loop(slots, order_ref, counts_ref, x, shares, acc, totals, tiles, ready):
    blocks = x.shape[0] // BLOCK
    cent = totals.shape[1]
    for p, slot in enumerate(slots):

        def some(first, number):
            work = some_pairs(order_ref, counts_ref, slot, blocks, first, number)
            for i, (j, _, _) in enumerate(work):
                if number == 2 and i:
                    pl.when(j < counts_ref[slot])(functools.partial(ready, p, j))
                else:
                    ready(p, j)
            partial, count = None, None
            for i, (j, b, at) in enumerate(work):
                share = shares[pl.ds(at, 1)]
                if number == 2 and i:
                    share = share * (j < counts_ref[slot]).astype(jnp.float32)
                    j = jnp.minimum(j, counts_ref[slot] - 1)
                weights = (tiles[p * blocks + j] * share).astype(jnp.bfloat16)
                wide = weights.astype(jnp.float32)
                wide = wide[:, :128] + wide[:, 128:]
                product = jnp.dot(weights, rows_of(x, b), preferred_element_type=jnp.float32)
                partial = product if partial is None else partial + product
                count = wide if count is None else count + wide
            totals[p] += count
            acc[p][pl.ds(0, cent)] += partial

        by_fours(counts_ref[slot], some)


def clear_sums(acc, totals):
    for ref in acc:
        ref[...] = jnp.zeros_like(ref)
    totals[...] = jnp.zeros_like(totals)


def store_totals(acc, totals):
    cent = totals.shape[1]
    for p, ref in enumerate(acc):
        row = jnp.sum(totals[p].T, axis=0, keepdims=True)
        ref[pl.ds(cent, EXTRA), pl.ds(0, cent)] = jnp.broadcast_to(row, (EXTRA, cent))


def over_tiles(slots, counts_ref, act):
    for p, slot in enumerate(slots):
        lax.fori_loop(0, counts_ref[slot], lambda i, _, p=p: (act(p, i), 0)[1], 0)


def score_kernel(slots, fetch, order_ref, counts_ref, rows_ref, *refs):
    pieces = len(slots)
    piece_refs = refs[:pieces]
    tiles_ref, tops, masses = refs[pieces : pieces + 3]
    refs = refs[pieces + 3 :]
    x = refs[0] if fetch else rows_ref
    panels, norms, tiles, tile_sem = refs[1:5] if fetch else refs[:4]
    blocks = x.shape[0] // BLOCK
    here = lambda b: None
    if fetch:
        row_sem, fetched, panel_sem = refs[5:]
        brought = [
            pltpu.make_async_copy(ref, panels.at[p], panel_sem.at[p])
            for p, ref in enumerate(piece_refs)
        ]
        for copy in brought:
            copy.start()

        def bring(b):
            span = pl.ds(pl.multiple_of(b * BLOCK, BLOCK), BLOCK)
            return pltpu.make_async_copy(rows_ref.at[span], x.at[span], row_sem.at[b])

        for b in range(blocks):
            bring(b).start()
        fetched[0] = 0

        def here(b):
            first = fetched[0]
            lax.fori_loop(first, b + 1, lambda k, _: (bring(k).wait(), 0)[1], 0)
            fetched[0] = jnp.maximum(first, b + 1)

        for copy in brought:
            copy.wait()
        piece_refs = [None] * pieces

    find_norms(piece_refs, panels, norms)

    def outgoing(j):
        return pltpu.make_async_copy(tiles.at[j], tiles_ref.at[j], tile_sem.at[j])

    score_loop(
        slots, order_ref, counts_ref, x, panels, norms, tops, masses, tiles, here,
        lambda j: outgoing(j).start(),
    )
    here(blocks - 1)
    over_tiles(slots, counts_ref, lambda p, i: outgoing(p * blocks + i).wait())


def sum_kernel(slots, sources, order_ref, counts_ref, x, shares, *refs):
    pieces = len(slots)
    arrays = len({which for which, _ in sources})
    tiles_refs, refs = refs[:arrays], refs[arrays:]
    out_refs = refs[:pieces]
    blocks = x.shape[0] // BLOCK
    totals, tiles, tile_sem = refs[pieces:]

    def incoming(p, i):
        which, first = sources[p]
        j = p * blocks + i
        return pltpu.make_async_copy(tiles_refs[which].at[first + i], tiles.at[j], tile_sem.at[j])

    over_tiles(slots, counts_ref, lambda p, i: incoming(p, i).start())
    clear_sums(out_refs, totals)
    sum_loop(
        slots, order_ref, counts_ref, x, shares, out_refs, totals, tiles,
        lambda p, i: incoming(p, i).wait(),
    )
    store_totals(out_refs, totals)


def middle_kernel(slots, listed, earlier, order_ref, counts_ref, x, *refs):
    pieces = len(slots)
    stat_refs = refs[: 2 * earlier]
    piece_refs = refs[2 * earlier : 2 * earlier + pieces]
    refs = refs[2 * earlier + pieces :]
    logs_ref, shares = refs[:2]
    out_refs = refs[2 : 2 + pieces]
    panels, norms, tiles, tops, masses, totals = refs[2 + pieces :]
    blocks = x.shape[0] // BLOCK
    clear_sums(out_refs, totals)
    find_norms(piece_refs, panels, norms)
    score_loop(
        slots, order_ref, counts_ref, x, panels, norms, tops, masses, tiles,
        lambda b: None, lambda j: None,
    )
    width = tops.shape[1]
    top = functools.reduce(jnp.maximum, [ref[...] for ref in stat_refs[:earlier]], tops[...])
    mass = functools.reduce(jnp.add, [ref[...] for ref in stat_refs[earlier:]], masses[...])
    top = top.reshape(listed, blocks, width)
    mass = mass.reshape(listed, blocks, width)
    highest = jnp.max(top, axis=0)
    factor = jnp.exp2(top - highest[None])
    whole = jnp.sum(factor * mass, axis=0)
    logs_ref[...] = (highest + jnp.log2(whole)) * (1.0 / LOG2E)
    shares[...] = (factor / whole[None]).reshape(listed * blocks, width)
    sum_loop(slots, order_ref, counts_ref, x, shares, out_refs, totals, tiles, lambda p, i: None)
    store_totals(out_refs, totals)


SMEM = pl.BlockSpec(memory_space=pltpu.SMEM)
HBM = pl.BlockSpec(memory_space=pltpu.HBM)
VMEM = pl.BlockSpec(memory_space=pltpu.VMEM)


class Sizes:
    def __init__(self, rows, blocks, listed, cent):
        self.blocks, self.listed, self.cent = blocks, listed, cent
        self.width = rows.shape[1]
        self.stats = jax.ShapeDtypeStruct((listed * blocks, BLOCK), jnp.float32)
        self.sums = jax.ShapeDtypeStruct((cent + EXTRA, self.width), jnp.float32)
        self.tiles = jax.ShapeDtypeStruct((5 * blocks, cent, BLOCK), jnp.float32)

    def cost(self, slots, products):
        pairs = self.blocks * self.listed * len(slots) / 14
        return pl.CostEstimate(
            flops=int(2 * products * pairs * self.cent * BLOCK * self.width),
            bytes_accessed=int(2 * self.blocks * BLOCK * self.width + 4 * pairs * self.cent * BLOCK),
            transcendentals=int(pairs * self.cent * BLOCK),
        )

    def panels(self, pieces):
        return pltpu.VMEM((pieces, self.cent, self.width), jnp.bfloat16)

    def columns(self, pieces):
        return pltpu.VMEM((pieces, self.cent, 128), jnp.float32)

    def tile_scratch(self, pieces):
        return pltpu.VMEM((pieces * self.blocks, self.cent, BLOCK), jnp.float32)


def score_group(sizes, slots, order, counts, rows, pieces, fetch):
    count = len(pieces)
    outs = (sizes.tiles, sizes.stats, sizes.stats)
    rows_outs, rows_scratch = (), []
    if fetch:
        rows_outs = (jax.ShapeDtypeStruct(rows.shape, rows.dtype),)
        rows_scratch = [
            pltpu.SemaphoreType.DMA((sizes.blocks,)),
            pltpu.SMEM((1,), jnp.int32),
            pltpu.SemaphoreType.DMA((count,)),
        ]
    return pl.pallas_call(
        functools.partial(score_kernel, slots, fetch),
        out_shape=outs + rows_outs,
        in_specs=[SMEM, SMEM] + ([HBM] * (1 + count) if fetch else [VMEM] * (1 + count)),
        out_specs=(HBM, VMEM, VMEM) + (VMEM,) * len(rows_outs),
        scratch_shapes=[
            sizes.panels(count),
            sizes.columns(count),
            sizes.tile_scratch(count),
            pltpu.SemaphoreType.DMA((count * sizes.blocks,)),
        ]
        + rows_scratch,
        compiler_params=pltpu.CompilerParams(vmem_limit_bytes=VMEM_GRANT),
        cost_estimate=sizes.cost(slots, 1),
        name="score_group",
    )(order, counts, rows, *pieces)


def sum_group(sizes, slots, order, counts, rows, shares, places, tiles):
    count = len(slots)
    used = sorted({places[slot][0] for slot in slots})
    sources = [(used.index(places[slot][0]), places[slot][1]) for slot in slots]
    return pl.pallas_call(
        functools.partial(sum_kernel, slots, sources),
        out_shape=(sizes.sums,) * count,
        in_specs=[SMEM, SMEM, VMEM, VMEM] + [HBM] * len(used),
        out_specs=(VMEM,) * count,
        scratch_shapes=[
            sizes.columns(count),
            sizes.tile_scratch(count),
            pltpu.SemaphoreType.DMA((count * sizes.blocks,)),
        ],
        compiler_params=pltpu.CompilerParams(vmem_limit_bytes=VMEM_GRANT),
        cost_estimate=sizes.cost(slots, 1),
        name="sum_group",
    )(order, counts, rows, shares, *[tiles[which] for which in used])


def middle_group(sizes, slots, order, counts, rows, tops, masses, pieces):
    count = len(pieces)
    earlier = len(tops)
    return pl.pallas_call(
        functools.partial(middle_kernel, slots, sizes.listed, earlier),
        out_shape=(jax.ShapeDtypeStruct((sizes.blocks, BLOCK), jnp.float32), sizes.stats)
        + (sizes.sums,) * count,
        in_specs=[SMEM, SMEM, VMEM] + [VMEM] * (2 * earlier + count),
        out_specs=(VMEM, VMEM) + (VMEM,) * count,
        scratch_shapes=[
            sizes.panels(count),
            sizes.columns(count),
            sizes.tile_scratch(count),
            pltpu.VMEM(sizes.stats.shape, jnp.float32),
            pltpu.VMEM(sizes.stats.shape, jnp.float32),
            sizes.columns(count),
        ],
        compiler_params=pltpu.CompilerParams(vmem_limit_bytes=VMEM_GRANT),
        cost_estimate=sizes.cost(slots, 2),
        name="middle_group",
    )(order, counts, rows, *tops, *masses, *pieces)


def add_kernel(mine_ref, back_ref, out_ref):
    out_ref[...] = mine_ref[...] * LINK_SCALE + back_ref[...]


def scaled_sum(mine, back):
    return pl.pallas_call(
        add_kernel,
        out_shape=jax.ShapeDtypeStruct(mine.shape, mine.dtype),
        in_specs=[VMEM, VMEM],
        out_specs=VMEM,
        compiler_params=pltpu.CompilerParams(vmem_limit_bytes=VMEM_GRANT),
        cost_estimate=pl.CostEstimate(flops=30 * 10**9, bytes_accessed=12 * mine.size, transcendentals=0),
        name="scaled_sum",
    )(mine, back)


def on_device(rows, centroids, lists):
    count = lax.axis_size("blk")
    device = lax.axis_index("blk")
    cent = centroids.shape[0]
    own, stages = plan_of(count)
    groups = [(own,)] + [tuple(q for q, _, _ in stage) for stage in stages]
    slots = (2 * chip_place(lists, device, count) + ((lists ^ device) & 1)).astype(jnp.int32)
    sizes = Sizes(rows, *slots.shape, cent)
    order, counts = pairs_of(slots, 2 * max(q for members in groups for q in members) + 2)

    near, far = {own: centroids}, {}
    tiles, tops, masses, places = [], [], [], {}

    def score(slots, fetch=False):
        pieces = [(far if slot & 1 else near)[slot >> 1] for slot in slots]
        for p, slot in enumerate(slots):
            places[slot] = (len(tiles), p * sizes.blocks)
        return score_group(sizes, slots, order, counts, rows, pieces, fetch)

    for number, stage in enumerate(stages):
        arriving = [moved(near[source], shift) for _, source, shift in stage]
        for q in groups[number]:
            far[q] = other_core(near[q])
        if number == 0:
            scored = score([2 * own], fetch=True)
        elif number == 1:
            scored = score([2 * own + 1] + local_slots(groups[1]))
        else:
            scored = score(local_slots(groups[number]))
        arriving, scored, near, far = lax.optimization_barrier((arriving, scored, near, far))
        if number == 0:
            rows = scored[3]
        tiles.append(scored[0])
        tops.append(scored[1])
        masses.append(scored[2])
        for (q, _, _), value in zip(stage, arriving):
            near[q] = value
    last = groups[-1]
    near_slots, far_slots = [2 * q for q in last], [2 * q + 1 for q in last]
    for q in last:
        far[q] = other_core(near[q])
    scored = score(near_slots)
    tiles.append(scored[0])
    tops.append(scored[1])
    masses.append(scored[2])
    log_totals, shares, *far_sums = middle_group(
        sizes, far_slots, order, counts, rows, tops, masses, [far[q] for q in last]
    )
    near_sums = sum_group(sizes, near_slots, order, counts, rows, shares, places, tiles)
    mine = dict(zip(last, near_sums))
    crossed = {q: other_core(packed(v)) for q, v in zip(last, far_sums)}
    total = {q: mine[q] * LINK_SCALE + crossed[q].astype(jnp.float32) for q in last}

    back = {q: [] for members in groups for q in members}
    for members, stage in zip(reversed(groups[:-1]), reversed(stages)):
        stage = sorted(stage, key=lambda move: move[2] is None)
        leaving = [total[q].astype(jnp.float16) for q, _, _ in stage]
        leaving, shares = lax.optimization_barrier((leaving, shares))
        arriving = [
            moved(value, shift if shift is None else -shift)
            for value, (_, _, shift) in zip(leaving, stage)
        ]
        sums = sum_group(sizes, local_slots(members), order, counts, rows, shares, places, tiles)
        crossed = {q: other_core(packed(v)) for q, v in zip(members, sums[1::2])}
        arriving = lax.optimization_barrier(arriving)
        for value, (_, source, _) in zip(arriving, stage):
            back[source].append(value.astype(jnp.float32))
        for q, near_sum in zip(members, sums[::2]):
            if back[q]:
                part = scaled_sum(near_sum, functools.reduce(jnp.add, back[q]))
            else:
                part = near_sum * LINK_SCALE
            total[q] = part + crossed[q].astype(jnp.float32)
    own_sums = total[own] * (1.0 / LINK_SCALE)
    updated = (own_sums[:cent] + PRIOR_MASS * centroids.astype(jnp.float32)) / (
        own_sums[cent, :cent][:, None] + PRIOR_MASS
    )
    return updated, log_totals.reshape(-1)


def solution(mesh):
    placed = P(("groups", "blk"), None)
    return jax.shard_map(
        on_device,
        mesh=mesh,
        in_specs=(placed, placed, placed),
        out_specs=(placed, P(("groups", "blk"))),
        check_vma=False,
    )
```

```python
import functools
import math

import jax
import jax.numpy as jnp
from jax import lax
from jax.experimental import pallas as pl
from jax.experimental.pallas import tpu as pltpu
from jax.sharding import PartitionSpec as P

BLOCK = 256
SPAN = 6
LOGIT_SCALE = 0.25
PRIOR_MASS = 8.0
LOG2E = math.log2(math.e)
LINK_SCALE = 1.0 / 16.0
EXTRA = 8
VMEM_GRANT = 42 << 20


def grid_plan():
    return 0, (
        ((1, 0, None), (2, 0, 4)),
        ((6, 0, -4), (3, 2, None)),
        ((5, 3, 4), (7, 6, None)),
    )


def ring_plan():
    reach = (SPAN + 1) // 2
    return reach, tuple(
        ((reach + hop + 1, reach + hop, 2), (reach - hop - 1, reach - hop, -2)) for hop in range(reach)
    )


def plan_of(count):
    return grid_plan() if count == 16 else ring_plan()


def chip_place(panel, device, count):
    if count == 16:
        return (device // 4 - panel // 4) % 4 * 2 + ((panel ^ device) >> 1 & 1)
    return (device // 2 - panel // 2 + (SPAN + 1) // 2) % (count // 2)


def moved(value, shift):
    count = lax.axis_size("blk")
    if shift is None:
        return lax.ppermute(value, "blk", [(i, i ^ 2) for i in range(count)])
    return lax.ppermute(value, "blk", [(i, (i + shift) % count) for i in range(count)])


def other_core(value):
    count = lax.axis_size("blk")
    return lax.ppermute(value, "blk", [(i, i ^ 1) for i in range(count)])


def packed(value):
    return (value * LINK_SCALE).astype(jnp.float16)


def pairs_of(slots, room):
    blocks, listed = slots.shape
    hit = slots[:, :, None] == jnp.arange(room, dtype=jnp.int32)
    listing = jnp.any(hit, axis=1)
    code = 8 * jnp.arange(blocks, dtype=jnp.int32)[:, None] + jnp.sum(
        jnp.where(hit, jnp.arange(listed, dtype=jnp.int32)[None, :, None], 0), axis=1
    )
    before = jnp.arange(blocks)[:, None] > jnp.arange(blocks)[None, :]
    rank = jnp.sum(jnp.where(before[:, :, None] & listing[None], 1, 0), axis=1)
    chosen = listing[:, :, None] & (rank[:, :, None] == jnp.arange(blocks))
    order = jnp.sum(jnp.where(chosen, code[:, :, None], 0), axis=0)
    return order.reshape(-1).astype(jnp.int32), jnp.sum(listing, axis=0).astype(jnp.int32)


def local_slots(members):
    return [2 * q + core for q in members for core in (0, 1)]


def some_pairs(order_ref, counts_ref, slot, blocks, first, number):
    work = []
    for i in range(number):
        code = order_ref[slot * blocks + jnp.minimum(first + i, counts_ref[slot] - 1)]
        work.append((first + i, code >> 3, (code & 7) * blocks + (code >> 3)))
    return work


def by_fours(count, act):
    fours = count // 4
    lax.fori_loop(0, fours, lambda k, _: (act(4 * k, 4), 0)[1], 0)
    lax.fori_loop(2 * fours, (count + 1) // 2, lambda k, _: (act(2 * k, 2), 0)[1], 0)


def by_eights(count, act):
    eights = count // 8
    lax.fori_loop(0, eights, lambda k, _: (act(8 * k, 8), 0)[1], 0)
    fours = (count - 8 * eights) // 4

    @pl.when(fours == 1)
    def _():
        act(8 * eights, 4)

    lax.fori_loop(
        4 * eights + 2 * fours, (count + 1) // 2, lambda k, _: (act(2 * k, 2), 0)[1], 0
    )


def rows_of(x, block):
    return x[pl.ds(pl.multiple_of(block * BLOCK, BLOCK), BLOCK)]


def find_norms(piece_refs, panels, norms):
    for p, piece in enumerate(piece_refs):
        if piece is not None:
            panels[p] = piece[...]
        wide = panels[p].astype(jnp.float32)
        norm = jnp.sum(wide * wide, axis=1, keepdims=True)
        norms[p] = jnp.broadcast_to(norm * (0.5 * LOGIT_SCALE * LOG2E), norms.shape[1:])


def tile_of(panel, norm, block):
    scores = lax.dot_general(
        panel, block, (((1,), (1,)), ((), ())), preferred_element_type=jnp.float32
    )
    scores = scores * (LOGIT_SCALE * LOG2E) - jnp.concatenate([norm, norm], axis=1)
    top = jnp.max(scores, axis=0, keepdims=True)
    powers = jnp.exp2(scores - top)
    return powers, top, jnp.sum(powers, axis=0, keepdims=True)


def score_loop(
    slots, order_ref, counts_ref, x, panels, norms, tops, masses, tiles, here, done
):
    blocks = x.shape[0] // BLOCK
    tops[...] = jnp.full_like(tops, -jnp.inf)
    masses[...] = jnp.zeros_like(masses)
    starts = [jnp.int32(0)]
    for slot in slots:
        starts.append(starts[-1] + counts_ref[slot])
    count = starts.pop()

    def pair(j):
        p = sum([(j >= start).astype(jnp.int32) for start in starts[1:]], jnp.int32(0))
        first, slot = starts[0], jnp.int32(slots[0])
        for later, start in zip(slots[1:], starts[1:]):
            first = jnp.where(j >= start, start, first)
            slot = jnp.where(j >= start, later, slot)
        code = order_ref[slot * blocks + j - first]
        return p, p * blocks + j - first, code >> 3, (code & 7) * blocks + (code >> 3)

    def some(first, number):
        work = [pair(jnp.minimum(first + i, count - 1)) for i in range(number)]
        for _, _, b, _ in work:
            here(b)
        found = [tile_of(panels[p], norms[p], rows_of(x, b)) for p, _, b, _ in work]
        for (_, tile, _, at), (powers, top, mass) in zip(work, found):
            tiles[tile] = powers
            tops[pl.ds(at, 1)] = top
            masses[pl.ds(at, 1)] = mass
        for i, (_, tile, _, _) in enumerate(work):
            if number == 2 and i:
                pl.when(first + i < count)(functools.partial(done, tile))
            else:
                done(tile)

    by_eights(count, some)


def sum_loop(slots, order_ref, counts_ref, x, shares, acc, totals, tiles, ready):
    blocks = x.shape[0] // BLOCK
    cent = totals.shape[1]
    for p, slot in enumerate(slots):

        def some(first, number):
            work = some_pairs(order_ref, counts_ref, slot, blocks, first, number)
            for i, (j, _, _) in enumerate(work):
                if number == 2 and i:
                    pl.when(j < counts_ref[slot])(functools.partial(ready, p, j))
                else:
                    ready(p, j)
            partial, count = None, None
            for i, (j, b, at) in enumerate(work):
                share = shares[pl.ds(at, 1)]
                if number == 2 and i:
                    share = share * (j < counts_ref[slot]).astype(jnp.float32)
                    j = jnp.minimum(j, counts_ref[slot] - 1)
                weights = (tiles[p * blocks + j] * share).astype(jnp.bfloat16)
                wide = weights.astype(jnp.float32)
                wide = wide[:, :128] + wide[:, 128:]
                product = jnp.dot(weights, rows_of(x, b), preferred_element_type=jnp.float32)
                partial = product if partial is None else partial + product
                count = wide if count is None else count + wide
            totals[p] += count
            acc[p][pl.ds(0, cent)] += partial

        by_fours(counts_ref[slot], some)


def clear_sums(acc, totals):
    for ref in acc:
        ref[...] = jnp.zeros_like(ref)
    totals[...] = jnp.zeros_like(totals)


def store_totals(acc, totals):
    cent = totals.shape[1]
    for p, ref in enumerate(acc):
        row = jnp.sum(totals[p].T, axis=0, keepdims=True)
        ref[pl.ds(cent, EXTRA), pl.ds(0, cent)] = jnp.broadcast_to(row, (EXTRA, cent))


def over_tiles(slots, counts_ref, act):
    for p, slot in enumerate(slots):
        lax.fori_loop(0, counts_ref[slot], lambda i, _, p=p: (act(p, i), 0)[1], 0)


def score_kernel(slots, fetch, order_ref, counts_ref, rows_ref, *refs):
    pieces = len(slots)
    piece_refs = refs[:pieces]
    tiles_ref, tops, masses = refs[pieces : pieces + 3]
    refs = refs[pieces + 3 :]
    x = refs[0] if fetch else rows_ref
    panels, norms, tiles, tile_sem = refs[1:5] if fetch else refs[:4]
    blocks = x.shape[0] // BLOCK
    here = lambda b: None
    if fetch:
        row_sem, fetched, panel_sem = refs[5:]
        brought = [
            pltpu.make_async_copy(ref, panels.at[p], panel_sem.at[p])
            for p, ref in enumerate(piece_refs)
        ]
        for copy in brought:
            copy.start()

        def bring(b):
            span = pl.ds(pl.multiple_of(b * BLOCK, BLOCK), BLOCK)
            return pltpu.make_async_copy(rows_ref.at[span], x.at[span], row_sem.at[b])

        for b in range(blocks):
            bring(b).start()
        fetched[0] = 0

        def here(b):
            first = fetched[0]
            lax.fori_loop(first, b + 1, lambda k, _: (bring(k).wait(), 0)[1], 0)
            fetched[0] = jnp.maximum(first, b + 1)

        for copy in brought:
            copy.wait()
        piece_refs = [None] * pieces

    find_norms(piece_refs, panels, norms)

    def outgoing(j):
        return pltpu.make_async_copy(tiles.at[j], tiles_ref.at[j], tile_sem.at[j])

    score_loop(
        slots, order_ref, counts_ref, x, panels, norms, tops, masses, tiles, here,
        lambda j: outgoing(j).start(),
    )
    here(blocks - 1)
    over_tiles(slots, counts_ref, lambda p, i: outgoing(p * blocks + i).wait())


def sum_kernel(slots, sources, order_ref, counts_ref, x, shares, *refs):
    pieces = len(slots)
    arrays = len({which for which, _ in sources})
    tiles_refs, refs = refs[:arrays], refs[arrays:]
    out_refs = refs[:pieces]
    blocks = x.shape[0] // BLOCK
    totals, tiles, tile_sem = refs[pieces:]

    def incoming(p, i):
        which, first = sources[p]
        j = p * blocks + i
        return pltpu.make_async_copy(tiles_refs[which].at[first + i], tiles.at[j], tile_sem.at[j])

    over_tiles(slots, counts_ref, lambda p, i: incoming(p, i).start())
    clear_sums(out_refs, totals)
    sum_loop(
        slots, order_ref, counts_ref, x, shares, out_refs, totals, tiles,
        lambda p, i: incoming(p, i).wait(),
    )
    store_totals(out_refs, totals)


def middle_kernel(
    slots, near_slots, sources, listed, earlier, order_ref, counts_ref, x, near_tiles_ref, *refs
):
    pieces = len(slots)
    both = slots + near_slots
    stat_refs = refs[: 2 * earlier]
    piece_refs = refs[2 * earlier : 2 * earlier + pieces]
    refs = refs[2 * earlier + pieces :]
    logs_ref, shares = refs[:2]
    out_refs = refs[2 : 2 + len(both)]
    panels, norms, tiles, tops, masses, totals, tile_sem = refs[2 + len(both) :]
    blocks = x.shape[0] // BLOCK

    def incoming(k, i):
        source = near_tiles_ref.at[sources[k] + i]
        return pltpu.make_async_copy(
            source, tiles.at[(pieces + k) * blocks + i], tile_sem.at[k * blocks + i]
        )

    def ready(p, i):
        if p >= pieces:
            incoming(p - pieces, i).wait()

    over_tiles(near_slots, counts_ref, lambda k, i: incoming(k, i).start())
    clear_sums(out_refs, totals)
    find_norms(piece_refs, panels, norms)
    score_loop(
        slots, order_ref, counts_ref, x, panels, norms, tops, masses, tiles,
        lambda b: None, lambda j: None,
    )
    width = tops.shape[1]
    top = functools.reduce(jnp.maximum, [ref[...] for ref in stat_refs[:earlier]], tops[...])
    mass = functools.reduce(jnp.add, [ref[...] for ref in stat_refs[earlier:]], masses[...])
    top = top.reshape(listed, blocks, width)
    mass = mass.reshape(listed, blocks, width)
    highest = jnp.max(top, axis=0)
    factor = jnp.exp2(top - highest[None])
    whole = jnp.sum(factor * mass, axis=0)
    logs_ref[...] = (highest + jnp.log2(whole)) * (1.0 / LOG2E)
    shares[...] = (factor / whole[None]).reshape(listed * blocks, width)
    sum_loop(both, order_ref, counts_ref, x, shares, out_refs, totals, tiles, ready)
    store_totals(out_refs, totals)


SMEM = pl.BlockSpec(memory_space=pltpu.SMEM)
HBM = pl.BlockSpec(memory_space=pltpu.HBM)
VMEM = pl.BlockSpec(memory_space=pltpu.VMEM)


class Sizes:
    def __init__(self, rows, blocks, listed, cent):
        self.blocks, self.listed, self.cent = blocks, listed, cent
        self.width = rows.shape[1]
        self.stats = jax.ShapeDtypeStruct((listed * blocks, BLOCK), jnp.float32)
        self.sums = jax.ShapeDtypeStruct((cent + EXTRA, self.width), jnp.float32)
        self.tiles = jax.ShapeDtypeStruct((5 * blocks, cent, BLOCK), jnp.float32)

    def cost(self, slots, products):
        pairs = self.blocks * self.listed * len(slots) / 14
        return pl.CostEstimate(
            flops=int(2 * products * pairs * self.cent * BLOCK * self.width),
            bytes_accessed=int(2 * self.blocks * BLOCK * self.width + 4 * pairs * self.cent * BLOCK),
            transcendentals=int(pairs * self.cent * BLOCK),
        )

    def panels(self, pieces):
        return pltpu.VMEM((pieces, self.cent, self.width), jnp.bfloat16)

    def columns(self, pieces):
        return pltpu.VMEM((pieces, self.cent, 128), jnp.float32)

    def tile_scratch(self, pieces):
        return pltpu.VMEM((pieces * self.blocks, self.cent, BLOCK), jnp.float32)


def score_group(sizes, slots, order, counts, rows, pieces, fetch):
    count = len(pieces)
    outs = (sizes.tiles, sizes.stats, sizes.stats)
    rows_outs, rows_scratch = (), []
    if fetch:
        rows_outs = (jax.ShapeDtypeStruct(rows.shape, rows.dtype),)
        rows_scratch = [
            pltpu.SemaphoreType.DMA((sizes.blocks,)),
            pltpu.SMEM((1,), jnp.int32),
            pltpu.SemaphoreType.DMA((count,)),
        ]
    return pl.pallas_call(
        functools.partial(score_kernel, slots, fetch),
        out_shape=outs + rows_outs,
        in_specs=[SMEM, SMEM] + ([HBM] * (1 + count) if fetch else [VMEM] * (1 + count)),
        out_specs=(HBM, VMEM, VMEM) + (VMEM,) * len(rows_outs),
        scratch_shapes=[
            sizes.panels(count),
            sizes.columns(count),
            sizes.tile_scratch(count),
            pltpu.SemaphoreType.DMA((count * sizes.blocks,)),
        ]
        + rows_scratch,
        compiler_params=pltpu.CompilerParams(vmem_limit_bytes=VMEM_GRANT),
        cost_estimate=sizes.cost(slots, 1),
        name="score_group",
    )(order, counts, rows, *pieces)


def sum_group(sizes, slots, order, counts, rows, shares, places, tiles):
    count = len(slots)
    used = sorted({places[slot][0] for slot in slots})
    sources = [(used.index(places[slot][0]), places[slot][1]) for slot in slots]
    return pl.pallas_call(
        functools.partial(sum_kernel, slots, sources),
        out_shape=(sizes.sums,) * count,
        in_specs=[SMEM, SMEM, VMEM, VMEM] + [HBM] * len(used),
        out_specs=(VMEM,) * count,
        scratch_shapes=[
            sizes.columns(count),
            sizes.tile_scratch(count),
            pltpu.SemaphoreType.DMA((count * sizes.blocks,)),
        ],
        compiler_params=pltpu.CompilerParams(vmem_limit_bytes=VMEM_GRANT),
        cost_estimate=sizes.cost(slots, 1),
        name="sum_group",
    )(order, counts, rows, shares, *[tiles[which] for which in used])


def middle_group(
    sizes, slots, near_slots, order, counts, rows, tops, masses, pieces, places, tiles
):
    count = len(pieces)
    sums = len(slots) + len(near_slots)
    earlier = len(tops)
    sources = [places[slot][1] for slot in near_slots]
    return pl.pallas_call(
        functools.partial(middle_kernel, slots, near_slots, sources, sizes.listed, earlier),
        out_shape=(jax.ShapeDtypeStruct((sizes.blocks, BLOCK), jnp.float32), sizes.stats)
        + (sizes.sums,) * sums,
        in_specs=[SMEM, SMEM, VMEM, HBM] + [VMEM] * (2 * earlier + count),
        out_specs=(VMEM, VMEM) + (VMEM,) * sums,
        scratch_shapes=[
            sizes.panels(count),
            sizes.columns(count),
            sizes.tile_scratch(sums),
            pltpu.VMEM(sizes.stats.shape, jnp.float32),
            pltpu.VMEM(sizes.stats.shape, jnp.float32),
            sizes.columns(sums),
            pltpu.SemaphoreType.DMA((len(near_slots) * sizes.blocks,)),
        ],
        compiler_params=pltpu.CompilerParams(vmem_limit_bytes=VMEM_GRANT),
        cost_estimate=sizes.cost(slots, 3),
        name="middle_group",
    )(order, counts, rows, tiles[places[near_slots[0]][0]], *tops, *masses, *pieces)


def add_kernel(mine_ref, back_ref, out_ref):
    out_ref[...] = mine_ref[...] * LINK_SCALE + back_ref[...]


def scaled_sum(mine, back):
    return pl.pallas_call(
        add_kernel,
        out_shape=jax.ShapeDtypeStruct(mine.shape, mine.dtype),
        in_specs=[VMEM, VMEM],
        out_specs=VMEM,
        compiler_params=pltpu.CompilerParams(vmem_limit_bytes=VMEM_GRANT),
        cost_estimate=pl.CostEstimate(flops=30 * 10**9, bytes_accessed=12 * mine.size, transcendentals=0),
        name="scaled_sum",
    )(mine, back)


def on_device(rows, centroids, lists):
    count = lax.axis_size("blk")
    device = lax.axis_index("blk")
    cent = centroids.shape[0]
    own, stages = plan_of(count)
    groups = [(own,)] + [tuple(q for q, _, _ in stage) for stage in stages]
    slots = (2 * chip_place(lists, device, count) + ((lists ^ device) & 1)).astype(jnp.int32)
    sizes = Sizes(rows, *slots.shape, cent)
    order, counts = pairs_of(slots, 2 * max(q for members in groups for q in members) + 2)

    near, far = {own: centroids}, {}
    tiles, tops, masses, places = [], [], [], {}

    def score(slots, fetch=False):
        pieces = [(far if slot & 1 else near)[slot >> 1] for slot in slots]
        for p, slot in enumerate(slots):
            places[slot] = (len(tiles), p * sizes.blocks)
        return score_group(sizes, slots, order, counts, rows, pieces, fetch)

    for number, stage in enumerate(stages):
        arriving = [moved(near[source], shift) for _, source, shift in stage]
        for q in groups[number]:
            far[q] = other_core(near[q])
        if number == 0:
            scored = score([2 * own], fetch=True)
        elif number == 1:
            scored = score([2 * own + 1] + local_slots(groups[1]))
        else:
            scored = score(local_slots(groups[number]))
        arriving, scored, near, far = lax.optimization_barrier((arriving, scored, near, far))
        if number == 0:
            rows = scored[3]
        tiles.append(scored[0])
        tops.append(scored[1])
        masses.append(scored[2])
        for (q, _, _), value in zip(stage, arriving):
            near[q] = value
    last = groups[-1]
    near_slots, far_slots = [2 * q for q in last], [2 * q + 1 for q in last]
    for q in last:
        far[q] = other_core(near[q])
    scored = score(near_slots)
    tiles.append(scored[0])
    tops.append(scored[1])
    masses.append(scored[2])
    log_totals, shares, *sums = middle_group(
        sizes, far_slots, near_slots, order, counts, rows, tops, masses,
        [far[q] for q in last], places, tiles,
    )
    far_sums, near_sums = sums[: len(last)], sums[len(last) :]
    mine = dict(zip(last, near_sums))
    crossed = {q: other_core(packed(v)) for q, v in zip(last, far_sums)}
    total = {q: mine[q] * LINK_SCALE + crossed[q].astype(jnp.float32) for q in last}

    back = {q: [] for members in groups for q in members}
    for members, stage in zip(reversed(groups[:-1]), reversed(stages)):
        stage = sorted(stage, key=lambda move: move[2] is None)
        leaving = [total[q].astype(jnp.float16) for q, _, _ in stage]
        leaving, shares = lax.optimization_barrier((leaving, shares))
        arriving = [
            moved(value, shift if shift is None else -shift)
            for value, (_, _, shift) in zip(leaving, stage)
        ]
        sums = sum_group(sizes, local_slots(members), order, counts, rows, shares, places, tiles)
        crossed = {q: other_core(packed(v)) for q, v in zip(members, sums[1::2])}
        arriving = lax.optimization_barrier(arriving)
        for value, (_, source, _) in zip(arriving, stage):
            back[source].append(value.astype(jnp.float32))
        for q, near_sum in zip(members, sums[::2]):
            if back[q]:
                part = scaled_sum(near_sum, functools.reduce(jnp.add, back[q]))
            else:
                part = near_sum * LINK_SCALE
            total[q] = part + crossed[q].astype(jnp.float32)
    own_sums = total[own] * (1.0 / LINK_SCALE)
    updated = (own_sums[:cent] + PRIOR_MASS * centroids.astype(jnp.float32)) / (
        own_sums[cent, :cent][:, None] + PRIOR_MASS
    )
    return updated, log_totals.reshape(-1)


def solution(mesh):
    placed = P(("groups", "blk"), None)
    return jax.shard_map(
        on_device,
        mesh=mesh,
        in_specs=(placed, placed, placed),
        out_specs=(placed, P(("groups", "blk"))),
        check_vma=False,
    )
```

```python
import functools
import math

import jax
import jax.numpy as jnp
from jax import lax
from jax.experimental import pallas as pl
from jax.experimental.pallas import tpu as pltpu
from jax.sharding import PartitionSpec as P

BLOCK = 256
SPAN = 6
LOGIT_SCALE = 0.25
PRIOR_MASS = 8.0
LOG2E = math.log2(math.e)
LINK_SCALE = 1.0 / 16.0
EXTRA = 8
VMEM_GRANT = 42 << 20


def grid_plan():
    return 0, (
        ((1, 0, None), (2, 0, 4)),
        ((6, 0, -4), (3, 2, None)),
        ((5, 3, 4), (7, 6, None)),
    )


def ring_plan():
    reach = (SPAN + 1) // 2
    return reach, tuple(
        ((reach + hop + 1, reach + hop, 2), (reach - hop - 1, reach - hop, -2)) for hop in range(reach)
    )


def plan_of(count):
    return grid_plan() if count == 16 else ring_plan()


def chip_place(panel, device, count):
    if count == 16:
        return (device // 4 - panel // 4) % 4 * 2 + ((panel ^ device) >> 1 & 1)
    return (device // 2 - panel // 2 + (SPAN + 1) // 2) % (count // 2)


def moved(value, shift):
    count = lax.axis_size("blk")
    if shift is None:
        return lax.ppermute(value, "blk", [(i, i ^ 2) for i in range(count)])
    return lax.ppermute(value, "blk", [(i, (i + shift) % count) for i in range(count)])


def other_core(value):
    count = lax.axis_size("blk")
    return lax.ppermute(value, "blk", [(i, i ^ 1) for i in range(count)])


def packed(value):
    return (value * LINK_SCALE).astype(jnp.float16)


def pairs_of(slots, room):
    blocks, listed = slots.shape
    hit = slots[:, :, None] == jnp.arange(room, dtype=jnp.int32)
    listing = jnp.any(hit, axis=1)
    code = 8 * jnp.arange(blocks, dtype=jnp.int32)[:, None] + jnp.sum(
        jnp.where(hit, jnp.arange(listed, dtype=jnp.int32)[None, :, None], 0), axis=1
    )
    before = jnp.arange(blocks)[:, None] > jnp.arange(blocks)[None, :]
    rank = jnp.sum(jnp.where(before[:, :, None] & listing[None], 1, 0), axis=1)
    chosen = listing[:, :, None] & (rank[:, :, None] == jnp.arange(blocks))
    order = jnp.sum(jnp.where(chosen, code[:, :, None], 0), axis=0)
    return order.reshape(-1).astype(jnp.int32), jnp.sum(listing, axis=0).astype(jnp.int32)


def local_slots(members):
    return [2 * q + core for q in members for core in (0, 1)]


def some_pairs(order_ref, counts_ref, slot, blocks, first, number):
    work = []
    for i in range(number):
        code = order_ref[slot * blocks + jnp.minimum(first + i, counts_ref[slot] - 1)]
        work.append((first + i, code >> 3, (code & 7) * blocks + (code >> 3)))
    return work


def by_fours(count, act):
    fours = count // 4
    lax.fori_loop(0, fours, lambda k, _: (act(4 * k, 4), 0)[1], 0)
    lax.fori_loop(2 * fours, (count + 1) // 2, lambda k, _: (act(2 * k, 2), 0)[1], 0)


def by_eights(count, act):
    eights = count // 8
    lax.fori_loop(0, eights, lambda k, _: (act(8 * k, 8), 0)[1], 0)
    fours = (count - 8 * eights) // 4

    @pl.when(fours == 1)
    def _():
        act(8 * eights, 4)

    lax.fori_loop(
        4 * eights + 2 * fours, (count + 1) // 2, lambda k, _: (act(2 * k, 2), 0)[1], 0
    )


def rows_of(x, block):
    return x[pl.ds(pl.multiple_of(block * BLOCK, BLOCK), BLOCK)]


def find_norms(piece_refs, panels, norms):
    for p, piece in enumerate(piece_refs):
        if piece is not None:
            panels[p] = piece[...]
        wide = panels[p].astype(jnp.float32)
        norm = jnp.sum(wide * wide, axis=1, keepdims=True)
        norms[p] = jnp.broadcast_to(norm * (0.5 * LOGIT_SCALE * LOG2E), norms.shape[1:])


def tile_of(panel, norm, block):
    scores = lax.dot_general(
        panel, block, (((1,), (1,)), ((), ())), preferred_element_type=jnp.float32
    )
    scores = scores * (LOGIT_SCALE * LOG2E) - jnp.concatenate([norm, norm], axis=1)
    top = jnp.max(scores, axis=0, keepdims=True)
    powers = jnp.exp2(scores - top)
    return powers, top, jnp.sum(powers, axis=0, keepdims=True)


def score_loop(
    slots, order_ref, counts_ref, x, panels, norms, tops, masses, tiles, here, done
):
    blocks = x.shape[0] // BLOCK
    tops[...] = jnp.full_like(tops, -jnp.inf)
    masses[...] = jnp.zeros_like(masses)
    starts = [jnp.int32(0)]
    for slot in slots:
        starts.append(starts[-1] + counts_ref[slot])
    count = starts.pop()

    def pair(j):
        p = sum([(j >= start).astype(jnp.int32) for start in starts[1:]], jnp.int32(0))
        first, slot = starts[0], jnp.int32(slots[0])
        for later, start in zip(slots[1:], starts[1:]):
            first = jnp.where(j >= start, start, first)
            slot = jnp.where(j >= start, later, slot)
        code = order_ref[slot * blocks + j - first]
        return p, p * blocks + j - first, code >> 3, (code & 7) * blocks + (code >> 3)

    def some(first, number):
        work = [pair(jnp.minimum(first + i, count - 1)) for i in range(number)]
        for _, _, b, _ in work:
            here(b)
        found = [tile_of(panels[p], norms[p], rows_of(x, b)) for p, _, b, _ in work]
        for (_, tile, _, at), (powers, top, mass) in zip(work, found):
            tiles[tile] = powers
            tops[pl.ds(at, 1)] = top
            masses[pl.ds(at, 1)] = mass
        for i, (_, tile, _, _) in enumerate(work):
            if number == 2 and i:
                pl.when(first + i < count)(functools.partial(done, tile))
            else:
                done(tile)

    by_eights(count, some)


def sum_loop(slots, order_ref, counts_ref, x, shares, acc, totals, tiles, ready):
    blocks = x.shape[0] // BLOCK
    cent = totals.shape[1]
    for p, slot in enumerate(slots):

        def some(first, number):
            work = some_pairs(order_ref, counts_ref, slot, blocks, first, number)
            for i, (j, _, _) in enumerate(work):
                if number == 2 and i:
                    pl.when(j < counts_ref[slot])(functools.partial(ready, p, j))
                else:
                    ready(p, j)
            partial, count = None, None
            for i, (j, b, at) in enumerate(work):
                share = shares[pl.ds(at, 1)]
                if number == 2 and i:
                    share = share * (j < counts_ref[slot]).astype(jnp.float32)
                    j = jnp.minimum(j, counts_ref[slot] - 1)
                weights = (tiles[p * blocks + j] * share).astype(jnp.bfloat16)
                wide = weights.astype(jnp.float32)
                wide = wide[:, :128] + wide[:, 128:]
                product = jnp.dot(weights, rows_of(x, b), preferred_element_type=jnp.float32)
                partial = product if partial is None else partial + product
                count = wide if count is None else count + wide
            totals[p] += count
            acc[p][pl.ds(0, cent)] += partial

        by_fours(counts_ref[slot], some)


def clear_sums(acc, totals):
    for ref in acc:
        ref[...] = jnp.zeros_like(ref)
    totals[...] = jnp.zeros_like(totals)


def store_totals(acc, totals):
    cent = totals.shape[1]
    for p, ref in enumerate(acc):
        row = jnp.sum(totals[p].T, axis=0, keepdims=True)
        ref[pl.ds(cent, EXTRA), pl.ds(0, cent)] = jnp.broadcast_to(row, (EXTRA, cent))


def over_tiles(slots, counts_ref, act):
    for p, slot in enumerate(slots):
        lax.fori_loop(0, counts_ref[slot], lambda i, _, p=p: (act(p, i), 0)[1], 0)


def score_kernel(slots, fetch, order_ref, counts_ref, rows_ref, *refs):
    pieces = len(slots)
    piece_refs = refs[:pieces]
    tiles_ref, tops, masses = refs[pieces : pieces + 3]
    refs = refs[pieces + 3 :]
    x = refs[0] if fetch else rows_ref
    panels, norms, tiles, tile_sem = refs[1:5] if fetch else refs[:4]
    blocks = x.shape[0] // BLOCK
    here = lambda b: None
    if fetch:
        row_sem, fetched, panel_sem = refs[5:]
        brought = [
            pltpu.make_async_copy(ref, panels.at[p], panel_sem.at[p])
            for p, ref in enumerate(piece_refs)
        ]
        for copy in brought:
            copy.start()

        def bring(b):
            span = pl.ds(pl.multiple_of(b * BLOCK, BLOCK), BLOCK)
            return pltpu.make_async_copy(rows_ref.at[span], x.at[span], row_sem.at[b])

        for b in range(blocks):
            bring(b).start()
        fetched[0] = 0

        def here(b):
            first = fetched[0]
            lax.fori_loop(first, b + 1, lambda k, _: (bring(k).wait(), 0)[1], 0)
            fetched[0] = jnp.maximum(first, b + 1)

        for copy in brought:
            copy.wait()
        piece_refs = [None] * pieces

    find_norms(piece_refs, panels, norms)

    def outgoing(j):
        return pltpu.make_async_copy(tiles.at[j], tiles_ref.at[j], tile_sem.at[j])

    score_loop(
        slots, order_ref, counts_ref, x, panels, norms, tops, masses, tiles, here,
        lambda j: outgoing(j).start(),
    )
    here(blocks - 1)
    over_tiles(slots, counts_ref, lambda p, i: outgoing(p * blocks + i).wait())


def sum_kernel(slots, sources, with_prior, order_ref, counts_ref, x, shares, *refs):
    pieces = len(slots)
    arrays = len({which for which, _ in sources})
    if with_prior:
        prior_ref, *refs, prior, prior_sem = refs
        bring = pltpu.make_async_copy(prior_ref, prior, prior_sem)
        bring.start()
    tiles_refs, refs = refs[:arrays], refs[arrays:]
    out_refs = refs[:pieces]
    blocks = x.shape[0] // BLOCK
    totals, tiles, tile_sem = refs[pieces:]

    def incoming(p, i):
        which, first = sources[p]
        j = p * blocks + i
        return pltpu.make_async_copy(tiles_refs[which].at[first + i], tiles.at[j], tile_sem.at[j])

    over_tiles(slots, counts_ref, lambda p, i: incoming(p, i).start())
    clear_sums(out_refs, totals)
    if with_prior:
        bring.wait()
        out_refs[0][pl.ds(0, prior.shape[0])] = PRIOR_MASS * prior[...].astype(jnp.float32)
    sum_loop(
        slots, order_ref, counts_ref, x, shares, out_refs, totals, tiles,
        lambda p, i: incoming(p, i).wait(),
    )
    store_totals(out_refs, totals)


def middle_kernel(slots, listed, earlier, order_ref, counts_ref, x, *refs):
    pieces = len(slots)
    stat_refs = refs[: 2 * earlier]
    piece_refs = refs[2 * earlier : 2 * earlier + pieces]
    refs = refs[2 * earlier + pieces :]
    logs_ref, shares = refs[:2]
    out_refs = refs[2 : 2 + pieces]
    panels, norms, tiles, tops, masses, totals = refs[2 + pieces :]
    blocks = x.shape[0] // BLOCK
    clear_sums(out_refs, totals)
    find_norms(piece_refs, panels, norms)
    score_loop(
        slots, order_ref, counts_ref, x, panels, norms, tops, masses, tiles,
        lambda b: None, lambda j: None,
    )
    width = tops.shape[1]
    top = functools.reduce(jnp.maximum, [ref[...] for ref in stat_refs[:earlier]], tops[...])
    mass = functools.reduce(jnp.add, [ref[...] for ref in stat_refs[earlier:]], masses[...])
    top = top.reshape(listed, blocks, width)
    mass = mass.reshape(listed, blocks, width)
    highest = jnp.max(top, axis=0)
    factor = jnp.exp2(top - highest[None])
    whole = jnp.sum(factor * mass, axis=0)
    logs_ref[...] = (highest + jnp.log2(whole)) * (1.0 / LOG2E)
    shares[...] = (factor / whole[None]).reshape(listed * blocks, width)
    sum_loop(slots, order_ref, counts_ref, x, shares, out_refs, totals, tiles, lambda p, i: None)
    store_totals(out_refs, totals)


SMEM = pl.BlockSpec(memory_space=pltpu.SMEM)
HBM = pl.BlockSpec(memory_space=pltpu.HBM)
VMEM = pl.BlockSpec(memory_space=pltpu.VMEM)


class Sizes:
    def __init__(self, rows, blocks, listed, cent):
        self.blocks, self.listed, self.cent = blocks, listed, cent
        self.width = rows.shape[1]
        self.stats = jax.ShapeDtypeStruct((listed * blocks, BLOCK), jnp.float32)
        self.sums = jax.ShapeDtypeStruct((cent + EXTRA, self.width), jnp.float32)
        self.tiles = jax.ShapeDtypeStruct((5 * blocks, cent, BLOCK), jnp.float32)

    def cost(self, slots, products):
        pairs = self.blocks * self.listed * len(slots) / 14
        return pl.CostEstimate(
            flops=int(2 * products * pairs * self.cent * BLOCK * self.width),
            bytes_accessed=int(2 * self.blocks * BLOCK * self.width + 4 * pairs * self.cent * BLOCK),
            transcendentals=int(pairs * self.cent * BLOCK),
        )

    def panels(self, pieces):
        return pltpu.VMEM((pieces, self.cent, self.width), jnp.bfloat16)

    def columns(self, pieces):
        return pltpu.VMEM((pieces, self.cent, 128), jnp.float32)

    def tile_scratch(self, pieces):
        return pltpu.VMEM((pieces * self.blocks, self.cent, BLOCK), jnp.float32)


def score_group(sizes, slots, order, counts, rows, pieces, fetch):
    count = len(pieces)
    outs = (sizes.tiles, sizes.stats, sizes.stats)
    rows_outs, rows_scratch = (), []
    if fetch:
        rows_outs = (jax.ShapeDtypeStruct(rows.shape, rows.dtype),)
        rows_scratch = [
            pltpu.SemaphoreType.DMA((sizes.blocks,)),
            pltpu.SMEM((1,), jnp.int32),
            pltpu.SemaphoreType.DMA((count,)),
        ]
    return pl.pallas_call(
        functools.partial(score_kernel, slots, fetch),
        out_shape=outs + rows_outs,
        in_specs=[SMEM, SMEM] + ([HBM] * (1 + count) if fetch else [VMEM] * (1 + count)),
        out_specs=(HBM, VMEM, VMEM) + (VMEM,) * len(rows_outs),
        scratch_shapes=[
            sizes.panels(count),
            sizes.columns(count),
            sizes.tile_scratch(count),
            pltpu.SemaphoreType.DMA((count * sizes.blocks,)),
        ]
        + rows_scratch,
        compiler_params=pltpu.CompilerParams(vmem_limit_bytes=VMEM_GRANT),
        cost_estimate=sizes.cost(slots, 1),
        name="score_group",
    )(order, counts, rows, *pieces)


def sum_group(sizes, slots, order, counts, rows, shares, places, tiles, prior):
    count = len(slots)
    used = sorted({places[slot][0] for slot in slots})
    sources = [(used.index(places[slot][0]), places[slot][1]) for slot in slots]
    return pl.pallas_call(
        functools.partial(sum_kernel, slots, sources, bool(prior)),
        out_shape=(sizes.sums,) * count,
        in_specs=[SMEM, SMEM, VMEM, VMEM] + [HBM] * (len(prior) + len(used)),
        out_specs=(VMEM,) * count,
        scratch_shapes=[
            sizes.columns(count),
            sizes.tile_scratch(count),
            pltpu.SemaphoreType.DMA((count * sizes.blocks,)),
        ]
        + [pltpu.VMEM((sizes.cent, sizes.width), jnp.bfloat16), pltpu.SemaphoreType.DMA] * len(prior),
        compiler_params=pltpu.CompilerParams(vmem_limit_bytes=VMEM_GRANT),
        cost_estimate=sizes.cost(slots, 1),
        name="sum_group",
    )(order, counts, rows, shares, *prior, *[tiles[which] for which in used])


def middle_group(sizes, slots, order, counts, rows, tops, masses, pieces):
    count = len(pieces)
    earlier = len(tops)
    return pl.pallas_call(
        functools.partial(middle_kernel, slots, sizes.listed, earlier),
        out_shape=(jax.ShapeDtypeStruct((sizes.blocks, BLOCK), jnp.float32), sizes.stats)
        + (sizes.sums,) * count,
        in_specs=[SMEM, SMEM, VMEM] + [VMEM] * (2 * earlier + count),
        out_specs=(VMEM, VMEM) + (VMEM,) * count,
        scratch_shapes=[
            sizes.panels(count),
            sizes.columns(count),
            sizes.tile_scratch(count),
            pltpu.VMEM(sizes.stats.shape, jnp.float32),
            pltpu.VMEM(sizes.stats.shape, jnp.float32),
            sizes.columns(count),
        ],
        compiler_params=pltpu.CompilerParams(vmem_limit_bytes=VMEM_GRANT),
        cost_estimate=sizes.cost(slots, 2),
        name="middle_group",
    )(order, counts, rows, *tops, *masses, *pieces)


def add_kernel(mine_ref, back_ref, out_ref):
    out_ref[...] = mine_ref[...] * LINK_SCALE + back_ref[...]


def scaled_sum(mine, back):
    return pl.pallas_call(
        add_kernel,
        out_shape=jax.ShapeDtypeStruct(mine.shape, mine.dtype),
        in_specs=[VMEM, VMEM],
        out_specs=VMEM,
        compiler_params=pltpu.CompilerParams(vmem_limit_bytes=VMEM_GRANT),
        cost_estimate=pl.CostEstimate(flops=30 * 10**9, bytes_accessed=12 * mine.size, transcendentals=0),
        name="scaled_sum",
    )(mine, back)


def on_device(rows, centroids, lists):
    count = lax.axis_size("blk")
    device = lax.axis_index("blk")
    cent = centroids.shape[0]
    own, stages = plan_of(count)
    groups = [(own,)] + [tuple(q for q, _, _ in stage) for stage in stages]
    slots = (2 * chip_place(lists, device, count) + ((lists ^ device) & 1)).astype(jnp.int32)
    sizes = Sizes(rows, *slots.shape, cent)
    order, counts = pairs_of(slots, 2 * max(q for members in groups for q in members) + 2)

    near, far = {own: centroids}, {}
    tiles, tops, masses, places = [], [], [], {}

    def score(slots, fetch=False):
        pieces = [(far if slot & 1 else near)[slot >> 1] for slot in slots]
        for p, slot in enumerate(slots):
            places[slot] = (len(tiles), p * sizes.blocks)
        return score_group(sizes, slots, order, counts, rows, pieces, fetch)

    for number, stage in enumerate(stages):
        arriving = [moved(near[source], shift) for _, source, shift in stage]
        for q in groups[number]:
            far[q] = other_core(near[q])
        if number == 0:
            scored = score([2 * own], fetch=True)
        elif number == 1:
            scored = score([2 * own + 1] + local_slots(groups[1]))
        else:
            scored = score(local_slots(groups[number]))
        arriving, scored, near, far = lax.optimization_barrier((arriving, scored, near, far))
        if number == 0:
            rows = scored[3]
        tiles.append(scored[0])
        tops.append(scored[1])
        masses.append(scored[2])
        for (q, _, _), value in zip(stage, arriving):
            near[q] = value
    last = groups[-1]
    near_slots, far_slots = [2 * q for q in last], [2 * q + 1 for q in last]
    for q in last:
        far[q] = other_core(near[q])
    scored = score(near_slots)
    tiles.append(scored[0])
    tops.append(scored[1])
    masses.append(scored[2])
    log_totals, shares, *far_sums = middle_group(
        sizes, far_slots, order, counts, rows, tops, masses, [far[q] for q in last]
    )
    near_sums = sum_group(sizes, near_slots, order, counts, rows, shares, places, tiles, ())
    mine = dict(zip(last, near_sums))
    crossed = {q: other_core(packed(v)) for q, v in zip(last, far_sums)}
    total = {q: mine[q] * LINK_SCALE + crossed[q].astype(jnp.float32) for q in last}

    back = {q: [] for members in groups for q in members}
    for members, stage in zip(reversed(groups[:-1]), reversed(stages)):
        stage = sorted(stage, key=lambda move: move[2] is None)
        leaving = [total[q].astype(jnp.float16) for q, _, _ in stage]
        leaving, shares = lax.optimization_barrier((leaving, shares))
        arriving = [
            moved(value, shift if shift is None else -shift)
            for value, (_, _, shift) in zip(leaving, stage)
        ]
        prior = (centroids,) if members == groups[0] else ()
        sums = sum_group(
            sizes, local_slots(members), order, counts, rows, shares, places, tiles, prior
        )
        crossed = {q: other_core(packed(v)) for q, v in zip(members, sums[1::2])}
        arriving = lax.optimization_barrier(arriving)
        for value, (_, source, _) in zip(arriving, stage):
            back[source].append(value.astype(jnp.float32))
        for q, near_sum in zip(members, sums[::2]):
            if back[q]:
                part = scaled_sum(near_sum, functools.reduce(jnp.add, back[q]))
            else:
                part = near_sum * LINK_SCALE
            total[q] = part + crossed[q].astype(jnp.float32)
    own_sums = total[own] * (1.0 / LINK_SCALE)
    updated = own_sums[:cent] / (own_sums[cent, :cent][:, None] + PRIOR_MASS)
    return updated, log_totals.reshape(-1)


def solution(mesh):
    placed = P(("groups", "blk"), None)
    return jax.shard_map(
        on_device,
        mesh=mesh,
        in_specs=(placed, placed, placed),
        out_specs=(placed, P(("groups", "blk"))),
        check_vma=False,
    )
```
